256 devices in a mesh: dp: 32 (over z_hi, y, core), rows: 8 (over z_lo, x).
Axes of the slice: x: 4, y: 4, z: 8 (z_hi: 4, z_lo: 2; z = z_hi * 2 + z_lo), core: 2. Of those that a mesh axis runs over, the one named last changes fastest.
Arguments:
- latent: bfloat16 [32, 320, 16, 128], P('dp', None, 'rows'), may hold values from -14 to 14
- hint_field: bfloat16 [32, 320, 16, 128], P('dp', None, 'rows'), may hold values from -6 to 6
- from_below: bfloat16 [32, 320, 16, 128], P('dp', None, 'rows'), may hold values from -6 to 6
- cotangent: bfloat16 [32, 320, 16, 128], P('dp', None, 'rows'), may hold values from -6 to 6
- timesteps: int32 [32], P('dp'), may hold values from 0 to 999
- time_weight: bfloat16 [320, 1280], replicated, may hold values from -0.3125 to 0.3125
- enc_proj: bfloat16 [1280, 320], replicated, may hold values from -0.4375 to 0.4375
- ctl_proj: bfloat16 [1280, 320], replicated, may hold values from -0.15625 to 0.15625
- dec_proj: bfloat16 [1280, 320], replicated, may hold values from -0.15625 to 0.15625
- enc_conv_one: bfloat16 [320, 3, 3, 320], replicated, may hold values from -0.109375 to 0.109375
- enc_conv_two: bfloat16 [320, 3, 3, 320], replicated, may hold values from -0.109375 to 0.109375
- ctl_conv_one: bfloat16 [320, 3, 3, 320], P('dp'), may hold values from -0.109375 to 0.109375
- ctl_conv_two: bfloat16 [320, 3, 3, 320], P('dp'), may hold values from -0.109375 to 0.109375
- dec_conv_one: bfloat16 [320, 3, 3, 640], P('dp'), may hold values from -0.078125 to 0.078125
- dec_conv_two: bfloat16 [320, 3, 3, 320], P('dp'), may hold values from -0.109375 to 0.109375
- dec_shortcut: bfloat16 [320, 640], P('dp'), may hold values from -0.25 to 0.25
- zero_conv: bfloat16 [320, 320], P('dp'), may hold values from -0.3125 to 0.3125
Outputs:
- ctl_conv_one_grad: float32 [320, 3, 3, 320], P('dp')
- ctl_conv_two_grad: float32 [320, 3, 3, 320], P('dp')
- zero_conv_grad: float32 [320, 320], P('dp')
The draws below stay inside these ranges and needn't reach their ends.
All inputs are finite; a program needn't handle non-finite values.
Results may differ from the reference program's by a relative error of at most 0.009.
Values may be sent and summed in bfloat16 or wider, within the bound.
A program may use at most 128 MiB of HBM per device.

```python
import math
import jax
import jax.numpy as jnp
from jax import lax

C = 320
TDIM = 1280
GROUPS = 32
WIDTH = 128
BATCH = 32
HEIGHT = 16


def draw_latent(key, part):
    noise_key = jax.random.fold_in(key, 0)
    full_shape = (BATCH, C, HEIGHT, WIDTH)
    rising = jnp.exp(jnp.log(3.0) * jnp.arange(HEIGHT, dtype=jnp.float32) / (HEIGHT - 1))[None, None, :, None]
    result = jax.random.truncated_normal(noise_key, -4.0, 4.0, full_shape, jnp.float32) * rising
    return result.astype(jnp.bfloat16)


def plant(drawn, rng, smallest, high):
    longest = drawn.shape.index(max(drawn.shape))
    spots = []
    for shift in (0, 1):
        where = [jax.random.randint(jax.random.fold_in(rng, axis), (), 0, length) for axis, length in enumerate(drawn.shape)]
        where[longest] = (where[longest] + shift) % drawn.shape[longest]
        spots.append(tuple(where))
    return drawn.at[spots[0]].set(smallest).at[spots[1]].set(high)


def steps_of(key, shape, pieces, smallest, top_value):
    level = 1.0
    for axis_at, parts in pieces:
        draws = jax.random.uniform(jax.random.fold_in(jax.random.fold_in(key, 6), axis_at), (parts,), jnp.float32, smallest / len(pieces), top_value / len(pieces))
        level = level * jnp.repeat(jnp.exp(draws), shape[axis_at] // parts).reshape((-1,) + (1,) * (len(shape) - 1 - axis_at))
    return level


def centred(key, dims, deviation, reach, pieces=(), held_as=jnp.bfloat16):
    factor_of = steps_of(key, dims, pieces, -0.22, 0.18) if pieces else 1.0
    array = jax.random.normal(key, dims, jnp.float32) * deviation * factor_of
    return jnp.minimum(jnp.maximum(array, -reach), reach).astype(held_as)


def setup_inputs(seed: int = 0) -> dict:
    key_of = jax.random.split(jax.random.key(seed), 18)
    return {
        "latent": draw_latent(jax.random.fold_in(key_of[17], 71), 0),
        "hint_field": centred(key_of[1], (BATCH, C, HEIGHT, WIDTH), 1.0, 6.0, ((0, 32), (2, 8))),
        "from_below": centred(key_of[2], (BATCH, C, HEIGHT, WIDTH), 1.0, 6.0, ((0, 32), (2, 8))),
        "cotangent": centred(key_of[3], (BATCH, C, HEIGHT, WIDTH), 1.0, 6.0, ((0, 32), (2, 8))),
        "timesteps": plant(jax.random.randint(key_of[4], (BATCH,), 0, 1000), jax.random.fold_in(key_of[4], 1), 0, 999).astype(jnp.int32),
        "time_weight": centred(key_of[5], (C, TDIM), C ** -0.5, 0.3125),
        "enc_proj": centred(key_of[6], (TDIM, C), (TDIM // 6) ** -0.5, 0.4375),
        "ctl_proj": centred(key_of[7], (TDIM, C), TDIM ** -0.5, 0.15625),
        "dec_proj": centred(key_of[8], (TDIM, C), TDIM ** -0.5, 0.15625),
        "enc_conv_one": centred(key_of[9], (C, 3, 3, C), (9 * C) ** -0.5, 0.109375),
        "enc_conv_two": centred(key_of[10], (C, 3, 3, C), (9 * C) ** -0.5, 0.109375),
        "ctl_conv_one": centred(key_of[11], (C, 3, 3, C), (9 * C) ** -0.5, 0.109375, ((0, 32),)),
        "ctl_conv_two": centred(key_of[12], (C, 3, 3, C), (9 * C) ** -0.5, 0.109375, ((0, 32),)),
        "dec_conv_one": centred(key_of[13], (C, 3, 3, 2 * C), (18 * C) ** -0.5, 0.078125, ((0, 32),)),
        "dec_conv_two": centred(key_of[14], (C, 3, 3, C), (9 * C) ** -0.5, 0.109375, ((0, 32),)),
        "dec_shortcut": centred(key_of[15], (C, 2 * C), (2 * C) ** -0.5, 0.25, ((0, 32),)),
        "zero_conv": centred(key_of[16], (C, C), C ** -0.5, 0.3125, ((0, 32),)),
    }


EPSILON = 1e-05
LAYOUT = ('NCHW', 'OHWI', 'NCHW')

def conv_same(source, weight):
    return lax.conv_general_dilated(source.astype(jnp.float32), weight.astype(jnp.float32), (1, 1), ((1, 1), (1, 1)), dimension_numbers=LAYOUT, precision=lax.Precision.HIGHEST)

def mix_channels(matrix, source):
    return jnp.einsum('oi,bihw->bohw', matrix.astype(jnp.float32), source.astype(jnp.float32), precision=lax.Precision.HIGHEST)

def mix_back(matrix, upstream):
    return jnp.einsum('oi,bohw->bihw', matrix.astype(jnp.float32), upstream.astype(jnp.float32), precision=lax.Precision.HIGHEST)

def outer_sum(upstream, source):
    return jnp.einsum('bohw,bihw->oi', upstream.astype(jnp.float32), source.astype(jnp.float32), precision=lax.Precision.HIGHEST)

def flip_kernel(weight):
    return jnp.transpose(weight[:, ::-1, ::-1, :], (3, 1, 2, 0))

def group_norm(source, groups_here):
    full_shape = source.shape
    grouped = source.reshape(full_shape[0], groups_here, full_shape[1] // groups_here, full_shape[2], full_shape[3])
    average = lax.optimization_barrier(jnp.mean(grouped, axis=(2, 3, 4)))
    centered = grouped - average[:, :, None, None, None]
    inv_spread = lax.rsqrt(lax.optimization_barrier(jnp.mean(centered * centered, axis=(2, 3, 4))) + EPSILON)
    return ((centered * inv_spread[:, :, None, None, None]).reshape(full_shape), inv_spread)

def norm_back(upstream, normed, inv_spread):
    full_shape = upstream.shape
    groups_here = inv_spread.shape[1]
    grouped = upstream.reshape(full_shape[0], groups_here, full_shape[1] // groups_here, full_shape[2], full_shape[3])
    normed_grouped = normed.reshape(grouped.shape)
    first_mean = lax.optimization_barrier(jnp.mean(grouped, axis=(2, 3, 4)))[:, :, None, None, None]
    cross_mean = lax.optimization_barrier(jnp.mean(grouped * normed_grouped, axis=(2, 3, 4)))[:, :, None, None, None]
    result = inv_spread[:, :, None, None, None] * (grouped - first_mean - normed_grouped * cross_mean)
    return result.reshape(full_shape)

def silu_slope(values):
    sigma = jax.nn.sigmoid(values)
    return sigma * (1.0 + values * (1.0 - sigma))

def kernel_grad(upstream, source):
    padded = jnp.pad(source, ((0, 0), (0, 0), (1, 1), (1, 1)))
    row_count = upstream.shape[2]
    col_count = upstream.shape[3]
    return jnp.stack([jnp.stack([outer_sum(upstream, padded[:, :, row_tap:row_tap + row_count, col_tap:col_tap + col_count]) for col_tap in range(3)], 1) for row_tap in range(3)], 1)

def block_front(source, conv_one, time_term):
    normed_in, spread_in = group_norm(source.astype(jnp.float32), GROUPS)
    first_act = jax.nn.silu(normed_in).astype(jnp.bfloat16)
    inner_sum = conv_same(first_act, conv_one) + time_term[:, :, None, None]
    normed, spread = group_norm(inner_sum, GROUPS)
    second_act = jax.nn.silu(normed).astype(jnp.bfloat16)
    return (normed_in, spread_in, first_act, normed, spread, second_act)

def reference(latent, hint_field, from_below, cotangent, timesteps, time_weight, enc_proj, ctl_proj, dec_proj, enc_conv_one, enc_conv_two, ctl_conv_one, ctl_conv_two, dec_conv_one, dec_conv_two, dec_shortcut, zero_conv):
    half_width = C // 2
    frequency = jnp.exp(-math.log(10000.0) * jnp.arange(half_width, dtype=jnp.float32) / half_width)
    angles = timesteps.astype(jnp.float32)[:, None] * frequency[None, :]
    sinusoid = jnp.concatenate([jnp.cos(angles), jnp.sin(angles)], axis=1).astype(jnp.bfloat16)
    time_embed = jnp.dot(sinusoid, time_weight, preferred_element_type=jnp.float32)
    time_act = jax.nn.silu(time_embed).astype(jnp.bfloat16)
    enc_term = jnp.dot(time_act, enc_proj, preferred_element_type=jnp.float32)
    ctl_term = jnp.dot(time_act, ctl_proj, preferred_element_type=jnp.float32)
    dec_term = jnp.dot(time_act, dec_proj, preferred_element_type=jnp.float32)
    enc_parts = block_front(latent, enc_conv_one, enc_term)
    enc_out = (latent.astype(jnp.float32) + conv_same(enc_parts[5], enc_conv_two)).astype(jnp.bfloat16)
    ctl_in = (latent.astype(jnp.float32) + hint_field.astype(jnp.float32)).astype(jnp.bfloat16)
    ctl_parts = block_front(ctl_in, ctl_conv_one, ctl_term)
    ctl_out = (ctl_in.astype(jnp.float32) + conv_same(ctl_parts[5], ctl_conv_two)).astype(jnp.bfloat16)
    skip_sum = (enc_out.astype(jnp.float32) + mix_channels(zero_conv, ctl_out)).astype(jnp.bfloat16)
    joined = jnp.concatenate([from_below, skip_sum], axis=1)
    dec_parts = block_front(joined, dec_conv_one, dec_term)
    loss_scale = float(BATCH * HEIGHT * WIDTH) ** (-0.5)
    out_grad = (cotangent.astype(jnp.float32) * loss_scale).astype(jnp.bfloat16)
    dec_second_grad = conv_same(out_grad, flip_kernel(dec_conv_two))
    dec_inner_grad = norm_back(dec_second_grad * silu_slope(dec_parts[3]), dec_parts[3], dec_parts[4]).astype(jnp.bfloat16)
    skip_first_grad = conv_same(dec_inner_grad, flip_kernel(dec_conv_one[:, :, :, C:]))
    skip_normed = dec_parts[0][:, C:]
    skip_spread = dec_parts[1][:, GROUPS // 2:]
    skip_grad = norm_back(skip_first_grad * silu_slope(skip_normed), skip_normed, skip_spread) + mix_back(dec_shortcut[:, C:], out_grad)
    skip_grad = skip_grad.astype(jnp.bfloat16)
    zero_conv_grad = outer_sum(skip_grad, ctl_out)
    ctl_out_grad = mix_back(zero_conv, skip_grad).astype(jnp.bfloat16)
    ctl_conv_two_grad = kernel_grad(ctl_out_grad, ctl_parts[5])
    ctl_second_grad = conv_same(ctl_out_grad, flip_kernel(ctl_conv_two))
    ctl_inner_grad = norm_back(ctl_second_grad * silu_slope(ctl_parts[3]), ctl_parts[3], ctl_parts[4]).astype(jnp.bfloat16)
    ctl_conv_one_grad = kernel_grad(ctl_inner_grad, ctl_parts[2])
    return (ctl_conv_one_grad, ctl_conv_two_grad, zero_conv_grad)
```

```python
import math

import jax
import jax.numpy as jnp
from jax import lax
from jax.experimental import pallas as pl
from jax.experimental.pallas import tpu as pltpu
from jax.sharding import PartitionSpec as P

C = 320
GROUPS = 32


EPSILON = 1e-05
LAYOUT = ("NCHW", "OHWI", "NCHW")


MESH = pl.DeviceIdType.MESH
LANES = 16384
GLANES = 8192
BF = jnp.bfloat16
F32 = jnp.float32


def place():
    d = lax.axis_index("dp")
    r = lax.axis_index("rows")
    return (d // 8, (d // 2) % 4, d % 2, r // 4, r % 4)


def device_of(zh, y, c, zl, x):
    return (zh * 8 + y * 2 + c, zl * 4 + x)


def remote(src, dst, send, recv, where):
    return pltpu.make_async_remote_copy(
        src_ref=src, dst_ref=dst, send_sem=send, recv_sem=recv, device_id=where, device_id_type=MESH
    )


def torus_peers(me):
    zh, y, c, zl, x = me
    found = []
    for k in range(1, 8):
        s = (y * 2 + c + k) % 8
        found.append(device_of(zh, s // 2, s % 2, zl, x))
    for k in range(1, 4):
        found.append(device_of((zh + k) % 4, y, c, zl, x))
        found.append(device_of(zh, y, c, zl, (x + k) % 4))
    return found


def greet(peers):
    barrier = pltpu.get_barrier_semaphore()
    for where in peers:
        pl.semaphore_signal(barrier, inc=1, device_id=where, device_id_type=MESH)
    pl.semaphore_wait(barrier, len(peers))


def gather_kernel(
    src, out, parts, column, wide, own_sem, send1, recv1, send2, recv2, send3, recv3, send4, recv4, send5, recv5
):
    me = place()
    zh, y, c, zl, x = me
    slot = y * 2 + c
    greet(torus_peers(me))
    first = []
    for k in range(1, 8):
        s = (slot + k) % 8
        first.append(
            remote(src.at[s], parts.at[slot], send1.at[k - 1], recv1.at[k - 1], device_of(zh, s // 2, s % 2, zl, x))
        )
        first[-1].start()
    mine = pltpu.make_async_copy(src.at[slot], parts.at[slot], own_sem.at[0])
    mine.start()
    mine.wait()
    for copy in first:
        copy.wait_recv()
    for s in range(8):
        column[10 * s : 10 * s + 10, :] = parts[s, 0:10, :].astype(F32)
    home = pl.multiple_of(zh * 80, 80)
    wide[pl.ds(home, 80), :] = column[...].astype(BF)
    second = []
    for k in range(1, 4):
        second.append(
            remote(
                wide.at[pl.ds(home, 80)],
                wide.at[pl.ds(home, 80)],
                send2.at[k - 1],
                recv2.at[k - 1],
                device_of((zh + k) % 4, y, c, zl, x),
            )
        )
        second[-1].start()
    for copy in second:
        copy.wait_recv()
    spot_a = pl.multiple_of(((y * 2 + c) * 4 + x) * 256, 256)
    spot_b = pl.multiple_of(8192 + ((x * 2 + c) * 4 + y) * 256, 256)
    third = []
    for k in range(1, 4):
        third.append(
            remote(
                wide.at[:, 0:256],
                out.at[:, pl.ds(spot_a, 256)],
                send3.at[0, k - 1],
                recv3.at[0, k - 1],
                device_of(zh, y, c, zl, (x + k) % 4),
            )
        )
        third.append(
            remote(
                wide.at[:, 256:512],
                out.at[:, pl.ds(spot_b, 256)],
                send3.at[1, k - 1],
                recv3.at[1, k - 1],
                device_of(zh, (y + k) % 4, c, zl, x),
            )
        )
    for copy in third:
        copy.start()
    mine_a = pltpu.make_async_copy(wide.at[:, 0:256], out.at[:, pl.ds(spot_a, 256)], own_sem.at[1])
    mine_b = pltpu.make_async_copy(wide.at[:, 256:512], out.at[:, pl.ds(spot_b, 256)], own_sem.at[2])
    mine_a.start()
    mine_b.start()
    mine_a.wait()
    mine_b.wait()
    for copy in third:
        copy.wait_recv()
    partner = device_of(zh, y, 1 - c, zl, x)
    row_a = pl.multiple_of((y * 2 + c) * 1024, 1024)
    row_b = pl.multiple_of(8192 + (x * 2 + c) * 1024, 1024)
    fourth = []
    fifth = []
    for k in range(1, 4):
        fourth.append(
            remote(
                out.at[:, pl.ds(row_a, 1024)],
                out.at[:, pl.ds(row_a, 1024)],
                send4.at[0, k - 1],
                recv4.at[0, k - 1],
                device_of(zh, (y + k) % 4, c, zl, x),
            )
        )
        fourth.append(
            remote(
                out.at[:, pl.ds(row_b, 1024)],
                out.at[:, pl.ds(row_b, 1024)],
                send4.at[1, k - 1],
                recv4.at[1, k - 1],
                device_of(zh, y, c, zl, (x + k) % 4),
            )
        )
    for copy in fourth:
        copy.start()
    for k in range(4):
        if k > 0:
            fourth[2 * k - 2].wait_recv()
            fourth[2 * k - 1].wait_recv()
        from_a = pl.multiple_of(((y + 4 - k) % 4 * 2 + c) * 1024, 1024)
        from_b = pl.multiple_of(8192 + ((x + 4 - k) % 4 * 2 + c) * 1024, 1024)
        for which, spot in ((0, from_a), (1, from_b)):
            copy = remote(
                out.at[:, pl.ds(spot, 1024)],
                out.at[:, pl.ds(spot, 1024)],
                send5.at[which, k],
                recv5.at[which, k],
                partner,
            )
            copy.start()
            fifth.append(copy)
    for copy in fifth:
        copy.wait_recv()
    for copy in first + second + third + fourth + fifth:
        copy.wait_send()


def gather_weights(shard):
    x = lax.axis_index("rows") % 4
    half_a = shard[:, :8192].reshape(10, 4, 2, 4, 256)
    half_b = shard[:, 8192:].reshape(10, 4, 2, 4, 256)
    part_a = lax.dynamic_index_in_dim(half_a, x, 3, keepdims=False)
    part_b = lax.dynamic_index_in_dim(half_b, x, 1, keepdims=False)
    part_b = jnp.transpose(part_b, (0, 2, 1, 3))
    both = jnp.concatenate([part_a, part_b], axis=3)
    both = jnp.transpose(both, (1, 2, 0, 3)).reshape(8, 10, 512)
    both = jnp.pad(both, ((0, 0), (0, 6), (0, 0)))
    dma = pltpu.SemaphoreType.DMA
    return pl.pallas_call(
        gather_kernel,
        out_shape=jax.ShapeDtypeStruct((320, LANES), BF),
        in_specs=[pl.BlockSpec(memory_space=pltpu.VMEM)],
        out_specs=pl.BlockSpec(memory_space=pl.ANY),
        scratch_shapes=[
            pltpu.VMEM((8, 16, 512), BF),
            pltpu.VMEM((80, 512), F32),
            pltpu.VMEM((320, 512), BF),
            dma((3,)),
            dma((7,)),
            dma((7,)),
            dma((3,)),
            dma((3,)),
            dma((2, 3)),
            dma((2, 3)),
            dma((2, 3)),
            dma((2, 3)),
            dma((2, 4)),
            dma((2, 4)),
        ],
        compiler_params=pltpu.CompilerParams(collective_id=0, has_side_effects=True),
        name="gather_weights",
    )(both)


def reduce_kernel(
    grads,
    out,
    swap,
    half,
    far,
    near,
    near_in,
    last,
    deep,
    deep_in,
    plane,
    plane_in,
    spread,
    own_sem,
    send1,
    recv1,
    send2,
    recv2,
    send3,
    recv3,
    send4,
    recv4,
    send5,
    recv5,
    send6,
    recv6,
    send7,
    recv7,
):
    me = place()
    zh, y, c, zl, x = me
    slot = y * 2 + c
    other_z = device_of(zh, y, c, 1 - zl, x)
    greet(torus_peers(me) + [other_z])
    partner = device_of(zh, y, 1 - c, zl, x)
    theirs = pl.multiple_of((1 - c) * 4096, 4096)
    ours = pl.multiple_of(c * 4096, 4096)
    one = remote(grads.at[:, pl.ds(theirs, 4096)], swap, send1.at[0], recv1.at[0], partner)
    one.start()
    one.wait_recv()

    @pl.loop(0, 20)
    def _(i):
        rows = pl.ds(pl.multiple_of(i * 16, 16), 16)
        total = grads[rows, pl.ds(ours, 4096)].astype(F32) + swap[rows, :].astype(F32)
        half[rows, :] = total.astype(BF)

    second = []
    for k in range(1, 4):
        ya = (y + k) % 4
        xb = (x + k) % 4
        second.append(
            remote(
                half.at[:, pl.ds(pl.multiple_of(ya * 512, 512), 512)],
                far.at[0, k - 1],
                send2.at[0, k - 1],
                recv2.at[0, k - 1],
                device_of(zh, ya, c, zl, x),
            )
        )
        second.append(
            remote(
                half.at[:, pl.ds(pl.multiple_of(2048 + xb * 512, 512), 512)],
                far.at[1, k - 1],
                send2.at[1, k - 1],
                recv2.at[1, k - 1],
                device_of(zh, y, c, zl, xb),
            )
        )
    for copy in second:
        copy.start()
    for copy in second:
        copy.wait_recv()
    mine_a = pl.ds(pl.multiple_of(y * 512, 512), 512)
    mine_b = pl.ds(pl.multiple_of(2048 + x * 512, 512), 512)

    @pl.loop(0, 20)
    def _(i):
        rows = pl.ds(pl.multiple_of(i * 16, 16), 16)
        for which, lanes in ((0, mine_a), (1, mine_b)):
            total = half[rows, lanes].astype(F32)
            for k in range(3):
                total = total + far[which, k, rows, :].astype(F32)
            near[which, rows, :] = total.astype(BF)

    third = []
    for k in range(1, 4):
        xa = (x + k) % 4
        yb = (y + k) % 4
        third.append(
            remote(
                near.at[0, :, pl.ds(pl.multiple_of(xa * 128, 128), 128)],
                near_in.at[0, k - 1],
                send3.at[0, k - 1],
                recv3.at[0, k - 1],
                device_of(zh, y, c, zl, xa),
            )
        )
        third.append(
            remote(
                near.at[1, :, pl.ds(pl.multiple_of(yb * 128, 128), 128)],
                near_in.at[1, k - 1],
                send3.at[1, k - 1],
                recv3.at[1, k - 1],
                device_of(zh, yb, c, zl, x),
            )
        )
    for copy in third:
        copy.start()
    for copy in third:
        copy.wait_recv()
    for which, where in ((0, x), (1, y)):
        total = near[which, :, pl.ds(pl.multiple_of(where * 128, 128), 128)].astype(F32)
        for k in range(3):
            total = total + near_in[which, k].astype(F32)
        deep[:, which * 128 : which * 128 + 128] = total.astype(BF)

    fourth = []
    for k in range(1, 4):
        zt = (zh + k) % 4
        fourth.append(
            remote(
                deep.at[pl.ds(pl.multiple_of(zt * 80, 80), 80)],
                deep_in.at[k - 1],
                send4.at[k - 1],
                recv4.at[k - 1],
                device_of(zt, y, c, zl, x),
            )
        )
        fourth[-1].start()
    for copy in fourth:
        copy.wait_recv()
    total = deep[pl.ds(pl.multiple_of(zh * 80, 80), 80), :].astype(F32)
    for k in range(3):
        total = total + deep_in[k].astype(F32)
    plane[...] = total
    five = remote(plane, plane_in, send5.at[0], recv5.at[0], other_z)
    five.start()
    five.wait_recv()
    last[...] = plane[...] + plane_in[...]
    for s in range(8):
        spread[s, 0:10, :] = last[10 * s : 10 * s + 10, :]
        spread[s, 10:16, :] = jnp.zeros((6, 256), F32)
    sixth = []
    for k in range(1, 8):
        s = (slot + k) % 8
        sixth.append(
            remote(
                spread.at[s],
                out.at[x, slot],
                send6.at[k - 1],
                recv6.at[k - 1],
                device_of(zh, s // 2, s % 2, zl, x),
            )
        )
        sixth[-1].start()
    mine = pltpu.make_async_copy(spread.at[slot], out.at[x, slot], own_sem.at[0])
    mine.start()
    mine.wait()
    for copy in sixth:
        copy.wait_recv()
    seventh = []
    for k in range(1, 4):
        seventh.append(
            remote(out.at[x], out.at[x], send7.at[k - 1], recv7.at[k - 1], device_of(zh, y, c, zl, (x + k) % 4))
        )
        seventh[-1].start()
    for copy in seventh:
        copy.wait_recv()
    for copy in [one] + second + third + fourth + [five] + sixth + seventh:
        copy.wait_send()


def reduce_grads(grads):
    dma = pltpu.SemaphoreType.DMA
    pieces = pl.pallas_call(
        reduce_kernel,
        out_shape=jax.ShapeDtypeStruct((4, 8, 16, 256), F32),
        in_specs=[pl.BlockSpec(memory_space=pltpu.VMEM)],
        out_specs=pl.BlockSpec(memory_space=pltpu.VMEM),
        scratch_shapes=[
            pltpu.VMEM((320, 4096), BF),
            pltpu.VMEM((320, 4096), BF),
            pltpu.VMEM((2, 3, 320, 512), BF),
            pltpu.VMEM((2, 320, 512), BF),
            pltpu.VMEM((2, 3, 320, 128), BF),
            pltpu.VMEM((80, 256), F32),
            pltpu.VMEM((320, 256), BF),
            pltpu.VMEM((3, 80, 256), BF),
            pltpu.VMEM((80, 256), F32),
            pltpu.VMEM((80, 256), F32),
            pltpu.VMEM((8, 16, 256), F32),
            dma((1,)),
            dma((1,)),
            dma((1,)),
            dma((2, 3)),
            dma((2, 3)),
            dma((2, 3)),
            dma((2, 3)),
            dma((3,)),
            dma((3,)),
            dma((1,)),
            dma((1,)),
            dma((7,)),
            dma((7,)),
            dma((3,)),
            dma((3,)),
        ],
        compiler_params=pltpu.CompilerParams(collective_id=1, has_side_effects=True),
        name="reduce_grads",
    )(grads)
    return spread_back(pieces)


def spread_back(pieces):
    pieces = pieces[:, :, :10, :].reshape(4, 4, 2, 10, 2, 128)
    part_a = jnp.transpose(pieces[:, :, :, :, 0], (3, 2, 1, 0, 4)).reshape(10, 2, 2048)
    part_b = jnp.transpose(pieces[:, :, :, :, 1], (3, 2, 0, 1, 4)).reshape(10, 2, 2048)
    return jnp.concatenate([part_a, part_b], axis=2).reshape(10, GLANES)


def extended(x, sides, width):
    for axis, dim in sides:
        peers, length = (lax.axis_size(axis), x.shape[dim])
        up = [(i, (i + 1) % peers) for i in range(peers - 1)]
        down = [(j, i) for i, j in up]
        last = lax.slice_in_dim(x, length - width, length, axis=dim)
        first = lax.slice_in_dim(x, 0, width, axis=dim)
        before = lax.ppermute(last, axis, up)
        after = lax.ppermute(first, axis, down)
        x = jnp.concatenate([before, x, after], axis=dim)
    return x


def shifted(value, axis, steps):
    count = lax.axis_size(axis)
    first, last = (max(0, -steps), min(count, count - steps))
    return lax.ppermute(value, axis, [(source, source + steps) for source in range(first, last)])


def conv_rows(padded, weight):
    return lax.conv_general_dilated(
        padded,
        weight,
        (1, 1),
        ((0, 0), (1, 1)),
        dimension_numbers=LAYOUT,
        preferred_element_type=jnp.float32,
    )


def with_halo(source):
    return extended(source, (("rows", 2),), 1)


def mix_channels(matrix, source):
    return jnp.einsum("oi,bihw->bohw", matrix, source, preferred_element_type=jnp.float32)


def mix_back(matrix, upstream):
    return jnp.einsum("oi,bohw->bihw", matrix, upstream, preferred_element_type=jnp.float32)


def flip_kernel(weight):
    return jnp.transpose(weight[:, ::-1, ::-1, :], (3, 1, 2, 0))


def group_norm(source):
    full_shape = source.shape
    grouped = source.reshape(
        full_shape[0], GROUPS, full_shape[1] // GROUPS, full_shape[2], full_shape[3]
    )
    group_count = full_shape[1] // GROUPS * full_shape[2] * full_shape[3] * lax.axis_size("rows")
    group_total, group_square = lax.psum(
        (jnp.sum(grouped, axis=(2, 3, 4)), jnp.sum(grouped * grouped, axis=(2, 3, 4))), "rows"
    )
    average = group_total / group_count
    inv_spread = lax.rsqrt(group_square / group_count - average * average + EPSILON)
    normed = (grouped - average[:, :, None, None, None]) * inv_spread[:, :, None, None, None]
    return (normed.reshape(full_shape), inv_spread)


def norm_back(upstream, normed, inv_spread):
    full_shape = upstream.shape
    groups_here = inv_spread.shape[1]
    grouped = upstream.reshape(
        full_shape[0], groups_here, full_shape[1] // groups_here, full_shape[2], full_shape[3]
    )
    normed_grouped = normed.reshape(grouped.shape)
    group_count = (
        full_shape[1] // groups_here * full_shape[2] * full_shape[3] * lax.axis_size("rows")
    )
    group_total, group_cross = lax.psum(
        (jnp.sum(grouped, axis=(2, 3, 4)), jnp.sum(grouped * normed_grouped, axis=(2, 3, 4))),
        "rows",
    )
    first_mean = (group_total / group_count)[:, :, None, None, None]
    cross_mean = (group_cross / group_count)[:, :, None, None, None]
    result = inv_spread[:, :, None, None, None] * (
        grouped - first_mean - normed_grouped * cross_mean
    )
    return result.reshape(full_shape)


def silu_slope(values):
    sigma = jax.nn.sigmoid(values)
    return sigma * (1.0 + values * (1.0 - sigma))


def input_grad(upstream, weight):
    flipped = flip_kernel(weight)
    padded = jnp.pad(upstream, ((0, 0), (0, 0), (2, 2), (0, 0)))
    spilled = conv_rows(padded, flipped)
    from_next = shifted(spilled[:, :, :1], "rows", -1)
    from_prev = shifted(spilled[:, :, -1:], "rows", 1)
    result = spilled[:, :, 1:-1]
    result = result.at[:, :, :1].add(from_prev)
    result = result.at[:, :, -1:].add(from_next)
    return result


def kernel_grad(upstream, padded):
    wide = jnp.pad(padded, ((0, 0), (0, 0), (0, 0), (1, 1)))
    row_count = upstream.shape[2]
    col_count = upstream.shape[3]
    return jnp.stack(
        [
            jnp.stack(
                [
                    jnp.einsum(
                        "bohw,bihw->oi",
                        upstream,
                        wide[:, :, row_tap : row_tap + row_count, col_tap : col_tap + col_count],
                        preferred_element_type=jnp.float32,
                    )
                    for col_tap in range(3)
                ],
                1,
            )
            for row_tap in range(3)
        ],
        1,
    )


def block_front(source, conv_one, time_term):
    normed_in, spread_in = group_norm(source.astype(jnp.float32))
    first_halo = with_halo(jax.nn.silu(normed_in).astype(jnp.bfloat16))
    inner_sum = conv_rows(first_halo, conv_one) + time_term[:, :, None, None]
    normed, spread = group_norm(inner_sum)
    second_act = jax.nn.silu(normed).astype(jnp.bfloat16)
    return (normed_in, spread_in, first_halo, normed, spread, second_act)


def per_device(
    latent,
    hint_field,
    from_below,
    cotangent,
    timesteps,
    time_weight,
    enc_proj,
    ctl_proj,
    dec_proj,
    enc_conv_one,
    enc_conv_two,
    ctl_conv_one,
    ctl_conv_two,
    dec_conv_one,
    dec_conv_two,
    dec_shortcut,
    zero_conv,
):
    def flat(kernel, width):
        kernel = kernel.reshape(kernel.shape[0], -1)
        return jnp.pad(kernel, ((0, 0), (0, width - kernel.shape[1])))

    shard = jnp.concatenate(
        [
            flat(ctl_conv_one, 2944),
            flat(ctl_conv_two, 2944),
            flat(zero_conv, 384),
            flat(dec_shortcut, 640),
            flat(dec_conv_two, 2944),
            flat(dec_conv_one, LANES - 9856),
        ],
        axis=1,
    )
    weights = gather_weights(shard)
    ctl_one = weights[:, :2880].reshape(C, 3, 3, C)
    ctl_two = weights[:, 2944:5824].reshape(C, 3, 3, C)
    zero_full = weights[:, 5888:6208]
    dec_short = weights[:, 6272:6912]
    dec_two = weights[:, 6912:9792].reshape(C, 3, 3, C)
    dec_one = weights[:, 9856:15616].reshape(C, 3, 3, 2 * C)
    half_width = C // 2
    frequency = jnp.exp(-math.log(10000.0) * jnp.arange(half_width, dtype=jnp.float32) / half_width)
    angles = timesteps.astype(jnp.float32)[:, None] * frequency[None, :]
    sinusoid = jnp.concatenate([jnp.cos(angles), jnp.sin(angles)], axis=1).astype(jnp.bfloat16)
    time_embed = jnp.dot(sinusoid, time_weight, preferred_element_type=jnp.float32)
    time_act = jax.nn.silu(time_embed).astype(jnp.bfloat16)
    enc_term = jnp.dot(time_act, enc_proj, preferred_element_type=jnp.float32)
    ctl_term = jnp.dot(time_act, ctl_proj, preferred_element_type=jnp.float32)
    dec_term = jnp.dot(time_act, dec_proj, preferred_element_type=jnp.float32)
    enc_parts = block_front(latent, enc_conv_one, enc_term)
    enc_out = (
        latent.astype(jnp.float32) + conv_rows(with_halo(enc_parts[5]), enc_conv_two)
    ).astype(jnp.bfloat16)
    ctl_in = (latent.astype(jnp.float32) + hint_field.astype(jnp.float32)).astype(jnp.bfloat16)
    ctl_parts = block_front(ctl_in, ctl_one, ctl_term)
    ctl_halo = with_halo(ctl_parts[5])
    ctl_out = (ctl_in.astype(jnp.float32) + conv_rows(ctl_halo, ctl_two)).astype(jnp.bfloat16)
    skip_sum = (enc_out.astype(jnp.float32) + mix_channels(zero_full, ctl_out)).astype(jnp.bfloat16)
    joined = jnp.concatenate([from_below, skip_sum], axis=1)
    dec_parts = block_front(joined, dec_one, dec_term)
    loss_scale = float(
        cotangent.shape[0]
        * lax.axis_size("dp")
        * cotangent.shape[2]
        * lax.axis_size("rows")
        * cotangent.shape[3]
    ) ** (-0.5)
    out_grad = (cotangent.astype(jnp.float32) * loss_scale).astype(jnp.bfloat16)
    dec_second_grad = input_grad(out_grad, dec_two)
    dec_inner_grad = norm_back(
        dec_second_grad * silu_slope(dec_parts[3]), dec_parts[3], dec_parts[4]
    ).astype(jnp.bfloat16)
    skip_first_grad = input_grad(dec_inner_grad, dec_one[:, :, :, C:])
    skip_normed = dec_parts[0][:, C:]
    skip_spread = dec_parts[1][:, GROUPS // 2 :]
    skip_grad = norm_back(
        skip_first_grad * silu_slope(skip_normed), skip_normed, skip_spread
    ) + mix_back(dec_short[:, C:], out_grad)
    skip_grad = skip_grad.astype(jnp.bfloat16)
    zero_local = jnp.einsum("bohw,bihw->oi", skip_grad, ctl_out, preferred_element_type=jnp.float32)
    ctl_out_grad = mix_back(zero_full, skip_grad).astype(jnp.bfloat16)
    two_local = kernel_grad(ctl_out_grad, ctl_halo)
    ctl_second_grad = input_grad(ctl_out_grad, ctl_two)
    ctl_inner_grad = norm_back(
        ctl_second_grad * silu_slope(ctl_parts[3]), ctl_parts[3], ctl_parts[4]
    ).astype(jnp.bfloat16)
    one_local = kernel_grad(ctl_inner_grad, ctl_parts[2])
    grads = jnp.concatenate(
        [
            flat(one_local.astype(BF), 2944),
            flat(two_local.astype(BF), 2944),
            flat(zero_local.astype(BF), GLANES - 5888),
        ],
        axis=1,
    )
    owned = reduce_grads(grads)
    return (
        owned[:, :2880].reshape(10, 3, 3, C),
        owned[:, 2944:5824].reshape(10, 3, 3, C),
        owned[:, 5888:6208],
    )


def solution(mesh):
    in_specs = (
        P("dp", None, "rows", None),
        P("dp", None, "rows", None),
        P("dp", None, "rows", None),
        P("dp", None, "rows", None),
        P("dp"),
        P(),
        P(),
        P(),
        P(),
        P(),
        P(),
        P("dp", None, None, None),
        P("dp", None, None, None),
        P("dp", None, None, None),
        P("dp", None, None, None),
        P("dp", None),
        P("dp", None),
    )
    out_specs = (P("dp", None, None, None), P("dp", None, None, None), P("dp", None))
    return jax.shard_map(
        per_device, mesh=mesh, in_specs=in_specs, out_specs=out_specs, check_vma=False
    )
```

```python
import math

import jax
import jax.numpy as jnp
from jax import lax
from jax.experimental import pallas as pl
from jax.experimental.pallas import tpu as pltpu
from jax.sharding import PartitionSpec as P

C = 320
EPSILON = 1e-05

MESH = pl.DeviceIdType.MESH
LANES = 16384
GLANES = 8192
BF = jnp.bfloat16
F32 = jnp.float32


def place():
    d = lax.axis_index("dp")
    r = lax.axis_index("rows")
    return (d // 8, (d // 2) % 4, d % 2, r // 4, r % 4)


def device_of(zh, y, c, zl, x):
    return (zh * 8 + y * 2 + c, zl * 4 + x)


def remote(src, dst, send, recv, where):
    return pltpu.make_async_remote_copy(
        src_ref=src, dst_ref=dst, send_sem=send, recv_sem=recv, device_id=where, device_id_type=MESH
    )


def torus_peers(me):
    zh, y, c, zl, x = me
    found = []
    for k in range(1, 8):
        s = (y * 2 + c + k) % 8
        found.append(device_of(zh, s // 2, s % 2, zl, x))
    for k in range(1, 4):
        found.append(device_of((zh + k) % 4, y, c, zl, x))
        found.append(device_of(zh, y, c, zl, (x + k) % 4))
    return found


def greet(peers):
    barrier = pltpu.get_barrier_semaphore()
    for where in peers:
        pl.semaphore_signal(barrier, inc=1, device_id=where, device_id_type=MESH)
    pl.semaphore_wait(barrier, len(peers))


def gather_kernel(
    src, out, parts, column, wide, own_sem, send1, recv1, send2, recv2, send3, recv3, send4, recv4, send5, recv5
):
    me = place()
    zh, y, c, zl, x = me
    slot = y * 2 + c
    greet(torus_peers(me))
    first = []
    for k in range(1, 8):
        s = (slot + k) % 8
        first.append(
            remote(src.at[s], parts.at[slot], send1.at[k - 1], recv1.at[k - 1], device_of(zh, s // 2, s % 2, zl, x))
        )
        first[-1].start()
    mine = pltpu.make_async_copy(src.at[slot], parts.at[slot], own_sem.at[0])
    mine.start()
    mine.wait()
    for copy in first:
        copy.wait_recv()
    for s in range(8):
        column[10 * s : 10 * s + 10, :] = parts[s, 0:10, :].astype(F32)
    home = pl.multiple_of(zh * 80, 80)
    wide[pl.ds(home, 80), :] = column[...].astype(BF)
    second = []
    for k in range(1, 4):
        second.append(
            remote(
                wide.at[pl.ds(home, 80)],
                wide.at[pl.ds(home, 80)],
                send2.at[k - 1],
                recv2.at[k - 1],
                device_of((zh + k) % 4, y, c, zl, x),
            )
        )
        second[-1].start()
    for copy in second:
        copy.wait_recv()
    spot_a = pl.multiple_of(((y * 2 + c) * 4 + x) * 256, 256)
    spot_b = pl.multiple_of(8192 + ((x * 2 + c) * 4 + y) * 256, 256)
    third = []
    for k in range(1, 4):
        third.append(
            remote(
                wide.at[:, 0:256],
                out.at[:, pl.ds(spot_a, 256)],
                send3.at[0, k - 1],
                recv3.at[0, k - 1],
                device_of(zh, y, c, zl, (x + k) % 4),
            )
        )
        third.append(
            remote(
                wide.at[:, 256:512],
                out.at[:, pl.ds(spot_b, 256)],
                send3.at[1, k - 1],
                recv3.at[1, k - 1],
                device_of(zh, (y + k) % 4, c, zl, x),
            )
        )
    for copy in third:
        copy.start()
    mine_a = pltpu.make_async_copy(wide.at[:, 0:256], out.at[:, pl.ds(spot_a, 256)], own_sem.at[1])
    mine_b = pltpu.make_async_copy(wide.at[:, 256:512], out.at[:, pl.ds(spot_b, 256)], own_sem.at[2])
    mine_a.start()
    mine_b.start()
    mine_a.wait()
    mine_b.wait()
    for copy in third:
        copy.wait_recv()
    partner = device_of(zh, y, 1 - c, zl, x)
    row_a = pl.multiple_of((y * 2 + c) * 1024, 1024)
    row_b = pl.multiple_of(8192 + (x * 2 + c) * 1024, 1024)
    fourth = []
    fifth = []
    for k in range(1, 4):
        fourth.append(
            remote(
                out.at[:, pl.ds(row_a, 1024)],
                out.at[:, pl.ds(row_a, 1024)],
                send4.at[0, k - 1],
                recv4.at[0, k - 1],
                device_of(zh, (y + k) % 4, c, zl, x),
            )
        )
        fourth.append(
            remote(
                out.at[:, pl.ds(row_b, 1024)],
                out.at[:, pl.ds(row_b, 1024)],
                send4.at[1, k - 1],
                recv4.at[1, k - 1],
                device_of(zh, y, c, zl, (x + k) % 4),
            )
        )
    for copy in fourth:
        copy.start()
    for k in range(4):
        if k > 0:
            fourth[2 * k - 2].wait_recv()
            fourth[2 * k - 1].wait_recv()
        from_a = pl.multiple_of(((y + 4 - k) % 4 * 2 + c) * 1024, 1024)
        from_b = pl.multiple_of(8192 + ((x + 4 - k) % 4 * 2 + c) * 1024, 1024)
        for which, spot in ((0, from_a), (1, from_b)):
            copy = remote(
                out.at[:, pl.ds(spot, 1024)],
                out.at[:, pl.ds(spot, 1024)],
                send5.at[which, k],
                recv5.at[which, k],
                partner,
            )
            copy.start()
            fifth.append(copy)
    for copy in fifth:
        copy.wait_recv()
    for copy in first + second + third + fourth + fifth:
        copy.wait_send()


def gather_weights(shard):
    x = lax.axis_index("rows") % 4
    half_a = shard[:, :8192].reshape(10, 4, 2, 4, 256)
    half_b = shard[:, 8192:].reshape(10, 4, 2, 4, 256)
    part_a = lax.dynamic_index_in_dim(half_a, x, 3, keepdims=False)
    part_b = lax.dynamic_index_in_dim(half_b, x, 1, keepdims=False)
    part_b = jnp.transpose(part_b, (0, 2, 1, 3))
    both = jnp.concatenate([part_a, part_b], axis=3)
    both = jnp.transpose(both, (1, 2, 0, 3)).reshape(8, 10, 512)
    both = jnp.pad(both, ((0, 0), (0, 6), (0, 0)))
    dma = pltpu.SemaphoreType.DMA
    return pl.pallas_call(
        gather_kernel,
        out_shape=jax.ShapeDtypeStruct((320, LANES), BF),
        in_specs=[pl.BlockSpec(memory_space=pltpu.VMEM)],
        out_specs=pl.BlockSpec(memory_space=pl.ANY),
        scratch_shapes=[
            pltpu.VMEM((8, 16, 512), BF),
            pltpu.VMEM((80, 512), F32),
            pltpu.VMEM((320, 512), BF),
            dma((3,)),
            dma((7,)),
            dma((7,)),
            dma((3,)),
            dma((3,)),
            dma((2, 3)),
            dma((2, 3)),
            dma((2, 3)),
            dma((2, 3)),
            dma((2, 4)),
            dma((2, 4)),
        ],
        compiler_params=pltpu.CompilerParams(collective_id=0, has_side_effects=True),
        name="gather_weights",
    )(both)


def reduce_kernel(
    grads,
    out,
    swap,
    half,
    far,
    near,
    near_in,
    last,
    deep,
    deep_in,
    plane,
    plane_in,
    spread,
    own_sem,
    send1,
    recv1,
    send2,
    recv2,
    send3,
    recv3,
    send4,
    recv4,
    send5,
    recv5,
    send6,
    recv6,
    send7,
    recv7,
):
    me = place()
    zh, y, c, zl, x = me
    slot = y * 2 + c
    other_z = device_of(zh, y, c, 1 - zl, x)
    greet(torus_peers(me) + [other_z])
    partner = device_of(zh, y, 1 - c, zl, x)
    theirs = pl.multiple_of((1 - c) * 4096, 4096)
    ours = pl.multiple_of(c * 4096, 4096)
    one = remote(grads.at[:, pl.ds(theirs, 4096)], swap, send1.at[0], recv1.at[0], partner)
    one.start()
    one.wait_recv()

    @pl.loop(0, 20)
    def _(i):
        rows = pl.ds(pl.multiple_of(i * 16, 16), 16)
        total = grads[rows, pl.ds(ours, 4096)].astype(F32) + swap[rows, :].astype(F32)
        half[rows, :] = total.astype(BF)

    second = []
    for k in range(1, 4):
        ya = (y + k) % 4
        xb = (x + k) % 4
        second.append(
            remote(
                half.at[:, pl.ds(pl.multiple_of(ya * 512, 512), 512)],
                far.at[0, k - 1],
                send2.at[0, k - 1],
                recv2.at[0, k - 1],
                device_of(zh, ya, c, zl, x),
            )
        )
        second.append(
            remote(
                half.at[:, pl.ds(pl.multiple_of(2048 + xb * 512, 512), 512)],
                far.at[1, k - 1],
                send2.at[1, k - 1],
                recv2.at[1, k - 1],
                device_of(zh, y, c, zl, xb),
            )
        )
    for copy in second:
        copy.start()
    for copy in second:
        copy.wait_recv()
    mine_a = pl.ds(pl.multiple_of(y * 512, 512), 512)
    mine_b = pl.ds(pl.multiple_of(2048 + x * 512, 512), 512)

    @pl.loop(0, 20)
    def _(i):
        rows = pl.ds(pl.multiple_of(i * 16, 16), 16)
        for which, lanes in ((0, mine_a), (1, mine_b)):
            total = half[rows, lanes].astype(F32)
            for k in range(3):
                total = total + far[which, k, rows, :].astype(F32)
            near[which, rows, :] = total.astype(BF)

    third = []
    for k in range(1, 4):
        xa = (x + k) % 4
        yb = (y + k) % 4
        third.append(
            remote(
                near.at[0, :, pl.ds(pl.multiple_of(xa * 128, 128), 128)],
                near_in.at[0, k - 1],
                send3.at[0, k - 1],
                recv3.at[0, k - 1],
                device_of(zh, y, c, zl, xa),
            )
        )
        third.append(
            remote(
                near.at[1, :, pl.ds(pl.multiple_of(yb * 128, 128), 128)],
                near_in.at[1, k - 1],
                send3.at[1, k - 1],
                recv3.at[1, k - 1],
                device_of(zh, yb, c, zl, x),
            )
        )
    for copy in third:
        copy.start()
    for copy in third:
        copy.wait_recv()
    for which, where in ((0, x), (1, y)):
        total = near[which, :, pl.ds(pl.multiple_of(where * 128, 128), 128)].astype(F32)
        for k in range(3):
            total = total + near_in[which, k].astype(F32)
        deep[:, which * 128 : which * 128 + 128] = total.astype(BF)

    fourth = []
    for k in range(1, 4):
        zt = (zh + k) % 4
        fourth.append(
            remote(
                deep.at[pl.ds(pl.multiple_of(zt * 80, 80), 80)],
                deep_in.at[k - 1],
                send4.at[k - 1],
                recv4.at[k - 1],
                device_of(zt, y, c, zl, x),
            )
        )
        fourth[-1].start()
    for copy in fourth:
        copy.wait_recv()
    total = deep[pl.ds(pl.multiple_of(zh * 80, 80), 80), :].astype(F32)
    for k in range(3):
        total = total + deep_in[k].astype(F32)
    plane[...] = total
    five = remote(plane, plane_in, send5.at[0], recv5.at[0], other_z)
    five.start()
    five.wait_recv()
    last[...] = plane[...] + plane_in[...]
    for s in range(8):
        spread[s, 0:10, :] = last[10 * s : 10 * s + 10, :]
        spread[s, 10:16, :] = jnp.zeros((6, 256), F32)
    sixth = []
    for k in range(1, 8):
        s = (slot + k) % 8
        sixth.append(
            remote(
                spread.at[s],
                out.at[x, slot],
                send6.at[k - 1],
                recv6.at[k - 1],
                device_of(zh, s // 2, s % 2, zl, x),
            )
        )
        sixth[-1].start()
    mine = pltpu.make_async_copy(spread.at[slot], out.at[x, slot], own_sem.at[0])
    mine.start()
    mine.wait()
    for copy in sixth:
        copy.wait_recv()
    seventh = []
    for k in range(1, 4):
        seventh.append(
            remote(out.at[x], out.at[x], send7.at[k - 1], recv7.at[k - 1], device_of(zh, y, c, zl, (x + k) % 4))
        )
        seventh[-1].start()
    for copy in seventh:
        copy.wait_recv()
    for copy in [one] + second + third + fourth + [five] + sixth + seventh:
        copy.wait_send()


def reduce_grads(grads):
    dma = pltpu.SemaphoreType.DMA
    pieces = pl.pallas_call(
        reduce_kernel,
        out_shape=jax.ShapeDtypeStruct((4, 8, 16, 256), F32),
        in_specs=[pl.BlockSpec(memory_space=pltpu.VMEM)],
        out_specs=pl.BlockSpec(memory_space=pltpu.VMEM),
        scratch_shapes=[
            pltpu.VMEM((320, 4096), BF),
            pltpu.VMEM((320, 4096), BF),
            pltpu.VMEM((2, 3, 320, 512), BF),
            pltpu.VMEM((2, 320, 512), BF),
            pltpu.VMEM((2, 3, 320, 128), BF),
            pltpu.VMEM((80, 256), F32),
            pltpu.VMEM((320, 256), BF),
            pltpu.VMEM((3, 80, 256), BF),
            pltpu.VMEM((80, 256), F32),
            pltpu.VMEM((80, 256), F32),
            pltpu.VMEM((8, 16, 256), F32),
            dma((1,)),
            dma((1,)),
            dma((1,)),
            dma((2, 3)),
            dma((2, 3)),
            dma((2, 3)),
            dma((2, 3)),
            dma((3,)),
            dma((3,)),
            dma((1,)),
            dma((1,)),
            dma((7,)),
            dma((7,)),
            dma((3,)),
            dma((3,)),
        ],
        compiler_params=pltpu.CompilerParams(collective_id=1, has_side_effects=True),
        name="reduce_grads",
    )(grads)
    return spread_back(pieces)


def spread_back(pieces):
    pieces = pieces[:, :, :10, :].reshape(4, 4, 2, 10, 2, 128)
    part_a = jnp.transpose(pieces[:, :, :, :, 0], (3, 2, 1, 0, 4)).reshape(10, 2, 2048)
    part_b = jnp.transpose(pieces[:, :, :, :, 1], (3, 2, 0, 1, 4)).reshape(10, 2, 2048)
    return jnp.concatenate([part_a, part_b], axis=2).reshape(10, GLANES)


ROWS = 16
STEPS = C // ROWS
NT = (((1,), (1,)), ((), ()))
TN = (((0,), (0,)), ((), ()))
EXACT = lax.Precision.HIGHEST
AT_CTL_ONE = 0
AT_CTL_TWO = 2944
AT_ZERO = 5888
AT_SHORT = 6272
AT_DEC_TWO = 6656
AT_DEC_ONE = 9600


def band(i):
    return pl.ds(pl.multiple_of(i * ROWS, ROWS), ROWS)


def put_columns(col, base_of, i, strips):
    lane = lax.broadcasted_iota(jnp.int32, (ROWS, 128), 1)
    shifted_of = []
    for strip in strips:
        left = jnp.where(lane == 0, 0.0, pltpu.roll(strip, 1, axis=1))
        right = jnp.where(lane == 127, 0.0, pltpu.roll(strip, 127, axis=1))
        shifted_of.append([left.astype(BF), strip.astype(BF), right.astype(BF)])
    for p in range(3):
        for q in range(3):
            start = pl.multiple_of(base_of(3 * p + q) + i * ROWS, ROWS)
            col[pl.ds(start, ROWS), 0:128] = shifted_of[p][q]
            col[pl.ds(start, ROWS), 128:256] = shifted_of[p + 1][q]


def sig(v):
    return jax.nn.sigmoid(v)


def slope(v):
    s = sig(v)
    return s * (1.0 + v * (1.0 - s))


def dot(a, b):
    return jnp.dot(a, b, preferred_element_type=F32)


def put_sums(cols, at, i, pairs):
    for k, value in enumerate(pairs):
        cols[band(i), at + k : at + k + 1] = jnp.sum(value, axis=1, keepdims=True)


def mid_kernel(
    acts,
    terms,
    enc_one,
    enc_two,
    weights,
    grads,
    member,
    ten,
    twenty,
    cols,
    coef,
    halo,
    halo_cot,
    inner,
    inner_halo,
    edge,
    col_t,
    col_a,
    col_b,
    col_d,
    col_g,
    back_dec_two,
    back_dec_one,
    back_ctl_two,
    zero_t,
    short_t,
    enc_raw,
    ctl_raw,
    ctl_out,
    skip,
    skip_halo,
    dec_raw,
    dec_halo,
    dec_edge,
    up_grad,
    sfg,
    sfg_edge,
    sfg_halo,
    keep_n,
    keep_skip,
    keep_dec,
    mixed,
    wide,
    wide_two,
    note,
    note_in,
    note_send,
    note_recv,
    halo_send,
    halo_recv,
):
    d = lax.axis_index("dp")
    r = lax.axis_index("rows")
    peers = [(d, (r + k) % 8) for k in range(1, 8)]
    greet(peers)
    before = (d, (r + 7) % 8)
    after = (d, (r + 1) % 8)
    waiting = []

    def send_rows(event, top, bottom, above, below):
        first = remote(top, below, halo_send.at[event, 0], halo_recv.at[event, 0], before)
        second = remote(bottom, above, halo_send.at[event, 1], halo_recv.at[event, 1], after)
        first.start()
        second.start()
        waiting.extend([first, second])
        return (first, second)

    def arrive(pair):
        pair[0].wait_recv()
        pair[1].wait_recv()

    raw = send_rows(
        0, acts.at[0:2, :, 0:128], acts.at[0:2, :, 128:256], halo.at[0, 0:2], halo.at[1, 0:2]
    )
    late = send_rows(1, acts.at[2, :, 0:128], acts.at[2, :, 128:256], halo.at[0, 2], halo.at[1, 2])
    late_cot = send_rows(2, acts.at[3], acts.at[3], halo_cot.at[0], halo_cot.at[1])

    lane = lax.broadcasted_iota(jnp.int32, (C, 128), 1)
    channel = lax.broadcasted_iota(jnp.int32, (C, 128), 0)
    in_ten = (channel >= 10 * lane) & (channel < 10 * lane + 10)
    other = lane - 32
    in_twenty = (channel >= 20 * other) & (channel < 20 * other + 20)
    ten[...] = jnp.where(in_ten, 1.0, 0.0)
    twenty[...] = jnp.where(in_twenty, 1.0, 0.0)
    member[...] = ten[...] + twenty[...]
    cols[...] = jnp.zeros((C, 128), F32)

    def share(turn):
        sums = lax.dot_general(cols[...], member[...], TN, precision=EXACT, preferred_element_type=F32)
        note[turn] = sums[0:8]
        copies = []
        for k in range(1, 8):
            copies.append(
                remote(
                    note.at[turn],
                    note_in.at[turn, k - 1],
                    note_send.at[turn, k - 1],
                    note_recv.at[turn, k - 1],
                    peers[k - 1],
                )
            )
            copies[-1].start()
        waiting.extend(copies)
        return copies

    def collect(turn, copies):
        for copy in copies:
            copy.wait_recv()
        total = note[turn]
        for k in range(7):
            total = total + note_in[turn, k]
        return total

    which = lax.broadcasted_iota(jnp.int32, (8, 128), 1)
    per_group = jnp.where(which < 32, 1.0 / (10 * 2048), 1.0 / (20 * 2048))

    def spread(table, at, rows):
        padded = jnp.concatenate(rows + [jnp.zeros((8 - len(rows), 128), F32)], axis=0)
        coef[:, at : at + 8] = lax.dot_general(
            table[...], padded, NT, precision=EXACT, preferred_element_type=F32
        )

    def norm_rows(total, k):
        mean = total[k : k + 1] * per_group[0:1]
        square = total[k + 1 : k + 2] * per_group[0:1]
        return [mean, lax.rsqrt(square - mean * mean + EPSILON)]

    def mean_rows(total, k):
        return [total[k : k + 1] * per_group[0:1], total[k + 1 : k + 2] * per_group[0:1]]

    has_up = r > 0
    has_down = r < 7

    def masked(strips):
        return [
            jnp.where(has_up, strips[0], 0.0),
            strips[1],
            strips[2],
            jnp.where(has_down, strips[3], 0.0),
        ]

    @pl.loop(0, STEPS)
    def _(i):
        latent = acts[0, band(i), :].astype(F32)
        ctl_in = (latent + acts[1, band(i), :].astype(F32)).astype(BF).astype(F32)
        under = acts[2, band(i), :].astype(F32)
        put_sums(cols, 0, i, [latent, latent * latent, ctl_in, ctl_in * ctl_in, under, under * under])

    first_note = share(0)

    for target in (back_dec_two, back_dec_one, back_ctl_two):
        target[...] = jnp.zeros((C, 3456), BF)
    for target, start, stride in (
        (back_dec_two, AT_DEC_TWO, 320),
        (back_dec_one, AT_DEC_ONE + 320, 640),
        (back_ctl_two, AT_CTL_TWO, 320),
    ):
        for tap in range(9):
            block = weights[:, start + stride * tap : start + stride * tap + 320].astype(F32)
            target[:, 384 * (8 - tap) : 384 * (8 - tap) + 320] = block.T.astype(BF)
    zero_t[...] = weights[:, AT_ZERO : AT_ZERO + 320].astype(F32).T.astype(BF)
    short_t[...] = weights[:, AT_SHORT : AT_SHORT + 320].astype(F32).T.astype(BF)
    for tap in range(9):
        col_g[384 * tap + 320 : 384 * tap + 384, :] = jnp.zeros((64, 256), BF)

    total = collect(0, first_note)
    spread(ten, 0, norm_rows(total, 0) + norm_rows(total, 2))
    spread(twenty, 8, norm_rows(total, 4))
    arrive(raw)

    def plain(tap):
        return 320 * tap

    def first_act(source_of, at, col, base_of):
        @pl.loop(0, STEPS)
        def _(i):
            mean = coef[band(i), at : at + 1]
            inv = coef[band(i), at + 1 : at + 2]
            strips = []
            for strip in source_of(i):
                normed = (strip - mean) * inv
                strips.append(normed * sig(normed))
            put_columns(col, base_of, i, masked(strips))

    def latent_of(i):
        own = acts[0, band(i), :].astype(F32)
        return [halo[0, 0, band(i), :].astype(F32), own[:, 0:128], own[:, 128:256], halo[1, 0, band(i), :].astype(F32)]

    def ctl_in_of(i):
        own = acts[1, band(i), :].astype(F32)
        hint = [halo[0, 1, band(i), :].astype(F32), own[:, 0:128], own[:, 128:256], halo[1, 1, band(i), :].astype(F32)]
        return [(a + b).astype(BF).astype(F32) for a, b in zip(latent_of(i), hint)]

    first_act(latent_of, 0, col_t, plain)
    enc_raw[...] = dot(enc_one[...], col_t[...])
    edge[0] = enc_raw[:, 0:128].astype(BF)
    edge[1] = enc_raw[:, 128:256].astype(BF)
    enc_rows = send_rows(3, edge.at[0], edge.at[1], inner_halo.at[0], inner_halo.at[1])
    first_act(ctl_in_of, 2, col_a, plain)
    ctl_raw[...] = dot(weights[:, AT_CTL_ONE : AT_CTL_ONE + 2880], col_a[...])
    edge[2] = ctl_raw[:, 0:128].astype(BF)
    edge[3] = ctl_raw[:, 128:256].astype(BF)
    ctl_rows = send_rows(4, edge.at[2], edge.at[3], inner_halo.at[2], inner_halo.at[3])

    @pl.loop(0, STEPS)
    def _(i):
        enc = enc_raw[band(i), :] + terms[band(i), 0:1]
        ctl = ctl_raw[band(i), :] + terms[band(i), 1:2]
        put_sums(cols, 0, i, [enc, enc * enc, ctl, ctl * ctl])

    second_note = share(1)

    def under_of(i):
        own = acts[2, band(i), :].astype(F32)
        return [halo[0, 2, band(i), :].astype(F32), own[:, 0:128], own[:, 128:256], halo[1, 2, band(i), :].astype(F32)]

    def joined_low(tap):
        return 640 * tap

    def joined_high(tap):
        return 640 * tap + 320

    def spaced(tap):
        return 384 * tap

    arrive(late)
    first_act(under_of, 8, col_d, joined_low)

    total = collect(1, second_note)
    spread(ten, 16, norm_rows(total, 0) + norm_rows(total, 2))

    def second_act(raw_ref, at_halo, term_at, at, col, keep):
        @pl.loop(0, STEPS)
        def _(i):
            mean = coef[band(i), at : at + 1]
            inv = coef[band(i), at + 1 : at + 2]
            own = raw_ref[band(i), :]
            term = terms[band(i), term_at : term_at + 1]
            strips = []
            for strip in (
                inner_halo[at_halo, band(i), :].astype(F32),
                own[:, 0:128],
                own[:, 128:256],
                inner_halo[at_halo + 1, band(i), :].astype(F32),
            ):
                strips.append((strip + term - mean) * inv)
            if keep is not None:
                keep[band(i), 0:128] = strips[1]
                keep[band(i), 128:256] = strips[2]
            put_columns(col, plain, i, masked([v * sig(v) for v in strips]))

    arrive(enc_rows)
    second_act(enc_raw, 0, 0, 16, col_t, None)
    enc_raw[...] = dot(enc_two[...], col_t[...])
    arrive(ctl_rows)
    second_act(ctl_raw, 2, 1, 18, col_b, keep_n)
    inner[...] = dot(weights[:, AT_CTL_TWO : AT_CTL_TWO + 2880], col_b[...])

    @pl.loop(0, STEPS)
    def _(i):
        latent = acts[0, band(i), :].astype(F32)
        ctl_in = (latent + acts[1, band(i), :].astype(F32)).astype(BF).astype(F32)
        ctl_out[band(i), :] = (ctl_in + inner[band(i), :]).astype(BF)

    inner[...] = dot(weights[:, AT_ZERO : AT_ZERO + 320], ctl_out[...])

    @pl.loop(0, STEPS)
    def _(i):
        latent = acts[0, band(i), :].astype(F32)
        enc_out = (latent + enc_raw[band(i), :]).astype(BF).astype(F32)
        joined = (enc_out + inner[band(i), :]).astype(BF)
        skip[0, band(i), :] = joined[:, 0:128]
        skip[1, band(i), :] = joined[:, 128:256]
        value = joined.astype(F32)
        put_sums(cols, 0, i, [value, value * value])

    skip_rows = send_rows(5, skip.at[0], skip.at[1], skip_halo.at[0], skip_halo.at[1])
    third_note = share(2)

    arrive(late_cot)
    scale = 2.0**-8

    def cot_of(i):
        far = halo_cot[0, band(i), :].astype(F32)
        own = acts[3, band(i), :].astype(F32)
        near = halo_cot[1, band(i), :].astype(F32)
        far = jnp.where(has_up, far, 0.0) * scale
        near = jnp.where(has_down, near, 0.0) * scale
        own = own * scale
        return [far[:, 0:128], far[:, 128:256], own[:, 0:128], own[:, 128:256], near[:, 0:128], near[:, 128:256]]

    for part in range(2):

        @pl.loop(0, STEPS)
        def _(i):
            strips = cot_of(i)[2 * part : 2 * part + 4]
            put_columns(col_g, spaced, i, strips)

        up_grad[:, 256 * part : 256 * part + 256] = dot(back_dec_two[...], col_g[...])

    @pl.loop(0, STEPS)
    def _(i):
        for k, strip in enumerate(cot_of(i)[1:5]):
            wide[band(i), 128 * k : 128 * k + 128] = strip.astype(BF)

    mixed[...] = dot(short_t[...], wide[...])

    total = collect(2, third_note)
    spread(twenty, 24, norm_rows(total, 0))
    arrive(skip_rows)

    @pl.loop(0, STEPS)
    def _(i):
        mean = coef[band(i), 24:25]
        inv = coef[band(i), 25:26]
        strips = []
        for k, strip in enumerate(
            (skip_halo[0, band(i), :], skip[0, band(i), :], skip[1, band(i), :], skip_halo[1, band(i), :])
        ):
            normed = (strip.astype(F32) - mean) * inv
            keep_skip[band(i), 128 * k : 128 * k + 128] = normed
            strips.append(normed * sig(normed))
        put_columns(col_d, joined_high, i, masked(strips))

    dec_raw[...] = dot(weights[:, AT_DEC_ONE : AT_DEC_ONE + 5760], col_d[...])
    dec_edge[0] = dec_raw[:, 0:128].astype(BF)
    dec_edge[1] = dec_raw[:, 128:256].astype(BF)
    dec_rows = send_rows(6, dec_edge.at[0], dec_edge.at[1], dec_halo.at[0], dec_halo.at[1])

    @pl.loop(0, STEPS)
    def _(i):
        value = dec_raw[band(i), :] + terms[band(i), 2:3]
        put_sums(cols, 0, i, [value, value * value])

    fourth_note = share(3)
    total = collect(3, fourth_note)
    spread(ten, 32, norm_rows(total, 0))

    def keep_dec_rows(i, strip, k):
        mean = coef[band(i), 32:33]
        inv = coef[band(i), 33:34]
        term = terms[band(i), 2:3]
        normed = (strip + term - mean) * inv
        keep_dec[band(i), 128 * k : 128 * k + 128] = normed
        upstream = up_grad[band(i), 128 * k : 128 * k + 128] * slope(normed)
        up_grad[band(i), 128 * k : 128 * k + 128] = upstream
        return (normed, upstream)

    @pl.loop(0, STEPS)
    def _(i):
        one_n, one_g = keep_dec_rows(i, dec_raw[band(i), 0:128], 1)
        two_n, two_g = keep_dec_rows(i, dec_raw[band(i), 128:256], 2)
        put_sums(cols, 0, i, [one_g + two_g, one_g * one_n + two_g * two_n])

    fifth_note = share(4)
    arrive(dec_rows)

    @pl.loop(0, STEPS)
    def _(i):
        keep_dec_rows(i, dec_halo[0, band(i), :].astype(F32), 0)
        keep_dec_rows(i, dec_halo[1, band(i), :].astype(F32), 3)

    total = collect(4, fifth_note)
    spread(ten, 40, mean_rows(total, 0))

    @pl.loop(0, STEPS)
    def _(i):
        inv = coef[band(i), 33:34]
        mean = coef[band(i), 40:41]
        cross = coef[band(i), 41:42]
        strips = []
        for k in range(4):
            lanes = slice(128 * k, 128 * k + 128)
            strips.append(inv * (up_grad[band(i), lanes] - mean - keep_dec[band(i), lanes] * cross))
        put_columns(col_g, spaced, i, masked(strips))

    sfg[...] = dot(back_dec_one[...], col_g[...])
    sfg_edge[0] = sfg[:, 0:128].astype(BF)
    sfg_edge[1] = sfg[:, 128:256].astype(BF)
    sfg_rows = send_rows(7, sfg_edge.at[0], sfg_edge.at[1], sfg_halo.at[0], sfg_halo.at[1])

    @pl.loop(0, STEPS)
    def _(i):
        normed = keep_skip[band(i), 128:384]
        value = sfg[band(i), :] * slope(normed)
        up_grad[band(i), 128:384] = value
        put_sums(cols, 0, i, [value, value * normed])

    sixth_note = share(5)
    arrive(sfg_rows)

    @pl.loop(0, STEPS)
    def _(i):
        for at, lanes in ((0, slice(0, 128)), (1, slice(384, 512))):
            up_grad[band(i), lanes] = sfg_halo[at, band(i), :].astype(F32) * slope(keep_skip[band(i), lanes])

    total = collect(5, sixth_note)
    spread(twenty, 48, mean_rows(total, 0))

    @pl.loop(0, STEPS)
    def _(i):
        inv = coef[band(i), 25:26]
        mean = coef[band(i), 48:49]
        cross = coef[band(i), 49:50]
        value = inv * (up_grad[band(i), :] - mean - keep_skip[band(i), :] * cross) + mixed[band(i), :]
        wide[band(i), :] = value.astype(BF)

    up_grad[...] = dot(zero_t[...], wide[...])

    @pl.loop(0, STEPS)
    def _(i):
        strips = []
        for k in range(4):
            strips.append(up_grad[band(i), 128 * k : 128 * k + 128].astype(BF).astype(F32))
        wide_two[band(i), 0:128] = strips[1].astype(BF)
        wide_two[band(i), 128:256] = strips[2].astype(BF)
        put_columns(col_g, spaced, i, masked(strips))

    sfg[...] = dot(back_ctl_two[...], col_g[...])

    @pl.loop(0, STEPS)
    def _(i):
        normed = keep_n[band(i), :]
        value = sfg[band(i), :] * slope(normed)
        sfg[band(i), :] = value
        put_sums(cols, 0, i, [value, value * normed])

    seventh_note = share(6)
    grads[:, 2944:5824] = lax.dot_general(
        wide_two[...], col_b[...], NT, preferred_element_type=F32
    ).astype(BF)
    grads[:, 5888:6208] = lax.dot_general(
        wide[:, 128:384], ctl_out[...], NT, preferred_element_type=F32
    ).astype(BF)
    grads[:, 6272:GLANES] = jnp.zeros((C, GLANES - 6272), BF)
    total = collect(6, seventh_note)
    spread(ten, 56, mean_rows(total, 0))

    @pl.loop(0, STEPS)
    def _(i):
        inv = coef[band(i), 19:20]
        mean = coef[band(i), 56:57]
        cross = coef[band(i), 57:58]
        value = inv * (sfg[band(i), :] - mean - keep_n[band(i), :] * cross)
        wide_two[band(i), :] = value.astype(BF)

    grads[:, 0:2880] = lax.dot_general(wide_two[...], col_a[...], NT, preferred_element_type=F32).astype(BF)
    for copy in waiting:
        copy.wait_send()


def middle(acts, terms, enc_one, enc_two, weights):
    dma = pltpu.SemaphoreType.DMA
    whole = pl.BlockSpec(memory_space=pltpu.VMEM)
    return pl.pallas_call(
        mid_kernel,
        out_shape=jax.ShapeDtypeStruct((C, GLANES), BF),
        in_specs=[whole] * 5,
        out_specs=whole,
        scratch_shapes=[
            pltpu.VMEM((C, 128), F32),
            pltpu.VMEM((C, 128), F32),
            pltpu.VMEM((C, 128), F32),
            pltpu.VMEM((C, 128), F32),
            pltpu.VMEM((C, 128), F32),
            pltpu.VMEM((2, 3, C, 128), BF),
            pltpu.VMEM((2, C, 256), BF),
            pltpu.VMEM((C, 256), F32),
            pltpu.VMEM((4, C, 128), BF),
            pltpu.VMEM((4, C, 128), BF),
            pltpu.VMEM((2880, 256), BF),
            pltpu.VMEM((2880, 256), BF),
            pltpu.VMEM((2880, 256), BF),
            pltpu.VMEM((5760, 256), BF),
            pltpu.VMEM((3456, 256), BF),
            pltpu.VMEM((C, 3456), BF),
            pltpu.VMEM((C, 3456), BF),
            pltpu.VMEM((C, 3456), BF),
            pltpu.VMEM((C, C), BF),
            pltpu.VMEM((C, C), BF),
            pltpu.VMEM((C, 256), F32),
            pltpu.VMEM((C, 256), F32),
            pltpu.VMEM((C, 256), BF),
            pltpu.VMEM((2, C, 128), BF),
            pltpu.VMEM((2, C, 128), BF),
            pltpu.VMEM((C, 256), F32),
            pltpu.VMEM((2, C, 128), BF),
            pltpu.VMEM((2, C, 128), BF),
            pltpu.VMEM((C, 512), F32),
            pltpu.VMEM((C, 256), F32),
            pltpu.VMEM((2, C, 128), BF),
            pltpu.VMEM((2, C, 128), BF),
            pltpu.VMEM((C, 256), F32),
            pltpu.VMEM((C, 512), F32),
            pltpu.VMEM((C, 512), F32),
            pltpu.VMEM((C, 512), F32),
            pltpu.VMEM((C, 512), BF),
            pltpu.VMEM((C, 256), BF),
            pltpu.VMEM((7, 8, 128), F32),
            pltpu.VMEM((7, 7, 8, 128), F32),
            dma((7, 7)),
            dma((7, 7)),
            dma((8, 2)),
            dma((8, 2)),
        ],
        compiler_params=pltpu.CompilerParams(
            collective_id=2, has_side_effects=True, vmem_limit_bytes=62 * 1024 * 1024
        ),
        name="middle",
    )(acts, terms, enc_one, enc_two, weights)


def flat(kernel, width):
    kernel = kernel.reshape(kernel.shape[0], -1)
    return jnp.pad(kernel, ((0, 0), (0, width - kernel.shape[1])))


def per_device(
    latent,
    hint_field,
    from_below,
    cotangent,
    timesteps,
    time_weight,
    enc_proj,
    ctl_proj,
    dec_proj,
    enc_conv_one,
    enc_conv_two,
    ctl_conv_one,
    ctl_conv_two,
    dec_conv_one,
    dec_conv_two,
    dec_shortcut,
    zero_conv,
):
    shard = jnp.concatenate(
        [
            flat(ctl_conv_one, 2944),
            flat(ctl_conv_two, 2944),
            flat(zero_conv, 384),
            flat(dec_shortcut[:, C:], 384),
            flat(dec_conv_two, 2944),
            flat(dec_conv_one, LANES - AT_DEC_ONE),
        ],
        axis=1,
    )
    weights = gather_weights(shard)
    half_width = C // 2
    frequency = jnp.exp(-math.log(10000.0) * jnp.arange(half_width, dtype=jnp.float32) / half_width)
    angles = timesteps.astype(jnp.float32)[:, None] * frequency[None, :]
    sinusoid = jnp.concatenate([jnp.cos(angles), jnp.sin(angles)], axis=1).astype(jnp.bfloat16)
    time_embed = jnp.dot(sinusoid, time_weight, preferred_element_type=jnp.float32)
    time_act = jax.nn.silu(time_embed).astype(jnp.bfloat16)
    terms = jnp.concatenate(
        [jnp.dot(time_act, proj, preferred_element_type=jnp.float32) for proj in (enc_proj, ctl_proj, dec_proj)],
        axis=0,
    ).T
    terms = jnp.pad(terms, ((0, 0), (0, 5)))
    acts = jnp.stack([a.reshape(C, 256) for a in (latent, hint_field, from_below, cotangent)])
    grads = middle(acts, terms, flat(enc_conv_one, 2880), flat(enc_conv_two, 2880), weights)
    owned = reduce_grads(grads)
    return (
        owned[:, :2880].reshape(10, 3, 3, C),
        owned[:, 2944:5824].reshape(10, 3, 3, C),
        owned[:, 5888:6208],
    )


def solution(mesh):
    in_specs = (
        P("dp", None, "rows", None),
        P("dp", None, "rows", None),
        P("dp", None, "rows", None),
        P("dp", None, "rows", None),
        P("dp"),
        P(),
        P(),
        P(),
        P(),
        P(),
        P(),
        P("dp", None, None, None),
        P("dp", None, None, None),
        P("dp", None, None, None),
        P("dp", None, None, None),
        P("dp", None),
        P("dp", None),
    )
    out_specs = (P("dp", None, None, None), P("dp", None, None, None), P("dp", None))
    return jax.shard_map(
        per_device, mesh=mesh, in_specs=in_specs, out_specs=out_specs, check_vma=False
    )
```

```python
import math

import jax
import jax.numpy as jnp
from jax import lax
from jax.experimental import pallas as pl
from jax.experimental.pallas import tpu as pltpu
from jax.sharding import PartitionSpec as P

C = 320
EPSILON = 1e-05
MESH = pl.DeviceIdType.MESH
LANES = 16384
HALF = 4096
BF = jnp.bfloat16
F32 = jnp.float32
ROWS = 16
STEPS = C // ROWS
NT = (((1,), (1,)), ((), ()))
TN = (((0,), (0,)), ((), ()))
EXACT = lax.Precision.HIGHEST
AT_CTL_ONE = 0
AT_CTL_TWO = 2944
AT_ZERO = 5888
AT_DEC_ONE = 6272
AT_SHORT = 12032
AT_DEC_TWO = 12416


def place():
    d = lax.axis_index("dp")
    r = lax.axis_index("rows")
    return (d // 8, (d // 2) % 4, d % 2, r // 4, r % 4)


def device_of(zh, y, c, zl, x):
    return (zh * 8 + y * 2 + c, zl * 4 + x)


def remote(src, dst, send, recv, where):
    return pltpu.make_async_remote_copy(
        src_ref=src, dst_ref=dst, send_sem=send, recv_sem=recv, device_id=where, device_id_type=MESH
    )


def greet(peers):
    barrier = pltpu.get_barrier_semaphore()
    for where in peers:
        pl.semaphore_signal(barrier, inc=1, device_id=where, device_id_type=MESH)
    pl.semaphore_wait(barrier, len(peers))


def lanes_at(start, size):
    return pl.ds(pl.multiple_of(start, 128), size)


def band(i):
    return pl.ds(pl.multiple_of(i * ROWS, ROWS), ROWS)


def put_columns(col, base_of, i, strips):
    lane = lax.broadcasted_iota(jnp.int32, (ROWS, 128), 1)
    shifted_of = []
    for strip in strips:
        left = jnp.where(lane == 0, 0.0, pltpu.roll(strip, 1, axis=1))
        right = jnp.where(lane == 127, 0.0, pltpu.roll(strip, 127, axis=1))
        shifted_of.append([left.astype(BF), strip.astype(BF), right.astype(BF)])
    for p in range(3):
        for q in range(3):
            start = pl.multiple_of(base_of(3 * p + q) + i * ROWS, ROWS)
            col[pl.ds(start, ROWS), 0:128] = shifted_of[p][q]
            col[pl.ds(start, ROWS), 128:256] = shifted_of[p + 1][q]


def sig(v):
    return jax.nn.sigmoid(v)


def slope(v):
    s = sig(v)
    return s * (1.0 + v * (1.0 - s))


def dot(a, b):
    return jnp.dot(a, b, preferred_element_type=F32)


def taps_dot(kernel, col):
    total = dot(kernel[0], col[0:C, :])
    for tap in range(1, 9):
        total = total + dot(kernel[tap], col[C * tap : C * tap + C, :])
    return total


def put_sums(cols, at, i, pairs):
    for k, value in enumerate(pairs):
        cols[band(i), at + k : at + k + 1] = jnp.sum(value, axis=1, keepdims=True)


def step_kernel(
    src,
    acts,
    terms,
    enc_one_hbm,
    enc_two_hbm,
    out,
    member,
    ten,
    twenty,
    cols,
    coef,
    halo,
    halo_cot,
    inner,
    inner_halo,
    edge,
    col_t,
    col_a,
    col_b,
    col_d,
    col_g,
    back_dec_two,
    back_dec_one,
    back_ctl_two,
    zero_t,
    short_t,
    enc_raw,
    ctl_raw,
    ctl_out,
    skip,
    skip_halo,
    dec_raw,
    dec_halo,
    dec_edge,
    up_grad,
    sfg,
    sfg_edge,
    sfg_halo,
    keep_n,
    keep_skip,
    keep_dec,
    mixed,
    wide,
    wide_two,
    note,
    note_in,
    note_send,
    note_recv,
    halo_send,
    halo_recv,
    enc_one,
    enc_two,
    enc_sem,
    weights,
    parts,
    column,
    gath,
    own_sem,
    ph1_send,
    ph1_recv,
    ph2_send,
    ph2_recv,
    ph3_send,
    ph3_recv,
    ph4_send,
    ph4_recv,
    ph5_send,
    ph5_recv,
    grads,
    swap,
    half,
    far,
    near,
    near_in,
    deep,
    deep_in,
    plane,
    plane_in,
    last,
    fan,
    out_sem,
    rs1_send,
    rs1_recv,
    rs2_send,
    rs2_recv,
    rs3_send,
    rs3_recv,
    rs4_send,
    rs4_recv,
    rs5_send,
    rs5_recv,
    rs6_send,
    rs6_recv,
    rs7_send,
    rs7_recv,
):
    d = lax.axis_index("dp")
    r = lax.axis_index("rows")
    zh, y, c, zl, x = place()
    slot = y * 2 + c
    peers = [(d, (r + k) % 8) for k in range(1, 8)]
    plane_peers = []
    for k in range(1, 8):
        s = (slot + k) % 8
        plane_peers.append(device_of(zh, s // 2, s % 2, zl, x))
    z_peers = [device_of((zh + k) % 4, y, c, zl, x) for k in range(1, 4)]
    x_peers = [device_of(zh, y, c, zl, (x + k) % 4) for k in range(1, 4)]
    y_peers = [device_of(zh, (y + k) % 4, c, zl, x) for k in range(1, 4)]
    partner = device_of(zh, y, 1 - c, zl, x)
    other_z = device_of(zh, y, c, 1 - zl, x)
    greet(peers + plane_peers + z_peers)
    before = (d, (r + 7) % 8)
    after = (d, (r + 1) % 8)
    waiting = []

    def send_rows(event, top, bottom, above, below):
        first = remote(top, below, halo_send.at[event, 0], halo_recv.at[event, 0], before)
        second = remote(bottom, above, halo_send.at[event, 1], halo_recv.at[event, 1], after)
        first.start()
        second.start()
        waiting.extend([first, second])
        return (first, second)

    def arrive(pair):
        pair[0].wait_recv()
        pair[1].wait_recv()

    raw = send_rows(
        0, acts.at[0:2, :, 0:128], acts.at[0:2, :, 128:256], halo.at[0, 0:2], halo.at[1, 0:2]
    )
    first = []
    for k in range(7):
        s = (slot + k + 1) % 8
        first.append(remote(src.at[s], parts.at[slot], ph1_send.at[k], ph1_recv.at[k], plane_peers[k]))
        first[-1].start()
    waiting.extend(first)
    mine = pltpu.make_async_copy(src.at[slot], parts.at[slot], own_sem.at[4])
    mine.start()
    load_one = pltpu.make_async_copy(enc_one_hbm, enc_one, enc_sem.at[0])
    load_two = pltpu.make_async_copy(enc_two_hbm, enc_two, enc_sem.at[1])
    load_one.start()
    load_two.start()

    second = {}
    third = {}
    fourth = {}
    fifth = {}
    held = {}

    def gather_z():
        mine.wait()
        for copy in first:
            copy.wait_recv()
        for s in range(8):
            column[10 * s : 10 * s + 10, :] = parts[s, 0:10, :].astype(F32)
        home = pl.multiple_of(zh * 80, 16)
        gath[pl.ds(home, 80), :] = column[...].astype(BF)
        for g in range(4):
            block = gath.at[pl.ds(home, 80), 128 * g : 128 * g + 128]
            second[g] = []
            for k in (0, 2, 1):
                second[g].append(remote(block, block, ph2_send.at[g, k], ph2_recv.at[g, k], z_peers[k]))
                second[g][-1].start()
            waiting.extend(second[g])

    def gather_x(g):
        for copy in second[g]:
            copy.wait_recv()
        block = gath.at[:, 128 * g : 128 * g + 128]
        spot = weights.at[:, lanes_at(g * 4096 + (slot * 4 + x) * 128, 128)]
        third[g] = []
        for k in (0, 2, 1):
            third[g].append(remote(block, spot, ph3_send.at[g, k], ph3_recv.at[g, k], x_peers[k]))
            third[g][-1].start()
        waiting.extend(third[g])
        held[g] = pltpu.make_async_copy(block, spot, own_sem.at[g])
        held[g].start()

    def column_of(g, steps, at, size):
        return weights.at[:, lanes_at(g * 4096 + ((y + 4 + steps) % 4 * 2 + c) * 512 + at, size)]

    def to_partner(g, k, steps):
        block = column_of(g, steps, 0, 512)
        copy = remote(block, block, ph5_send.at[g, k], ph5_recv.at[g, k], partner)
        copy.start()
        fifth[g].append(copy)
        waiting.append(copy)

    def gather_y_start(g):
        held[g].wait()
        for copy in third[g]:
            copy.wait_recv()
        block = column_of(g, 0, 0, 512)
        fourth[g] = [
            remote(block, block, ph4_send.at[g, 0], ph4_recv.at[g, 0], y_peers[0]),
            remote(block, block, ph4_send.at[g, 1], ph4_recv.at[g, 1], y_peers[2]),
        ]
        for copy in fourth[g]:
            copy.start()
        waiting.extend(fourth[g])
        fifth[g] = []
        to_partner(g, 0, 0)

    def gather_y_relay(g):
        fourth[g][0].wait_recv()
        block = column_of(g, -1, 0, 256)
        up = remote(block, block, ph4_send.at[g, 2], ph4_recv.at[g, 2], y_peers[0])
        up.start()
        fourth[g][1].wait_recv()
        block = column_of(g, 1, 256, 256)
        down = remote(block, block, ph4_send.at[g, 3], ph4_recv.at[g, 3], y_peers[2])
        down.start()
        fourth[g].extend([up, down])
        waiting.extend([up, down])
        to_partner(g, 1, -1)
        to_partner(g, 2, 1)

    def gather_y_finish(g):
        fourth[g][2].wait_recv()
        fourth[g][3].wait_recv()
        to_partner(g, 3, 2)

    def gather_done(g):
        for copy in fifth[g]:
            copy.wait_recv()


    lane = lax.broadcasted_iota(jnp.int32, (C, 128), 1)
    channel = lax.broadcasted_iota(jnp.int32, (C, 128), 0)
    in_ten = (channel >= 10 * lane) & (channel < 10 * lane + 10)
    other = lane - 32
    in_twenty = (channel >= 20 * other) & (channel < 20 * other + 20)
    ten[...] = jnp.where(in_ten, 1.0, 0.0)
    twenty[...] = jnp.where(in_twenty, 1.0, 0.0)
    member[...] = ten[...] + twenty[...]
    cols[...] = jnp.zeros((C, 128), F32)

    def share(turn):
        sums = lax.dot_general(cols[...], member[...], TN, precision=EXACT, preferred_element_type=F32)
        note[turn] = sums[0:8]
        copies = []
        for k in range(1, 8):
            copies.append(
                remote(
                    note.at[turn],
                    note_in.at[turn, k - 1],
                    note_send.at[turn, k - 1],
                    note_recv.at[turn, k - 1],
                    peers[k - 1],
                )
            )
            copies[-1].start()
        waiting.extend(copies)
        return copies

    def collect(turn, copies):
        for copy in copies:
            copy.wait_recv()
        total = note[turn]
        for k in range(7):
            total = total + note_in[turn, k]
        return total

    which = lax.broadcasted_iota(jnp.int32, (8, 128), 1)
    per_group = jnp.where(which < 32, 1.0 / (10 * 2048), 1.0 / (20 * 2048))

    def spread(table, at, rows):
        padded = jnp.concatenate(rows + [jnp.zeros((8 - len(rows), 128), F32)], axis=0)
        coef[:, at : at + 8] = lax.dot_general(
            table[...], padded, NT, precision=EXACT, preferred_element_type=F32
        )

    def norm_rows(total, k):
        mean = total[k : k + 1] * per_group[0:1]
        square = total[k + 1 : k + 2] * per_group[0:1]
        return [mean, lax.rsqrt(square - mean * mean + EPSILON)]

    def mean_rows(total, k):
        return [total[k : k + 1] * per_group[0:1], total[k + 1 : k + 2] * per_group[0:1]]

    has_up = r > 0
    has_down = r < 7

    def masked(strips):
        return [
            jnp.where(has_up, strips[0], 0.0),
            strips[1],
            strips[2],
            jnp.where(has_down, strips[3], 0.0),
        ]

    @pl.loop(0, STEPS)
    def _(i):
        latent = acts[0, band(i), :].astype(F32)
        ctl_in = (latent + acts[1, band(i), :].astype(F32)).astype(BF).astype(F32)
        under = acts[2, band(i), :].astype(F32)
        put_sums(cols, 0, i, [latent, latent * latent, ctl_in, ctl_in * ctl_in, under, under * under])

    first_note = share(0)
    gather_z()
    late = send_rows(1, acts.at[2, :, 0:128], acts.at[2, :, 128:256], halo.at[0, 2], halo.at[1, 2])
    for target in (back_dec_two, back_dec_one, back_ctl_two):
        for tap in range(9):
            target[:, 384 * tap + 320 : 384 * tap + 384] = jnp.zeros((C, 64), BF)
    for tap in range(9):
        col_g[384 * tap + 320 : 384 * tap + 384, :] = jnp.zeros((64, 256), BF)
    grads[0, :, 2816:HALF] = jnp.zeros((C, HALF - 2816), BF)
    grads[0, 160:C, :] = jnp.zeros((160, HALF), BF)
    grads[1, :, 2816:HALF] = jnp.zeros((C, HALF - 2816), BF)
    grads[1, 160:C, :] = jnp.zeros((160, HALF), BF)

    def turn(target, start, stride):
        for tap in range(9):
            block = weights[:, start + stride * tap : start + stride * tap + 320].astype(F32)
            target[:, 384 * (8 - tap) : 384 * (8 - tap) + 320] = block.T.astype(BF)

    def turn_square(target, start):
        target[...] = weights[:, start : start + 320].astype(F32).T.astype(BF)

    total = collect(0, first_note)
    spread(ten, 0, norm_rows(total, 0) + norm_rows(total, 2))
    spread(twenty, 8, norm_rows(total, 4))
    arrive(raw)

    def plain(tap):
        return 320 * tap

    def first_act(source_of, at, col, base_of):
        @pl.loop(0, STEPS)
        def _(i):
            mean = coef[band(i), at : at + 1]
            inv = coef[band(i), at + 1 : at + 2]
            strips = []
            for strip in source_of(i):
                normed = (strip - mean) * inv
                strips.append(normed * sig(normed))
            put_columns(col, base_of, i, masked(strips))

    def latent_of(i):
        own = acts[0, band(i), :].astype(F32)
        return [halo[0, 0, band(i), :].astype(F32), own[:, 0:128], own[:, 128:256], halo[1, 0, band(i), :].astype(F32)]

    def ctl_in_of(i):
        own = acts[1, band(i), :].astype(F32)
        hint = [halo[0, 1, band(i), :].astype(F32), own[:, 0:128], own[:, 128:256], halo[1, 1, band(i), :].astype(F32)]
        return [(a + b).astype(BF).astype(F32) for a, b in zip(latent_of(i), hint)]

    gather_x(0)
    first_act(latent_of, 0, col_t, plain)
    load_one.wait()
    enc_raw[...] = taps_dot(enc_one, col_t)
    edge[0] = enc_raw[:, 0:128].astype(BF)
    edge[1] = enc_raw[:, 128:256].astype(BF)
    enc_rows = send_rows(3, edge.at[0], edge.at[1], inner_halo.at[0], inner_halo.at[1])

    @pl.loop(0, STEPS)
    def _(i):
        enc = enc_raw[band(i), :] + terms[band(i), 0:1]
        put_sums(cols, 0, i, [enc, enc * enc])

    second_note = share(1)
    gather_x(1)
    first_act(ctl_in_of, 2, col_a, plain)
    gather_y_start(0)

    def under_of(i):
        own = acts[2, band(i), :].astype(F32)
        return [halo[0, 2, band(i), :].astype(F32), own[:, 0:128], own[:, 128:256], halo[1, 2, band(i), :].astype(F32)]

    def joined_low(tap):
        return 640 * tap

    def joined_high(tap):
        return 640 * tap + 320

    def spaced(tap):
        return 384 * tap

    arrive(late)
    first_act(under_of, 8, col_d, joined_low)

    total = collect(1, second_note)
    spread(ten, 16, norm_rows(total, 0))

    def second_act(raw_ref, at_halo, term_at, at, col, keep):
        @pl.loop(0, STEPS)
        def _(i):
            mean = coef[band(i), at : at + 1]
            inv = coef[band(i), at + 1 : at + 2]
            own = raw_ref[band(i), :]
            term = terms[band(i), term_at : term_at + 1]
            strips = []
            for strip in (
                inner_halo[at_halo, band(i), :].astype(F32),
                own[:, 0:128],
                own[:, 128:256],
                inner_halo[at_halo + 1, band(i), :].astype(F32),
            ):
                strips.append((strip + term - mean) * inv)
            if keep is not None:
                keep[band(i), 0:128] = strips[1]
                keep[band(i), 128:256] = strips[2]
            put_columns(col, plain, i, masked([v * sig(v) for v in strips]))

    arrive(enc_rows)
    second_act(enc_raw, 0, 0, 16, col_t, None)
    load_two.wait()
    enc_raw[...] = taps_dot(enc_two, col_t)
    gather_y_relay(0)
    gather_y_start(1)
    gather_x(2)
    gather_y_finish(0)
    gather_done(0)
    ctl_raw[...] = dot(weights[:, AT_CTL_ONE : AT_CTL_ONE + 2880], col_a[...])
    edge[2] = ctl_raw[:, 0:128].astype(BF)
    edge[3] = ctl_raw[:, 128:256].astype(BF)
    ctl_rows = send_rows(4, edge.at[2], edge.at[3], inner_halo.at[2], inner_halo.at[3])

    @pl.loop(0, STEPS)
    def _(i):
        ctl = ctl_raw[band(i), :] + terms[band(i), 1:2]
        put_sums(cols, 0, i, [ctl, ctl * ctl])

    ctl_note = share(2)
    gather_y_relay(1)
    gather_y_start(2)
    gather_x(3)
    total = collect(2, ctl_note)
    spread(ten, 64, norm_rows(total, 0))
    arrive(ctl_rows)
    second_act(ctl_raw, 2, 1, 64, col_b, keep_n)
    gather_y_finish(1)
    gather_done(1)
    inner[...] = dot(weights[:, AT_CTL_TWO : AT_CTL_TWO + 2880], col_b[...])

    @pl.loop(0, STEPS)
    def _(i):
        latent = acts[0, band(i), :].astype(F32)
        ctl_in = (latent + acts[1, band(i), :].astype(F32)).astype(BF).astype(F32)
        ctl_out[band(i), :] = (ctl_in + inner[band(i), :]).astype(BF)

    inner[...] = dot(weights[:, AT_ZERO : AT_ZERO + 320], ctl_out[...])

    @pl.loop(0, STEPS)
    def _(i):
        latent = acts[0, band(i), :].astype(F32)
        enc_out = (latent + enc_raw[band(i), :]).astype(BF).astype(F32)
        joined = (enc_out + inner[band(i), :]).astype(BF)
        skip[0, band(i), :] = joined[:, 0:128]
        skip[1, band(i), :] = joined[:, 128:256]
        value = joined.astype(F32)
        put_sums(cols, 0, i, [value, value * value])

    skip_rows = send_rows(5, skip.at[0], skip.at[1], skip_halo.at[0], skip_halo.at[1])
    third_note = share(3)
    late_cot = send_rows(2, acts.at[3], acts.at[3], halo_cot.at[0], halo_cot.at[1])
    gather_y_relay(2)
    gather_y_start(3)
    turn(back_ctl_two, AT_CTL_TWO, 320)
    turn_square(zero_t, AT_ZERO)

    total = collect(3, third_note)
    spread(twenty, 24, norm_rows(total, 0))
    arrive(skip_rows)

    @pl.loop(0, STEPS)
    def _(i):
        mean = coef[band(i), 24:25]
        inv = coef[band(i), 25:26]
        strips = []
        for k, strip in enumerate(
            (skip_halo[0, band(i), :], skip[0, band(i), :], skip[1, band(i), :], skip_halo[1, band(i), :])
        ):
            normed = (strip.astype(F32) - mean) * inv
            keep_skip[band(i), 128 * k : 128 * k + 128] = normed
            strips.append(normed * sig(normed))
        put_columns(col_d, joined_high, i, masked(strips))

    gather_y_finish(2)
    gather_done(2)
    dec_raw[...] = dot(weights[:, AT_DEC_ONE : AT_DEC_ONE + 5760], col_d[...])
    dec_edge[0] = dec_raw[:, 0:128].astype(BF)
    dec_edge[1] = dec_raw[:, 128:256].astype(BF)
    dec_rows = send_rows(6, dec_edge.at[0], dec_edge.at[1], dec_halo.at[0], dec_halo.at[1])

    @pl.loop(0, STEPS)
    def _(i):
        value = dec_raw[band(i), :] + terms[band(i), 2:3]
        put_sums(cols, 0, i, [value, value * value])

    fourth_note = share(4)
    turn(back_dec_one, AT_DEC_ONE + 320, 640)
    gather_y_relay(3)
    gather_y_finish(3)
    arrive(late_cot)
    scale = 2.0**-8

    def cot_of(i):
        far = halo_cot[0, band(i), :].astype(F32)
        own = acts[3, band(i), :].astype(F32)
        near = halo_cot[1, band(i), :].astype(F32)
        far = jnp.where(has_up, far, 0.0) * scale
        near = jnp.where(has_down, near, 0.0) * scale
        own = own * scale
        return [far[:, 0:128], far[:, 128:256], own[:, 0:128], own[:, 128:256], near[:, 0:128], near[:, 128:256]]

    gather_done(3)
    turn(back_dec_two, AT_DEC_TWO, 320)
    turn_square(short_t, AT_SHORT)
    for part in range(2):

        @pl.loop(0, STEPS)
        def _(i):
            strips = cot_of(i)[2 * part : 2 * part + 4]
            put_columns(col_g, spaced, i, strips)

        up_grad[:, 256 * part : 256 * part + 256] = dot(back_dec_two[...], col_g[...])

    @pl.loop(0, STEPS)
    def _(i):
        for k, strip in enumerate(cot_of(i)[1:5]):
            wide[band(i), 128 * k : 128 * k + 128] = strip.astype(BF)

    mixed[...] = dot(short_t[...], wide[...])

    total = collect(4, fourth_note)
    spread(ten, 32, norm_rows(total, 0))

    def keep_dec_rows(i, strip, k):
        mean = coef[band(i), 32:33]
        inv = coef[band(i), 33:34]
        term = terms[band(i), 2:3]
        normed = (strip + term - mean) * inv
        keep_dec[band(i), 128 * k : 128 * k + 128] = normed
        upstream = up_grad[band(i), 128 * k : 128 * k + 128] * slope(normed)
        up_grad[band(i), 128 * k : 128 * k + 128] = upstream
        return (normed, upstream)

    @pl.loop(0, STEPS)
    def _(i):
        one_n, one_g = keep_dec_rows(i, dec_raw[band(i), 0:128], 1)
        two_n, two_g = keep_dec_rows(i, dec_raw[band(i), 128:256], 2)
        put_sums(cols, 0, i, [one_g + two_g, one_g * one_n + two_g * two_n])

    fifth_note = share(5)
    arrive(dec_rows)

    @pl.loop(0, STEPS)
    def _(i):
        keep_dec_rows(i, dec_halo[0, band(i), :].astype(F32), 0)
        keep_dec_rows(i, dec_halo[1, band(i), :].astype(F32), 3)

    total = collect(5, fifth_note)
    spread(ten, 40, mean_rows(total, 0))

    @pl.loop(0, STEPS)
    def _(i):
        inv = coef[band(i), 33:34]
        mean = coef[band(i), 40:41]
        cross = coef[band(i), 41:42]
        strips = []
        for k in range(4):
            lanes = slice(128 * k, 128 * k + 128)
            strips.append(inv * (up_grad[band(i), lanes] - mean - keep_dec[band(i), lanes] * cross))
        put_columns(col_g, spaced, i, masked(strips))

    sfg[...] = dot(back_dec_one[...], col_g[...])
    sfg_edge[0] = sfg[:, 0:128].astype(BF)
    sfg_edge[1] = sfg[:, 128:256].astype(BF)
    sfg_rows = send_rows(7, sfg_edge.at[0], sfg_edge.at[1], sfg_halo.at[0], sfg_halo.at[1])

    @pl.loop(0, STEPS)
    def _(i):
        normed = keep_skip[band(i), 128:384]
        value = sfg[band(i), :] * slope(normed)
        up_grad[band(i), 128:384] = value
        put_sums(cols, 0, i, [value, value * normed])

    sixth_note = share(6)
    arrive(sfg_rows)

    @pl.loop(0, STEPS)
    def _(i):
        for at, lanes in ((0, slice(0, 128)), (1, slice(384, 512))):
            up_grad[band(i), lanes] = sfg_halo[at, band(i), :].astype(F32) * slope(keep_skip[band(i), lanes])

    total = collect(6, sixth_note)
    spread(twenty, 48, mean_rows(total, 0))

    @pl.loop(0, STEPS)
    def _(i):
        inv = coef[band(i), 25:26]
        mean = coef[band(i), 48:49]
        cross = coef[band(i), 49:50]
        value = inv * (up_grad[band(i), :] - mean - keep_skip[band(i), :] * cross) + mixed[band(i), :]
        wide[band(i), :] = value.astype(BF)

    up_grad[...] = dot(zero_t[...], wide[...])

    @pl.loop(0, STEPS)
    def _(i):
        strips = []
        for k in range(4):
            strips.append(up_grad[band(i), 128 * k : 128 * k + 128].astype(BF).astype(F32))
        wide_two[band(i), 0:128] = strips[1].astype(BF)
        wide_two[band(i), 128:256] = strips[2].astype(BF)
        put_columns(col_g, spaced, i, masked(strips))

    sfg[...] = dot(back_ctl_two[...], col_g[...])

    @pl.loop(0, STEPS)
    def _(i):
        normed = keep_n[band(i), :]
        value = sfg[band(i), :] * slope(normed)
        sfg[band(i), :] = value
        put_sums(cols, 0, i, [value, value * normed])

    seventh_note = share(7)

    def store_grads(k, value, at):
        count = value.shape[1]
        grads[k, 0:160, at : at + count] = value[0:160].astype(BF)
        for start in range(0, count, 128):
            tile = (at + start) // 128
            spot = (tile // 16 * 16 + tile % 4 * 4 + tile // 4 % 4) * 128
            size = min(128, count - start)
            grads[k, 160:C, spot : spot + size] = value[160:C, start : start + size].astype(BF)

    swaps = {}
    pairs = {}
    fours = {}

    def reduce_core(k):
        swaps[k] = remote(
            grads.at[k, :, lanes_at((1 - c) * 2048, 2048)], swap.at[k], rs1_send.at[k], rs1_recv.at[k], partner
        )
        swaps[k].start()
        waiting.append(swaps[k])

    def reduce_far(k):
        swaps[k].wait_recv()

        @pl.loop(0, STEPS)
        def _(i):
            total = grads[k, band(i), lanes_at(c * 2048, 2048)].astype(F32) + swap[k, band(i), :].astype(F32)
            half[k, band(i), :] = total.astype(BF)

        pairs[k] = []
        for j in (1, 3, 2):
            ya = (y + j) % 4
            xb = (x + j) % 4
            pairs[k].append(
                remote(
                    half.at[k, 0:160, lanes_at(ya * 512, 512)],
                    far.at[k, 0, j - 1],
                    rs2_send.at[k, 0, j - 1],
                    rs2_recv.at[k, 0, j - 1],
                    y_peers[j - 1],
                )
            )
            pairs[k].append(
                remote(
                    half.at[k, 160:C, lanes_at(xb * 512, 512)],
                    far.at[k, 1, j - 1],
                    rs2_send.at[k, 1, j - 1],
                    rs2_recv.at[k, 1, j - 1],
                    x_peers[j - 1],
                )
            )
        for copy in pairs[k]:
            copy.start()
        waiting.extend(pairs[k])

    def reduce_near(k):
        for copy in pairs[k]:
            copy.wait_recv()

        @pl.loop(0, STEPS // 2)
        def _(i):
            for which, where in ((0, y), (1, x)):
                rows = pl.ds(pl.multiple_of(160 * which + i * ROWS, ROWS), ROWS)
                total = half[k, rows, lanes_at(where * 512, 512)].astype(F32)
                for j in range(3):
                    total = total + far[k, which, j, band(i), :].astype(F32)
                near[k, which, band(i), :] = total.astype(BF)

        fours[k] = []
        for j in (1, 3, 2):
            xa = (x + j) % 4
            yb = (y + j) % 4
            fours[k].append(
                remote(
                    near.at[k, 0, :, lanes_at(xa * 128, 128)],
                    near_in.at[k, 0, j - 1],
                    rs3_send.at[k, 0, j - 1],
                    rs3_recv.at[k, 0, j - 1],
                    x_peers[j - 1],
                )
            )
            fours[k].append(
                remote(
                    near.at[k, 1, :, lanes_at(yb * 128, 128)],
                    near_in.at[k, 1, j - 1],
                    rs3_send.at[k, 1, j - 1],
                    rs3_recv.at[k, 1, j - 1],
                    y_peers[j - 1],
                )
            )
        for copy in fours[k]:
            copy.start()
        waiting.extend(fours[k])

    def reduce_deep(k):
        for copy in fours[k]:
            copy.wait_recv()
        for which, where in ((0, x), (1, y)):
            total = near[k, which, :, lanes_at(where * 128, 128)].astype(F32)
            for j in range(3):
                total = total + near_in[k, which, j].astype(F32)
            deep[160 * which : 160 * which + 160, 128 * k : 128 * k + 128] = total.astype(BF)

    two_value = lax.dot_general(wide_two[...], col_b[...], NT, preferred_element_type=F32)
    store_grads(0, two_value, 0)
    zero_value = lax.dot_general(wide[:, 128:384], ctl_out[...], NT, preferred_element_type=F32)
    store_grads(0, zero_value, 2944)
    reduce_core(0)
    total = collect(7, seventh_note)
    spread(ten, 56, mean_rows(total, 0))

    @pl.loop(0, STEPS)
    def _(i):
        inv = coef[band(i), 65:66]
        mean = coef[band(i), 56:57]
        cross = coef[band(i), 57:58]
        value = inv * (sfg[band(i), :] - mean - keep_n[band(i), :] * cross)
        wide_two[band(i), :] = value.astype(BF)

    reduce_far(0)
    one_value = lax.dot_general(wide_two[...], col_a[...], NT, preferred_element_type=F32)
    store_grads(1, one_value, 0)
    reduce_core(1)
    reduce_far(1)
    reduce_near(0)
    reduce_near(1)
    reduce_deep(0)
    reduce_deep(1)
    ring = []
    for k in (0, 2, 1):
        zt = (zh + k + 1) % 4
        ring.append(
            remote(
                deep.at[pl.ds(pl.multiple_of(zt * 80, 16), 80)],
                deep_in.at[k],
                rs4_send.at[k],
                rs4_recv.at[k],
                z_peers[k],
            )
        )
        ring[-1].start()
    for copy in ring:
        copy.wait_recv()
    total = deep[pl.ds(pl.multiple_of(zh * 80, 16), 80), :].astype(F32)
    for k in range(3):
        total = total + deep_in[k].astype(F32)
    plane[...] = total
    cross = remote(plane, plane_in, rs5_send.at[0], rs5_recv.at[0], other_z)
    cross.start()
    cross.wait_recv()
    last[...] = plane[...] + plane_in[...]
    for s in range(8):
        fan[s, 0:10, :] = last[10 * s : 10 * s + 10, :]
        fan[s, 10:16, :] = jnp.zeros((6, 256), F32)
    sixth = []
    for k in range(7):
        s = (slot + k + 1) % 8
        sixth.append(remote(fan.at[s], out.at[x, slot], rs6_send.at[k], rs6_recv.at[k], plane_peers[k]))
        sixth[-1].start()
    mine = pltpu.make_async_copy(fan.at[slot], out.at[x, slot], out_sem.at[0])
    mine.start()
    mine.wait()
    for copy in sixth:
        copy.wait_recv()
    seventh = []
    for k in range(3):
        seventh.append(remote(out.at[x], out.at[x], rs7_send.at[k], rs7_recv.at[k], x_peers[k]))
        seventh[-1].start()
    for copy in seventh:
        copy.wait_recv()
    for copy in waiting + ring + [cross] + sixth + seventh:
        copy.wait_send()


def run_step(shard, acts, terms, enc_one, enc_two):
    x = lax.axis_index("rows") % 4
    pieces = shard.reshape(10, 4, 4, 2, 4, 128)
    pieces = lax.dynamic_index_in_dim(pieces, x, 4, keepdims=False)
    pieces = jnp.transpose(pieces, (2, 3, 0, 1, 4)).reshape(8, 10, 512)
    pieces = jnp.pad(pieces, ((0, 0), (0, 6), (0, 0)))
    dma = pltpu.SemaphoreType.DMA
    whole = pl.BlockSpec(memory_space=pltpu.VMEM)
    far_off = pl.BlockSpec(memory_space=pl.ANY)
    return pl.pallas_call(
        step_kernel,
        out_shape=jax.ShapeDtypeStruct((4, 8, 16, 256), F32),
        in_specs=[whole, whole, whole, far_off, far_off],
        out_specs=whole,
        scratch_shapes=[
            pltpu.VMEM((C, 128), F32),
            pltpu.VMEM((C, 128), F32),
            pltpu.VMEM((C, 128), F32),
            pltpu.VMEM((C, 128), F32),
            pltpu.VMEM((C, 128), F32),
            pltpu.VMEM((2, 3, C, 128), BF),
            pltpu.VMEM((2, C, 256), BF),
            pltpu.VMEM((C, 256), F32),
            pltpu.VMEM((4, C, 128), BF),
            pltpu.VMEM((4, C, 128), BF),
            pltpu.VMEM((2880, 256), BF),
            pltpu.VMEM((2880, 256), BF),
            pltpu.VMEM((2880, 256), BF),
            pltpu.VMEM((5760, 256), BF),
            pltpu.VMEM((3456, 256), BF),
            pltpu.VMEM((C, 3456), BF),
            pltpu.VMEM((C, 3456), BF),
            pltpu.VMEM((C, 3456), BF),
            pltpu.VMEM((C, C), BF),
            pltpu.VMEM((C, C), BF),
            pltpu.VMEM((C, 256), F32),
            pltpu.VMEM((C, 256), F32),
            pltpu.VMEM((C, 256), BF),
            pltpu.VMEM((2, C, 128), BF),
            pltpu.VMEM((2, C, 128), BF),
            pltpu.VMEM((C, 256), F32),
            pltpu.VMEM((2, C, 128), BF),
            pltpu.VMEM((2, C, 128), BF),
            pltpu.VMEM((C, 512), F32),
            pltpu.VMEM((C, 256), F32),
            pltpu.VMEM((2, C, 128), BF),
            pltpu.VMEM((2, C, 128), BF),
            pltpu.VMEM((C, 256), F32),
            pltpu.VMEM((C, 512), F32),
            pltpu.VMEM((C, 512), F32),
            pltpu.VMEM((C, 512), F32),
            pltpu.VMEM((C, 512), BF),
            pltpu.VMEM((C, 256), BF),
            pltpu.VMEM((8, 8, 128), F32),
            pltpu.VMEM((8, 7, 8, 128), F32),
            dma((8, 7)),
            dma((8, 7)),
            dma((8, 2)),
            dma((8, 2)),
            pltpu.VMEM((9, C, C), BF),
            pltpu.VMEM((9, C, C), BF),
            dma((2,)),
            pltpu.VMEM((C, LANES), BF),
            pltpu.VMEM((8, 16, 512), BF),
            pltpu.VMEM((80, 512), F32),
            pltpu.VMEM((C, 512), BF),
            dma((5,)),
            dma((7,)),
            dma((7,)),
            dma((4, 3)),
            dma((4, 3)),
            dma((4, 3)),
            dma((4, 3)),
            dma((4, 4)),
            dma((4, 4)),
            dma((4, 4)),
            dma((4, 4)),
            pltpu.VMEM((2, C, HALF), BF),
            pltpu.VMEM((2, C, 2048), BF),
            pltpu.VMEM((2, C, 2048), BF),
            pltpu.VMEM((2, 2, 3, 160, 512), BF),
            pltpu.VMEM((2, 2, 160, 512), BF),
            pltpu.VMEM((2, 2, 3, 160, 128), BF),
            pltpu.VMEM((C, 256), BF),
            pltpu.VMEM((3, 80, 256), BF),
            pltpu.VMEM((80, 256), F32),
            pltpu.VMEM((80, 256), F32),
            pltpu.VMEM((80, 256), F32),
            pltpu.VMEM((8, 16, 256), F32),
            dma((1,)),
            dma((2,)),
            dma((2,)),
            dma((2, 2, 3)),
            dma((2, 2, 3)),
            dma((2, 2, 3)),
            dma((2, 2, 3)),
            dma((3,)),
            dma((3,)),
            dma((1,)),
            dma((1,)),
            dma((7,)),
            dma((7,)),
            dma((3,)),
            dma((3,)),
        ],
        compiler_params=pltpu.CompilerParams(
            collective_id=0, has_side_effects=True, vmem_limit_bytes=63 * 1024 * 1024
        ),
        name="train_step",
    )(pieces, acts, terms, enc_one, enc_two)


def flat(kernel, width):
    kernel = kernel.reshape(kernel.shape[0], -1)
    return jnp.pad(kernel, ((0, 0), (0, width - kernel.shape[1])))


def per_device(
    latent,
    hint_field,
    from_below,
    cotangent,
    timesteps,
    time_weight,
    enc_proj,
    ctl_proj,
    dec_proj,
    enc_conv_one,
    enc_conv_two,
    ctl_conv_one,
    ctl_conv_two,
    dec_conv_one,
    dec_conv_two,
    dec_shortcut,
    zero_conv,
):
    shard = jnp.concatenate(
        [
            flat(ctl_conv_one, 2944),
            flat(ctl_conv_two, 2944),
            flat(zero_conv, 384),
            flat(dec_conv_one, 5760),
            flat(dec_shortcut[:, C:], 384),
            flat(dec_conv_two, LANES - AT_DEC_TWO),
        ],
        axis=1,
    )
    half_width = C // 2
    frequency = jnp.exp(-math.log(10000.0) * jnp.arange(half_width, dtype=jnp.float32) / half_width)
    angles = timesteps.astype(jnp.float32)[:, None] * frequency[None, :]
    sinusoid = jnp.concatenate([jnp.cos(angles), jnp.sin(angles)], axis=1).astype(jnp.bfloat16)
    time_embed = jnp.dot(sinusoid, time_weight, preferred_element_type=jnp.float32)
    time_act = jax.nn.silu(time_embed).astype(jnp.bfloat16)
    terms = jnp.concatenate(
        [jnp.dot(time_act, proj, preferred_element_type=jnp.float32) for proj in (enc_proj, ctl_proj, dec_proj)],
        axis=0,
    ).T
    terms = jnp.pad(terms, ((0, 0), (0, 5)))
    acts = jnp.stack([a.reshape(C, 256) for a in (latent, hint_field, from_below, cotangent)])
    enc_one = jnp.transpose(enc_conv_one, (1, 2, 0, 3)).reshape(9, C, C)
    enc_two = jnp.transpose(enc_conv_two, (1, 2, 0, 3)).reshape(9, C, C)
    pieces = run_step(shard, acts, terms, enc_one, enc_two)
    pieces = pieces[:, :, :10, :].reshape(4, 4, 2, 10, 2, 128)
    owned = jnp.transpose(pieces, (3, 4, 2, 1, 0, 5)).reshape(10, 2, HALF)
    return (
        owned[:, 1, :2880].reshape(10, 3, 3, C),
        owned[:, 0, :2880].reshape(10, 3, 3, C),
        owned[:, 0, 2944:3264],
    )


def solution(mesh):
    in_specs = (
        P("dp", None, "rows", None),
        P("dp", None, "rows", None),
        P("dp", None, "rows", None),
        P("dp", None, "rows", None),
        P("dp"),
        P(),
        P(),
        P(),
        P(),
        P(),
        P(),
        P("dp", None, None, None),
        P("dp", None, None, None),
        P("dp", None, None, None),
        P("dp", None, None, None),
        P("dp", None),
        P("dp", None),
    )
    out_specs = (P("dp", None, None, None), P("dp", None, None, None), P("dp", None))
    return jax.shard_map(
        per_device, mesh=mesh, in_specs=in_specs, out_specs=out_specs, check_vma=False
    )
```

```python
import math

import jax
import jax.numpy as jnp
from jax import lax
from jax.experimental import pallas as pl
from jax.experimental.pallas import tpu as pltpu
from jax.sharding import PartitionSpec as P

C = 320
EPSILON = 1e-05
MESH = pl.DeviceIdType.MESH
LANES = 16384
HALF = 4096
BF = jnp.bfloat16
F32 = jnp.float32
ROWS = 16
STEPS = C // ROWS
NT = (((1,), (1,)), ((), ()))
TN = (((0,), (0,)), ((), ()))
EXACT = lax.Precision.HIGHEST
AT_CTL_ONE = 0
AT_CTL_TWO = 2944
AT_ZERO = 5888
AT_DEC_ONE = 6272
AT_SHORT = 12032
AT_DEC_TWO = 12416


def place():
    d = lax.axis_index("dp")
    r = lax.axis_index("rows")
    return (d // 8, (d // 2) % 4, d % 2, r // 4, r % 4)


def device_of(zh, y, c, zl, x):
    return (zh * 8 + y * 2 + c, zl * 4 + x)


def remote(src, dst, send, recv, where):
    return pltpu.make_async_remote_copy(
        src_ref=src, dst_ref=dst, send_sem=send, recv_sem=recv, device_id=where, device_id_type=MESH
    )


def greet(peers):
    barrier = pltpu.get_barrier_semaphore()
    for where in peers:
        pl.semaphore_signal(barrier, inc=1, device_id=where, device_id_type=MESH)
    pl.semaphore_wait(barrier, len(peers))


def lanes_at(start, size):
    return pl.ds(pl.multiple_of(start, 128), size)


def band(i):
    return slice(i * ROWS, i * ROWS + ROWS)


def each(count):
    def run(body):
        for i in range(count):
            body(i)

    return run


def put_columns(col, base_of, i, strips):
    lane = lax.broadcasted_iota(jnp.int32, (ROWS, 128), 1)
    shifted_of = []
    for strip in strips:
        left = jnp.where(lane == 0, 0.0, pltpu.roll(strip, 1, axis=1))
        right = jnp.where(lane == 127, 0.0, pltpu.roll(strip, 127, axis=1))
        shifted_of.append([left.astype(BF), strip.astype(BF), right.astype(BF)])
    for p in range(3):
        for q in range(3):
            start = base_of(3 * p + q) + i * ROWS
            col[start : start + ROWS, 0:128] = shifted_of[p][q]
            col[start : start + ROWS, 128:256] = shifted_of[p + 1][q]


def sig(v):
    return jax.nn.sigmoid(v)


def slope(v):
    s = sig(v)
    return s * (1.0 + v * (1.0 - s))


def dot(a, b):
    return jnp.dot(a, b, preferred_element_type=F32)


def taps_dot(kernel, col):
    total = dot(kernel[0], col[0:C, :])
    for tap in range(1, 9):
        total = total + dot(kernel[tap], col[C * tap : C * tap + C, :])
    return total


def put_sums(cols, at, i, pairs):
    for k, value in enumerate(pairs):
        cols[band(i), at + k : at + k + 1] = jnp.sum(value, axis=1, keepdims=True)


def step_kernel(
    sinus,
    latent_ref,
    hint_ref,
    under_ref,
    cot_ref,
    shard_ctl_one,
    shard_ctl_two,
    shard_dec_one,
    shard_dec_two,
    shard_short,
    shard_zero,
    time_weight_hbm,
    enc_proj_hbm,
    ctl_proj_hbm,
    dec_proj_hbm,
    enc_one_hbm,
    enc_two_hbm,
    one_out,
    two_out,
    zero_out,
    member,
    ten,
    twenty,
    cols,
    coef,
    halo,
    halo_cot,
    inner,
    inner_halo,
    edge,
    col_t,
    col_a,
    col_b,
    col_d,
    col_g,
    back_dec_two,
    back_dec_one,
    back_ctl_two,
    zero_t,
    short_t,
    enc_raw,
    ctl_raw,
    ctl_out,
    skip,
    skip_halo,
    dec_raw,
    dec_halo,
    dec_edge,
    up_grad,
    sfg,
    sfg_edge,
    sfg_halo,
    keep_n,
    keep_skip,
    keep_dec,
    mixed,
    wide,
    wide_two,
    note,
    note_in,
    note_send,
    note_recv,
    halo_send,
    halo_recv,
    terms,
    time_weight,
    projections,
    stage,
    src,
    enc_one,
    enc_two,
    enc_sem,
    weights,
    parts,
    column,
    gath,
    own_sem,
    ph1_send,
    ph1_recv,
    ph2_send,
    ph2_recv,
    ph3_send,
    ph3_recv,
    ph4_send,
    ph4_recv,
    ph5_send,
    ph5_recv,
    grads,
    swap,
    half,
    far,
    near,
    passing,
    near_in,
    deep,
    deep_in,
    last,
    fan,
    pool,
    out_sem,
    rs1_send,
    rs1_recv,
    rs2_send,
    rs2_recv,
    rs3_send,
    rs3_recv,
    rs4_send,
    rs4_recv,
    rs6_send,
    rs6_recv,
    rs7_send,
    rs7_recv,
):
    d = lax.axis_index("dp")
    r = lax.axis_index("rows")
    zh, y, c, zl, x = place()
    slot = y * 2 + c
    peers = [(d, (r + k) % 8) for k in range(1, 8)]
    plane_peers = []
    for k in range(1, 8):
        s = (slot + k) % 8
        plane_peers.append(device_of(zh, s // 2, s % 2, zl, x))
    z_peers = [device_of((zh + k) % 4, y, c, zl, x) for k in range(1, 4)]
    x_peers = [device_of(zh, y, c, zl, (x + k) % 4) for k in range(1, 4)]
    y_peers = [device_of(zh, (y + k) % 4, c, zl, x) for k in range(1, 4)]
    partner = device_of(zh, y, 1 - c, zl, x)
    other_z = device_of(zh, y, c, 1 - zl, x)
    z_all = [device_of((zh + k // 2) % 4, y, c, (zl + k) % 2, x) for k in range(1, 8)]
    everyone = peers + plane_peers + z_all[1:]
    barrier = pltpu.get_barrier_semaphore()
    for where in everyone:
        pl.semaphore_signal(barrier, inc=1, device_id=where, device_id_type=MESH)
    loads = []
    for k, (source, target) in enumerate(
        (
            (time_weight_hbm, time_weight),
            (enc_proj_hbm, projections.at[0]),
            (ctl_proj_hbm, projections.at[1]),
            (dec_proj_hbm, projections.at[2]),
            (enc_one_hbm, enc_one),
            (enc_two_hbm, enc_two),
        )
    ):
        loads.append(pltpu.make_async_copy(source, target, enc_sem.at[k]))
        loads[-1].start()
    load_one, load_two = loads[4:]

    stage[...] = jnp.zeros((16, LANES), BF)
    for kernel, start, count, width in (
        (shard_ctl_one, AT_CTL_ONE, 9, C),
        (shard_ctl_two, AT_CTL_TWO, 9, C),
        (shard_dec_one, AT_DEC_ONE, 9, 2 * C),
        (shard_dec_two, AT_DEC_TWO, 9, C),
    ):
        for tap in range(count):
            stage[0:10, start + width * tap : start + width * tap + width] = kernel[tap]
    stage[0:10, AT_ZERO : AT_ZERO + C] = shard_zero[...]
    stage[0:10, AT_SHORT : AT_SHORT + C] = shard_short[:, C : 2 * C]
    for s in range(8):
        for g in range(4):
            src[s, :, 128 * g : 128 * g + 128] = stage[:, lanes_at(g * 4096 + (s * 4 + x) * 128, 128)]

    lane = lax.broadcasted_iota(jnp.int32, (C, 128), 1)
    channel = lax.broadcasted_iota(jnp.int32, (C, 128), 0)
    in_ten = (channel >= 10 * lane) & (channel < 10 * lane + 10)
    other = lane - 32
    in_twenty = (channel >= 20 * other) & (channel < 20 * other + 20)
    ten[...] = jnp.where(in_ten, 1.0, 0.0)
    twenty[...] = jnp.where(in_twenty, 1.0, 0.0)
    member[...] = ten[...] + twenty[...]
    cols[...] = jnp.zeros((C, 128), F32)

    @each(STEPS)
    def _(i):
        sums = [0.0] * 6
        for h in range(2):
            latent = latent_ref[h, band(i), :].astype(F32)
            ctl_in = (latent + hint_ref[h, band(i), :].astype(F32)).astype(BF).astype(F32)
            under = under_ref[h, band(i), :].astype(F32)
            for k, value in enumerate((latent, latent * latent, ctl_in, ctl_in * ctl_in, under, under * under)):
                sums[k] = sums[k] + value
        put_sums(cols, 0, i, sums)

    pl.semaphore_wait(barrier, len(everyone))
    before = (d, (r + 7) % 8)
    after = (d, (r + 1) % 8)
    waiting = []

    def send_rows(event, top, bottom, above, below):
        first = remote(top, below, halo_send.at[event, 0], halo_recv.at[event, 0], before)
        second = remote(bottom, above, halo_send.at[event, 1], halo_recv.at[event, 1], after)
        first.start()
        second.start()
        waiting.extend([first, second])
        return (first, second)

    def arrive(pair):
        pair[0].wait_recv()
        pair[1].wait_recv()

    raw = send_rows(0, latent_ref.at[0], latent_ref.at[1], halo.at[0, 0], halo.at[1, 0])
    raw_hint = send_rows(8, hint_ref.at[0], hint_ref.at[1], halo.at[0, 1], halo.at[1, 1])
    first = []
    for k in range(7):
        s = (slot + k + 1) % 8
        first.append(remote(src.at[s], parts.at[slot], ph1_send.at[k], ph1_recv.at[k], plane_peers[k]))
        first[-1].start()
    waiting.extend(first)
    mine = pltpu.make_async_copy(src.at[slot], parts.at[slot], own_sem.at[4])
    mine.start()

    second = {}
    third = {}
    fourth = {}
    fifth = {}
    held = {}

    def gather_z():
        mine.wait()
        for copy in first:
            copy.wait_recv()
        for s in range(8):
            column[10 * s : 10 * s + 10, :] = parts[s, 0:10, :].astype(F32)
        home = pl.multiple_of(zh * 80, 16)
        gath[pl.ds(home, 80), :] = column[...].astype(BF)
        for g in range(4):
            block = gath.at[pl.ds(home, 80), 128 * g : 128 * g + 128]
            second[g] = []
            for k in (0, 2, 1):
                second[g].append(remote(block, block, ph2_send.at[g, k], ph2_recv.at[g, k], z_peers[k]))
                second[g][-1].start()
            waiting.extend(second[g])

    def gather_x(g):
        for copy in second[g]:
            copy.wait_recv()
        block = gath.at[:, 128 * g : 128 * g + 128]
        spot = weights.at[:, lanes_at(g * 4096 + (slot * 4 + x) * 128, 128)]
        third[g] = []
        for k in (0, 2, 1):
            third[g].append(remote(block, spot, ph3_send.at[g, k], ph3_recv.at[g, k], x_peers[k]))
            third[g][-1].start()
        waiting.extend(third[g])
        held[g] = pltpu.make_async_copy(block, spot, own_sem.at[g])
        held[g].start()

    def column_of(g, steps, at, size):
        return weights.at[:, lanes_at(g * 4096 + ((y + 4 + steps) % 4 * 2 + c) * 512 + at, size)]

    def to_partner(g, k, steps):
        block = column_of(g, steps, 0, 512)
        copy = remote(block, block, ph5_send.at[g, k], ph5_recv.at[g, k], partner)
        copy.start()
        fifth[g].append(copy)
        waiting.append(copy)

    def gather_y_start(g):
        held[g].wait()
        for copy in third[g]:
            copy.wait_recv()
        block = column_of(g, 0, 0, 512)
        fourth[g] = [
            remote(block, block, ph4_send.at[g, 0], ph4_recv.at[g, 0], y_peers[0]),
            remote(block, block, ph4_send.at[g, 1], ph4_recv.at[g, 1], y_peers[2]),
        ]
        for copy in fourth[g]:
            copy.start()
        waiting.extend(fourth[g])
        fifth[g] = []
        to_partner(g, 0, 0)

    def gather_y_relay(g):
        fourth[g][0].wait_recv()
        block = column_of(g, -1, 0, 256)
        up = remote(block, block, ph4_send.at[g, 2], ph4_recv.at[g, 2], y_peers[0])
        up.start()
        fourth[g][1].wait_recv()
        block = column_of(g, 1, 256, 256)
        down = remote(block, block, ph4_send.at[g, 3], ph4_recv.at[g, 3], y_peers[2])
        down.start()
        fourth[g].extend([up, down])
        waiting.extend([up, down])
        to_partner(g, 1, -1)
        to_partner(g, 2, 1)

    def gather_y_finish(g):
        fourth[g][2].wait_recv()
        fourth[g][3].wait_recv()
        to_partner(g, 3, 2)

    def gather_done(g):
        for copy in fifth[g]:
            copy.wait_recv()


    def share(turn):
        sums = lax.dot_general(cols[...], member[...], TN, precision=EXACT, preferred_element_type=F32)
        note[turn] = sums[0:8]
        copies = []
        for k in range(1, 8):
            copies.append(
                remote(
                    note.at[turn],
                    note_in.at[turn, k - 1],
                    note_send.at[turn, k - 1],
                    note_recv.at[turn, k - 1],
                    peers[k - 1],
                )
            )
            copies[-1].start()
        waiting.extend(copies)
        return copies

    def collect(turn, copies):
        for copy in copies:
            copy.wait_recv()
        total = note[turn]
        for k in range(7):
            total = total + note_in[turn, k]
        return total

    which = lax.broadcasted_iota(jnp.int32, (8, 128), 1)
    per_group = jnp.where(which < 32, 1.0 / (10 * 2048), 1.0 / (20 * 2048))

    def spread(table, at, rows):
        padded = jnp.concatenate(rows + [jnp.zeros((8 - len(rows), 128), F32)], axis=0)
        coef[:, at : at + 8] = lax.dot_general(
            table[...], padded, NT, precision=EXACT, preferred_element_type=F32
        )

    def norm_rows(total, k):
        mean = total[k : k + 1] * per_group[0:1]
        square = total[k + 1 : k + 2] * per_group[0:1]
        return [mean, lax.rsqrt(square - mean * mean + EPSILON)]

    def mean_rows(total, k):
        return [total[k : k + 1] * per_group[0:1], total[k + 1 : k + 2] * per_group[0:1]]

    has_up = r > 0
    has_down = r < 7

    def masked(strips):
        return [
            jnp.where(has_up, strips[0], 0.0),
            strips[1],
            strips[2],
            jnp.where(has_down, strips[3], 0.0),
        ]

    first_note = share(0)
    gather_z()
    late = send_rows(1, under_ref.at[0], under_ref.at[1], halo.at[0, 2], halo.at[1, 2])
    for load in loads[0:4]:
        load.wait()
    embed = dot(sinus[...], time_weight[...])
    embed = (embed * sig(embed)).astype(BF)
    for k in range(3):
        term = lax.dot_general(projections[k], embed, NT, preferred_element_type=F32)
        terms[:, k : k + 1] = term[:, 0:1]
    for target in (back_dec_two, back_dec_one, back_ctl_two):
        for tap in range(9):
            target[:, 384 * tap + 320 : 384 * tap + 384] = jnp.zeros((C, 64), BF)
    for tap in range(9):
        col_g[384 * tap + 320 : 384 * tap + 384, :] = jnp.zeros((64, 256), BF)
    grads[0, :, 2816:HALF] = jnp.zeros((C, HALF - 2816), BF)
    grads[0, 160:C, :] = jnp.zeros((160, HALF), BF)
    grads[1, :, 2816:HALF] = jnp.zeros((C, HALF - 2816), BF)
    grads[1, 160:C, :] = jnp.zeros((160, HALF), BF)

    def turn(target, start, stride):
        for tap in range(9):
            block = weights[:, start + stride * tap : start + stride * tap + 320].astype(F32)
            target[:, 384 * (8 - tap) : 384 * (8 - tap) + 320] = block.T.astype(BF)

    def turn_square(target, start):
        target[...] = weights[:, start : start + 320].astype(F32).T.astype(BF)

    total = collect(0, first_note)
    spread(ten, 0, norm_rows(total, 0) + norm_rows(total, 2))
    spread(twenty, 8, norm_rows(total, 4))
    arrive(raw)
    arrive(raw_hint)

    def plain(tap):
        return 320 * tap

    def first_act(source_of, at, col, base_of):
        @each(STEPS)
        def _(i):
            mean = coef[band(i), at : at + 1]
            inv = coef[band(i), at + 1 : at + 2]
            strips = []
            for strip in source_of(i):
                normed = (strip - mean) * inv
                strips.append(normed * sig(normed))
            put_columns(col, base_of, i, masked(strips))

    def latent_of(i):
        return [
            halo[0, 0, band(i), :].astype(F32),
            latent_ref[0, band(i), :].astype(F32),
            latent_ref[1, band(i), :].astype(F32),
            halo[1, 0, band(i), :].astype(F32),
        ]

    def ctl_in_of(i):
        hint = [
            halo[0, 1, band(i), :].astype(F32),
            hint_ref[0, band(i), :].astype(F32),
            hint_ref[1, band(i), :].astype(F32),
            halo[1, 1, band(i), :].astype(F32),
        ]
        return [(a + b).astype(BF).astype(F32) for a, b in zip(latent_of(i), hint)]

    gather_x(0)
    first_act(latent_of, 0, col_t, plain)
    load_one.wait()
    enc_raw[...] = taps_dot(enc_one, col_t)
    edge[0] = enc_raw[:, 0:128].astype(BF)
    edge[1] = enc_raw[:, 128:256].astype(BF)
    enc_rows = send_rows(3, edge.at[0], edge.at[1], inner_halo.at[0], inner_halo.at[1])

    @each(STEPS)
    def _(i):
        enc = enc_raw[band(i), :] + terms[band(i), 0:1]
        put_sums(cols, 0, i, [enc, enc * enc])

    second_note = share(1)
    gather_x(1)
    first_act(ctl_in_of, 2, col_a, plain)
    gather_y_start(0)

    def under_of(i):
        return [
            halo[0, 2, band(i), :].astype(F32),
            under_ref[0, band(i), :].astype(F32),
            under_ref[1, band(i), :].astype(F32),
            halo[1, 2, band(i), :].astype(F32),
        ]

    def joined_low(tap):
        return 640 * tap

    def joined_high(tap):
        return 640 * tap + 320

    def spaced(tap):
        return 384 * tap

    arrive(late)
    first_act(under_of, 8, col_d, joined_low)

    total = collect(1, second_note)
    spread(ten, 16, norm_rows(total, 0))

    def second_act(raw_ref, at_halo, term_at, at, col, keep):
        @each(STEPS)
        def _(i):
            mean = coef[band(i), at : at + 1]
            inv = coef[band(i), at + 1 : at + 2]
            own = raw_ref[band(i), :]
            term = terms[band(i), term_at : term_at + 1]
            strips = []
            for strip in (
                inner_halo[at_halo, band(i), :].astype(F32),
                own[:, 0:128],
                own[:, 128:256],
                inner_halo[at_halo + 1, band(i), :].astype(F32),
            ):
                strips.append((strip + term - mean) * inv)
            if keep is not None:
                keep[band(i), 0:128] = strips[1]
                keep[band(i), 128:256] = strips[2]
            put_columns(col, plain, i, masked([v * sig(v) for v in strips]))

    arrive(enc_rows)
    second_act(enc_raw, 0, 0, 16, col_t, None)
    load_two.wait()
    enc_raw[...] = taps_dot(enc_two, col_t)
    gather_y_relay(0)
    gather_y_start(1)
    gather_x(2)
    gather_y_finish(0)
    gather_done(0)
    ctl_raw[...] = dot(weights[:, AT_CTL_ONE : AT_CTL_ONE + 2880], col_a[...])
    edge[2] = ctl_raw[:, 0:128].astype(BF)
    edge[3] = ctl_raw[:, 128:256].astype(BF)
    ctl_rows = send_rows(4, edge.at[2], edge.at[3], inner_halo.at[2], inner_halo.at[3])

    @each(STEPS)
    def _(i):
        ctl = ctl_raw[band(i), :] + terms[band(i), 1:2]
        put_sums(cols, 0, i, [ctl, ctl * ctl])

    ctl_note = share(2)
    gather_y_relay(1)
    gather_y_start(2)
    gather_x(3)
    total = collect(2, ctl_note)
    spread(ten, 64, norm_rows(total, 0))
    arrive(ctl_rows)
    second_act(ctl_raw, 2, 1, 64, col_b, keep_n)
    gather_y_finish(1)
    gather_done(1)
    inner[...] = dot(weights[:, AT_CTL_TWO : AT_CTL_TWO + 2880], col_b[...])

    @each(STEPS)
    def _(i):
        own = ctl_in_of(i)
        ctl_out[band(i), 0:128] = (own[1] + inner[band(i), 0:128]).astype(BF)
        ctl_out[band(i), 128:256] = (own[2] + inner[band(i), 128:256]).astype(BF)

    inner[...] = dot(weights[:, AT_ZERO : AT_ZERO + 320], ctl_out[...])

    @each(STEPS)
    def _(i):
        sums = [0.0, 0.0]
        for h in range(2):
            lanes = slice(128 * h, 128 * h + 128)
            latent = latent_ref[h, band(i), :].astype(F32)
            enc_out = (latent + enc_raw[band(i), lanes]).astype(BF).astype(F32)
            joined = (enc_out + inner[band(i), lanes]).astype(BF)
            skip[h, band(i), :] = joined
            value = joined.astype(F32)
            sums = [sums[0] + value, sums[1] + value * value]
        put_sums(cols, 0, i, sums)

    skip_rows = send_rows(5, skip.at[0], skip.at[1], skip_halo.at[0], skip_halo.at[1])
    third_note = share(3)
    late_cot = send_rows(2, cot_ref, cot_ref, halo_cot.at[0], halo_cot.at[1])
    gather_y_relay(2)
    gather_y_start(3)
    turn(back_ctl_two, AT_CTL_TWO, 320)
    turn_square(zero_t, AT_ZERO)

    total = collect(3, third_note)
    spread(twenty, 24, norm_rows(total, 0))
    arrive(skip_rows)

    @each(STEPS)
    def _(i):
        mean = coef[band(i), 24:25]
        inv = coef[band(i), 25:26]
        strips = []
        for k, strip in enumerate(
            (skip_halo[0, band(i), :], skip[0, band(i), :], skip[1, band(i), :], skip_halo[1, band(i), :])
        ):
            normed = (strip.astype(F32) - mean) * inv
            keep_skip[band(i), 128 * k : 128 * k + 128] = normed
            strips.append(normed * sig(normed))
        put_columns(col_d, joined_high, i, masked(strips))

    gather_y_finish(2)
    gather_done(2)
    dec_raw[...] = dot(weights[:, AT_DEC_ONE : AT_DEC_ONE + 5760], col_d[...])
    dec_edge[0] = dec_raw[:, 0:128].astype(BF)
    dec_edge[1] = dec_raw[:, 128:256].astype(BF)
    dec_rows = send_rows(6, dec_edge.at[0], dec_edge.at[1], dec_halo.at[0], dec_halo.at[1])

    @each(STEPS)
    def _(i):
        value = dec_raw[band(i), :] + terms[band(i), 2:3]
        put_sums(cols, 0, i, [value, value * value])

    fourth_note = share(4)
    turn(back_dec_one, AT_DEC_ONE + 320, 640)
    gather_y_relay(3)
    gather_y_finish(3)
    arrive(late_cot)
    scale = 2.0**-8

    def cot_of(i):
        far_rows = [jnp.where(has_up, halo_cot[0, h, band(i), :].astype(F32), 0.0) for h in range(2)]
        own = [cot_ref[h, band(i), :].astype(F32) for h in range(2)]
        near_rows = [jnp.where(has_down, halo_cot[1, h, band(i), :].astype(F32), 0.0) for h in range(2)]
        return [strip * scale for strip in far_rows + own + near_rows]

    gather_done(3)
    turn(back_dec_two, AT_DEC_TWO, 320)
    turn_square(short_t, AT_SHORT)
    for part in range(2):

        @each(STEPS)
        def _(i):
            strips = cot_of(i)[2 * part : 2 * part + 4]
            put_columns(col_g, spaced, i, strips)

        up_grad[:, 256 * part : 256 * part + 256] = dot(back_dec_two[...], col_g[...])

    @each(STEPS)
    def _(i):
        for k, strip in enumerate(cot_of(i)[1:5]):
            wide[band(i), 128 * k : 128 * k + 128] = strip.astype(BF)

    mixed[...] = dot(short_t[...], wide[...])

    total = collect(4, fourth_note)
    spread(ten, 32, norm_rows(total, 0))

    def keep_dec_rows(i, strip, k):
        mean = coef[band(i), 32:33]
        inv = coef[band(i), 33:34]
        term = terms[band(i), 2:3]
        normed = (strip + term - mean) * inv
        keep_dec[band(i), 128 * k : 128 * k + 128] = normed
        upstream = up_grad[band(i), 128 * k : 128 * k + 128] * slope(normed)
        up_grad[band(i), 128 * k : 128 * k + 128] = upstream
        return (normed, upstream)

    @each(STEPS)
    def _(i):
        one_n, one_g = keep_dec_rows(i, dec_raw[band(i), 0:128], 1)
        two_n, two_g = keep_dec_rows(i, dec_raw[band(i), 128:256], 2)
        put_sums(cols, 0, i, [one_g + two_g, one_g * one_n + two_g * two_n])

    fifth_note = share(5)
    arrive(dec_rows)

    @each(STEPS)
    def _(i):
        keep_dec_rows(i, dec_halo[0, band(i), :].astype(F32), 0)
        keep_dec_rows(i, dec_halo[1, band(i), :].astype(F32), 3)

    total = collect(5, fifth_note)
    spread(ten, 40, mean_rows(total, 0))

    @each(STEPS)
    def _(i):
        inv = coef[band(i), 33:34]
        mean = coef[band(i), 40:41]
        cross = coef[band(i), 41:42]
        strips = []
        for k in range(4):
            lanes = slice(128 * k, 128 * k + 128)
            strips.append(inv * (up_grad[band(i), lanes] - mean - keep_dec[band(i), lanes] * cross))
        put_columns(col_g, spaced, i, masked(strips))

    sfg[...] = dot(back_dec_one[...], col_g[...])
    sfg_edge[0] = sfg[:, 0:128].astype(BF)
    sfg_edge[1] = sfg[:, 128:256].astype(BF)
    sfg_rows = send_rows(7, sfg_edge.at[0], sfg_edge.at[1], sfg_halo.at[0], sfg_halo.at[1])

    @each(STEPS)
    def _(i):
        normed = keep_skip[band(i), 128:384]
        value = sfg[band(i), :] * slope(normed)
        up_grad[band(i), 128:384] = value
        put_sums(cols, 0, i, [value, value * normed])

    sixth_note = share(6)
    arrive(sfg_rows)

    @each(STEPS)
    def _(i):
        for at, lanes in ((0, slice(0, 128)), (1, slice(384, 512))):
            up_grad[band(i), lanes] = sfg_halo[at, band(i), :].astype(F32) * slope(keep_skip[band(i), lanes])

    total = collect(6, sixth_note)
    spread(twenty, 48, mean_rows(total, 0))

    @each(STEPS)
    def _(i):
        inv = coef[band(i), 25:26]
        mean = coef[band(i), 48:49]
        cross = coef[band(i), 49:50]
        value = inv * (up_grad[band(i), :] - mean - keep_skip[band(i), :] * cross) + mixed[band(i), :]
        wide[band(i), :] = value.astype(BF)

    up_grad[...] = dot(zero_t[...], wide[...])

    @each(STEPS)
    def _(i):
        strips = []
        for k in range(4):
            strips.append(up_grad[band(i), 128 * k : 128 * k + 128].astype(BF).astype(F32))
        wide_two[band(i), 0:128] = strips[1].astype(BF)
        wide_two[band(i), 128:256] = strips[2].astype(BF)
        put_columns(col_g, spaced, i, masked(strips))

    def store_grads(k, value, at):
        count = value.shape[1]
        grads[k, 0:160, at : at + count] = value[0:160].astype(BF)
        for start in range(0, count, 128):
            tile = (at + start) // 128
            spot = (tile // 16 * 16 + tile % 4 * 4 + tile // 4 % 4) * 128
            size = min(128, count - start)
            grads[k, 160:C, spot : spot + size] = value[160:C, start : start + size].astype(BF)

    swaps = {}
    pairs = {}
    fours = {}

    def reduce_core(k):
        swaps[k] = remote(
            grads.at[k, :, lanes_at((1 - c) * 2048, 2048)], swap.at[k], rs1_send.at[k], rs1_recv.at[k], partner
        )
        swaps[k].start()
        waiting.append(swaps[k])

    def reduce_far(k):
        swaps[k].wait_recv()

        @each(STEPS)
        def _(i):
            total = grads[k, band(i), lanes_at(c * 2048, 2048)].astype(F32) + swap[k, band(i), :].astype(F32)
            half[k, band(i), :] = total.astype(BF)

        pairs[k] = []
        for axis, (where, ring_peers) in enumerate(((y, y_peers), (x, x_peers))):
            rows = slice(160 * axis, 160 * axis + 160)
            for j, (steps, part, target) in enumerate(((1, 256, 0), (2, 0, 0), (3, 0, 2), (2, 256, 2))):
                block = half.at[k, rows, lanes_at((where + steps) % 4 * 512 + part, 256)]
                pairs[k].append(
                    remote(
                        block,
                        far.at[k, axis, j],
                        rs2_send.at[k, axis, j],
                        rs2_recv.at[k, axis, j],
                        ring_peers[target],
                    )
                )
                pairs[k][-1].start()
        waiting.extend(pairs[k])

    relays = {}

    def reduce_relay(k):
        relays[k] = []
        for axis, (where, ring_peers) in enumerate(((y, y_peers), (x, x_peers))):
            rows = slice(160 * axis, 160 * axis + 160)
            for j, (steps, part, target, source) in enumerate(((1, 0, 0, 1), (3, 256, 2, 3))):
                pairs[k][4 * axis + source].wait_recv()
                own = half[k, rows, lanes_at((where + steps) % 4 * 512 + part, 256)].astype(F32)
                passing[k, axis, j] = (own + far[k, axis, source].astype(F32)).astype(BF)
                relays[k].append(
                    remote(
                        passing.at[k, axis, j],
                        far.at[k, axis, 4 + j],
                        rs2_send.at[k, axis, 4 + j],
                        rs2_recv.at[k, axis, 4 + j],
                        ring_peers[target],
                    )
                )
                relays[k][-1].start()
        waiting.extend(relays[k])

    def reduce_near(k):
        for axis in range(2):
            pairs[k][4 * axis].wait_recv()
            pairs[k][4 * axis + 2].wait_recv()
        for copy in relays[k]:
            copy.wait_recv()
        for axis, where in ((0, y), (1, x)):
            rows = slice(160 * axis, 160 * axis + 160)
            for part, direct, relayed in ((0, 2, 4), (256, 0, 5)):
                total = half[k, rows, lanes_at(where * 512 + part, 256)].astype(F32)
                total = total + far[k, axis, direct].astype(F32) + far[k, axis, relayed].astype(F32)
                near[k, axis, :, part : part + 256] = total.astype(BF)

        fours[k] = []
        for j in (1, 3, 2):
            xa = (x + j) % 4
            yb = (y + j) % 4
            fours[k].append(
                remote(
                    near.at[k, 0, :, lanes_at(xa * 128, 128)],
                    near_in.at[k, 0, j - 1],
                    rs3_send.at[k, 0, j - 1],
                    rs3_recv.at[k, 0, j - 1],
                    x_peers[j - 1],
                )
            )
            fours[k].append(
                remote(
                    near.at[k, 1, :, lanes_at(yb * 128, 128)],
                    near_in.at[k, 1, j - 1],
                    rs3_send.at[k, 1, j - 1],
                    rs3_recv.at[k, 1, j - 1],
                    y_peers[j - 1],
                )
            )
        for copy in fours[k]:
            copy.start()
        waiting.extend(fours[k])

    def reduce_deep(k):
        for copy in fours[k]:
            copy.wait_recv()
        for which, where in ((0, x), (1, y)):
            total = near[k, which, :, lanes_at(where * 128, 128)].astype(F32)
            for j in range(3):
                total = total + near_in[k, which, j].astype(F32)
            deep[160 * which : 160 * which + 160, 128 * k : 128 * k + 128] = total.astype(BF)

    two_value = lax.dot_general(wide_two[...], col_b[...], NT, preferred_element_type=F32)
    store_grads(0, two_value, 0)
    zero_value = lax.dot_general(wide[:, 128:384], ctl_out[...], NT, preferred_element_type=F32)
    store_grads(0, zero_value, 2944)
    reduce_core(0)
    sfg[...] = dot(back_ctl_two[...], col_g[...])

    @each(STEPS)
    def _(i):
        normed = keep_n[band(i), :]
        value = sfg[band(i), :] * slope(normed)
        sfg[band(i), :] = value
        put_sums(cols, 0, i, [value, value * normed])

    seventh_note = share(7)
    reduce_far(0)
    total = collect(7, seventh_note)
    spread(ten, 56, mean_rows(total, 0))

    @each(STEPS)
    def _(i):
        inv = coef[band(i), 65:66]
        mean = coef[band(i), 56:57]
        cross = coef[band(i), 57:58]
        value = inv * (sfg[band(i), :] - mean - keep_n[band(i), :] * cross)
        wide_two[band(i), :] = value.astype(BF)

    one_value = lax.dot_general(wide_two[...], col_a[...], NT, preferred_element_type=F32)
    store_grads(1, one_value, 0)
    reduce_core(1)
    reduce_relay(0)
    reduce_far(1)
    reduce_near(0)
    reduce_relay(1)
    reduce_deep(0)
    reduce_near(1)
    reduce_deep(1)
    ring = []
    for k in range(1, 8):
        zt = (zh + k // 2) % 4
        lt = (zl + k) % 2
        ring.append(
            remote(
                deep.at[pl.ds(pl.multiple_of(zt * 80, 16), 80), lanes_at(lt * 128, 128)],
                deep_in.at[k - 1],
                rs4_send.at[k - 1],
                rs4_recv.at[k - 1],
                z_all[k - 1],
            )
        )
        ring[-1].start()
    total = deep[pl.ds(pl.multiple_of(zh * 80, 16), 80), lanes_at(zl * 128, 128)].astype(F32)
    for k in range(7):
        ring[k].wait_recv()
        total = total + deep_in[k].astype(F32)
    last[...] = total
    for s in range(8):
        spaced_rows = jnp.concatenate([last[10 * s : 10 * s + 10, :], jnp.zeros((6, 128), F32)], axis=0)
        fan[s] = spaced_rows.astype(BF)
    sixth = []
    for k in range(7):
        s = (slot + k + 1) % 8
        sixth.append(remote(fan.at[s], pool.at[r, slot], rs6_send.at[k], rs6_recv.at[k], plane_peers[k]))
        sixth[-1].start()
    mine = pltpu.make_async_copy(fan.at[slot], pool.at[r, slot], out_sem.at[0])
    mine.start()
    mine.wait()
    for copy in sixth:
        copy.wait_recv()
    seventh = []
    for k in range(1, 8):
        seventh.append(
            remote(pool.at[r], pool.at[r], rs7_send.at[k - 1], rs7_recv.at[k - 1], peers[k - 1])
        )
        seventh[-1].start()
    for copy in seventh:
        copy.wait_recv()
    for which, target, count in ((0, two_out, 23), (1, one_out, 23), (0, None, 26)):
        for tile in range(23 if target is None else 0, count):
            core, row_at, column_at = tile // 16, tile // 4 % 4, tile % 4
            value = pool[which * 4 + column_at, row_at * 2 + core, 0:10, :].astype(F32)
            if target is None:
                size = min(128, C - (tile - 23) * 128)
                zero_out[:, (tile - 23) * 128 : (tile - 23) * 128 + size] = value[:, 0:size]
                continue
            at = tile * 128
            while at < min(tile * 128 + 128, 2880):
                tap, offset = divmod(at, C)
                size = min(C - offset, tile * 128 + 128 - at)
                target[tap, :, offset : offset + size] = value[:, at - tile * 128 : at - tile * 128 + size]
                at += size
    for copy in waiting + ring + sixth + seventh:
        copy.wait_send()


def run_step(small, large):
    dma = pltpu.SemaphoreType.DMA
    whole = pl.BlockSpec(memory_space=pltpu.VMEM)
    far_off = pl.BlockSpec(memory_space=pl.ANY)
    return pl.pallas_call(
        step_kernel,
        out_shape=(
            jax.ShapeDtypeStruct((9, 10, C), F32),
            jax.ShapeDtypeStruct((9, 10, C), F32),
            jax.ShapeDtypeStruct((10, C), F32),
        ),
        in_specs=[whole] * len(small) + [far_off] * len(large),
        out_specs=(whole, whole, whole),
        scratch_shapes=[
            pltpu.VMEM((C, 128), F32),
            pltpu.VMEM((C, 128), F32),
            pltpu.VMEM((C, 128), F32),
            pltpu.VMEM((C, 128), F32),
            pltpu.VMEM((C, 128), F32),
            pltpu.VMEM((2, 3, C, 128), BF),
            pltpu.VMEM((2, 2, C, 128), BF),
            pltpu.VMEM((C, 256), F32),
            pltpu.VMEM((4, C, 128), BF),
            pltpu.VMEM((4, C, 128), BF),
            pltpu.VMEM((2880, 256), BF),
            pltpu.VMEM((2880, 256), BF),
            pltpu.VMEM((2880, 256), BF),
            pltpu.VMEM((5760, 256), BF),
            pltpu.VMEM((3456, 256), BF),
            pltpu.VMEM((C, 3456), BF),
            pltpu.VMEM((C, 3456), BF),
            pltpu.VMEM((C, 3456), BF),
            pltpu.VMEM((C, C), BF),
            pltpu.VMEM((C, C), BF),
            pltpu.VMEM((C, 256), F32),
            pltpu.VMEM((C, 256), F32),
            pltpu.VMEM((C, 256), BF),
            pltpu.VMEM((2, C, 128), BF),
            pltpu.VMEM((2, C, 128), BF),
            pltpu.VMEM((C, 256), F32),
            pltpu.VMEM((2, C, 128), BF),
            pltpu.VMEM((2, C, 128), BF),
            pltpu.VMEM((C, 512), F32),
            pltpu.VMEM((C, 256), F32),
            pltpu.VMEM((2, C, 128), BF),
            pltpu.VMEM((2, C, 128), BF),
            pltpu.VMEM((C, 256), F32),
            pltpu.VMEM((C, 512), F32),
            pltpu.VMEM((C, 512), F32),
            pltpu.VMEM((C, 512), F32),
            pltpu.VMEM((C, 512), BF),
            pltpu.VMEM((C, 256), BF),
            pltpu.VMEM((8, 8, 128), F32),
            pltpu.VMEM((8, 7, 8, 128), F32),
            dma((8, 7)),
            dma((8, 7)),
            dma((9, 2)),
            dma((9, 2)),
            pltpu.VMEM((C, 128), F32),
            pltpu.VMEM((C, 1280), BF),
            pltpu.VMEM((3, C, 1280), BF),
            pltpu.VMEM((16, LANES), BF),
            pltpu.VMEM((8, 16, 512), BF),
            pltpu.VMEM((9, C, C), BF),
            pltpu.VMEM((9, C, C), BF),
            dma((6,)),
            pltpu.VMEM((C, LANES), BF),
            pltpu.VMEM((8, 16, 512), BF),
            pltpu.VMEM((80, 512), F32),
            pltpu.VMEM((C, 512), BF),
            dma((5,)),
            dma((7,)),
            dma((7,)),
            dma((4, 3)),
            dma((4, 3)),
            dma((4, 3)),
            dma((4, 3)),
            dma((4, 4)),
            dma((4, 4)),
            dma((4, 4)),
            dma((4, 4)),
            pltpu.VMEM((2, C, HALF), BF),
            pltpu.VMEM((2, C, 2048), BF),
            pltpu.VMEM((2, C, 2048), BF),
            pltpu.VMEM((2, 2, 6, 160, 256), BF),
            pltpu.VMEM((2, 2, 160, 512), BF),
            pltpu.VMEM((2, 2, 2, 160, 256), BF),
            pltpu.VMEM((2, 2, 3, 160, 128), BF),
            pltpu.VMEM((C, 256), BF),
            pltpu.VMEM((7, 80, 128), BF),
            pltpu.VMEM((80, 128), F32),
            pltpu.VMEM((8, 16, 128), BF),
            pltpu.VMEM((8, 8, 16, 128), BF),
            dma((1,)),
            dma((2,)),
            dma((2,)),
            dma((2, 2, 6)),
            dma((2, 2, 6)),
            dma((2, 2, 3)),
            dma((2, 2, 3)),
            dma((7,)),
            dma((7,)),
            dma((7,)),
            dma((7,)),
            dma((7,)),
            dma((7,)),
        ],
        compiler_params=pltpu.CompilerParams(
            collective_id=0, has_side_effects=True, vmem_limit_bytes=63 * 1024 * 1024
        ),
        name="train_step",
    )(*small, *large)


def per_device(
    latent,
    hint_field,
    from_below,
    cotangent,
    timesteps,
    time_weight,
    enc_proj,
    ctl_proj,
    dec_proj,
    enc_conv_one,
    enc_conv_two,
    ctl_conv_one,
    ctl_conv_two,
    dec_conv_one,
    dec_conv_two,
    dec_shortcut,
    zero_conv,
):
    half_width = C // 2
    frequency = jnp.exp(-math.log(10000.0) * jnp.arange(half_width, dtype=jnp.float32) / half_width)
    angles = timesteps.astype(jnp.float32)[:, None] * frequency[None, :]
    sinusoid = jnp.concatenate([jnp.cos(angles), jnp.sin(angles)], axis=1).astype(jnp.bfloat16)
    def by_row(field):
        return jnp.transpose(field[0], (1, 0, 2))

    def by_tap(kernel):
        return jnp.transpose(kernel, (1, 2, 0, 3)).reshape(9, kernel.shape[0], kernel.shape[3])

    def from_tap(grad):
        return jnp.transpose(grad.reshape(3, 3, 10, C), (2, 0, 1, 3))

    one_grad, two_grad, zero_grad = run_step(
        (
            jnp.broadcast_to(sinusoid, (16, C)),
            by_row(latent),
            by_row(hint_field),
            by_row(from_below),
            by_row(cotangent),
            by_tap(ctl_conv_one),
            by_tap(ctl_conv_two),
            by_tap(dec_conv_one),
            by_tap(dec_conv_two),
            dec_shortcut,
            zero_conv,
        ),
        (time_weight, enc_proj.T, ctl_proj.T, dec_proj.T, by_tap(enc_conv_one), by_tap(enc_conv_two)),
    )
    return (from_tap(one_grad), from_tap(two_grad), zero_grad)


def solution(mesh):
    in_specs = (
        P("dp", None, "rows", None),
        P("dp", None, "rows", None),
        P("dp", None, "rows", None),
        P("dp", None, "rows", None),
        P("dp"),
        P(),
        P(),
        P(),
        P(),
        P(),
        P(),
        P("dp", None, None, None),
        P("dp", None, None, None),
        P("dp", None, None, None),
        P("dp", None, None, None),
        P("dp", None),
        P("dp", None),
    )
    out_specs = (P("dp", None, None, None), P("dp", None, None, None), P("dp", None))
    return jax.shard_map(
        per_device, mesh=mesh, in_specs=in_specs, out_specs=out_specs, check_vma=False
    )
```

```python
import math

import jax
import jax.numpy as jnp
from jax import lax
from jax.experimental import pallas as pl
from jax.experimental.pallas import tpu as pltpu
from jax.sharding import PartitionSpec as P

C = 320
EPSILON = 1e-05
MESH = pl.DeviceIdType.MESH
LANES = 16384
HALF = 4096
BF = jnp.bfloat16
F32 = jnp.float32
ROWS = 16
STEPS = C // ROWS
NT = (((1,), (1,)), ((), ()))
TN = (((0,), (0,)), ((), ()))
EXACT = lax.Precision.HIGHEST
AT_CTL_ONE = 0
AT_CTL_TWO = 2944
AT_ZERO = 5888
AT_DEC_ONE = 6272
AT_SHORT = 12032
AT_DEC_TWO = 12416


def place():
    d = lax.axis_index("dp")
    r = lax.axis_index("rows")
    return (d // 8, (d // 2) % 4, d % 2, r // 4, r % 4)


def device_of(zh, y, c, zl, x):
    return (zh * 8 + y * 2 + c, zl * 4 + x)


def remote(src, dst, send, recv, where):
    return pltpu.make_async_remote_copy(
        src_ref=src, dst_ref=dst, send_sem=send, recv_sem=recv, device_id=where, device_id_type=MESH
    )


def greet(peers):
    barrier = pltpu.get_barrier_semaphore()
    for where in peers:
        pl.semaphore_signal(barrier, inc=1, device_id=where, device_id_type=MESH)
    pl.semaphore_wait(barrier, len(peers))


def lanes_at(start, size):
    return pl.ds(pl.multiple_of(start, 128), size)


def band(i):
    return slice(i * ROWS, i * ROWS + ROWS)


def each(count):
    def run(body):
        for i in range(count):
            body(i)

    return run


def put_columns(col, base_of, i, strips):
    lane = lax.broadcasted_iota(jnp.int32, (ROWS, 128), 1)
    shifted_of = []
    for strip in strips:
        left = jnp.where(lane == 0, 0.0, pltpu.roll(strip, 1, axis=1))
        right = jnp.where(lane == 127, 0.0, pltpu.roll(strip, 127, axis=1))
        shifted_of.append([left.astype(BF), strip.astype(BF), right.astype(BF)])
    for p in range(3):
        for q in range(3):
            start = base_of(3 * p + q) + i * ROWS
            col[start : start + ROWS, 0:128] = shifted_of[p][q]
            col[start : start + ROWS, 128:256] = shifted_of[p + 1][q]


def sig(v):
    return jax.nn.sigmoid(v)


def slope(v):
    s = sig(v)
    return s * (1.0 + v * (1.0 - s))


def dot(a, b):
    return jnp.dot(a, b, preferred_element_type=F32)


def taps_dot(kernel, col):
    total = dot(kernel[0], col[0:C, :])
    for tap in range(1, 9):
        total = total + dot(kernel[tap], col[C * tap : C * tap + C, :])
    return total


def three_parts(value):
    high = value.astype(BF).astype(F32)
    rest = value - high
    middle = rest.astype(BF).astype(F32)
    return [high, middle, rest - middle]


def put_sums(cols, at, i, pairs):
    for k, value in enumerate(pairs):
        cols[band(i), at + k : at + k + 1] = jnp.sum(value, axis=1, keepdims=True)


def step_kernel(
    sinus,
    latent_ref,
    hint_ref,
    under_ref,
    cot_ref,
    shard_ctl_one,
    shard_ctl_two,
    shard_dec_one,
    shard_dec_two,
    shard_short,
    shard_zero,
    time_weight_hbm,
    enc_proj_hbm,
    ctl_proj_hbm,
    dec_proj_hbm,
    enc_one_hbm,
    enc_two_hbm,
    one_out,
    two_out,
    zero_out,
    member,
    ten,
    twenty,
    cols,
    coef,
    halo,
    halo_cot,
    inner,
    inner_halo,
    edge,
    col_t,
    col_a,
    col_b,
    col_d,
    col_g,
    back_dec_two,
    back_dec_one,
    back_ctl_two,
    zero_t,
    short_t,
    enc_raw,
    ctl_raw,
    ctl_out,
    skip,
    skip_halo,
    dec_raw,
    dec_halo,
    dec_edge,
    up_grad,
    sfg,
    sfg_edge,
    sfg_halo,
    keep_n,
    keep_skip,
    keep_dec,
    mixed,
    wide,
    wide_two,
    note,
    note_in,
    note_send,
    note_recv,
    halo_send,
    halo_recv,
    time_weight,
    projections,
    stage,
    src,
    enc_one,
    enc_two,
    enc_sem,
    weights,
    parts,
    column,
    gath,
    own_sem,
    ph1_send,
    ph1_recv,
    ph2_send,
    ph2_recv,
    ph3_send,
    ph3_recv,
    ph4_send,
    ph4_recv,
    ph5_send,
    ph5_recv,
    grads,
    swap,
    half,
    far,
    near,
    passing,
    near_in,
    deep,
    deep_in,
    last,
    fan,
    pool,
    tight,
    opened,
    out_sem,
    rs1_send,
    rs1_recv,
    rs2_send,
    rs2_recv,
    rs3_send,
    rs3_recv,
    rs4_send,
    rs4_recv,
    rs6_send,
    rs6_recv,
    rs7_send,
    rs7_recv,
):
    d = lax.axis_index("dp")
    r = lax.axis_index("rows")
    zh, y, c, zl, x = place()
    slot = y * 2 + c
    peers = [(d, (r + k) % 8) for k in range(1, 8)]
    plane_peers = []
    for k in range(1, 8):
        s = (slot + k) % 8
        plane_peers.append(device_of(zh, s // 2, s % 2, zl, x))
    z_peers = [device_of((zh + k) % 4, y, c, zl, x) for k in range(1, 4)]
    x_peers = [device_of(zh, y, c, zl, (x + k) % 4) for k in range(1, 4)]
    y_peers = [device_of(zh, (y + k) % 4, c, zl, x) for k in range(1, 4)]
    partner = device_of(zh, y, 1 - c, zl, x)
    other_z = device_of(zh, y, c, 1 - zl, x)
    z_all = [device_of((zh + k // 2) % 4, y, c, (zl + k) % 2, x) for k in range(1, 8)]
    everyone = peers + plane_peers + z_all[1:]
    barrier = pltpu.get_barrier_semaphore()
    for where in everyone:
        pl.semaphore_signal(barrier, inc=1, device_id=where, device_id_type=MESH)
    loads = []
    for k, (source, target) in enumerate(
        (
            (time_weight_hbm, time_weight),
            (enc_proj_hbm, projections.at[0]),
            (ctl_proj_hbm, projections.at[1]),
            (dec_proj_hbm, projections.at[2]),
            (enc_one_hbm, enc_one),
            (enc_two_hbm, enc_two),
        )
    ):
        loads.append(pltpu.make_async_copy(source, target, enc_sem.at[k]))
        loads[-1].start()
    load_one, load_two = loads[4:]

    stage[...] = jnp.zeros((16, LANES), BF)
    for kernel, start, count, width in (
        (shard_ctl_one, AT_CTL_ONE, 9, C),
        (shard_ctl_two, AT_CTL_TWO, 9, C),
        (shard_dec_one, AT_DEC_ONE, 9, 2 * C),
        (shard_dec_two, AT_DEC_TWO, 9, C),
    ):
        for tap in range(count):
            stage[0:10, start + width * tap : start + width * tap + width] = kernel[tap]
    stage[0:10, AT_ZERO : AT_ZERO + C] = shard_zero[...]
    stage[0:10, AT_SHORT : AT_SHORT + C] = shard_short[:, C : 2 * C]
    for s in range(8):
        for g in range(4):
            tile = (x * 2 + s % 2) * 4 + s // 2 if g % 2 else s * 4 + x
            src[s, :, 128 * g : 128 * g + 128] = stage[:, lanes_at(g * 4096 + tile * 128, 128)]

    lane = lax.broadcasted_iota(jnp.int32, (C, 128), 1)
    channel = lax.broadcasted_iota(jnp.int32, (C, 128), 0)
    in_ten = (channel >= 10 * lane) & (channel < 10 * lane + 10)
    other = lane - 32
    in_twenty = (channel >= 20 * other) & (channel < 20 * other + 20)
    one_ten = jnp.where(in_ten, 1.0, 0.0)
    one_twenty = jnp.where(in_twenty, 1.0, 0.0)
    member[...] = (one_ten + one_twenty).astype(BF)
    for k in range(3):
        ten[:, 128 * k : 128 * k + 128] = one_ten.astype(BF)
        twenty[:, 128 * k : 128 * k + 128] = one_twenty.astype(BF)
    cols[...] = jnp.zeros((C, 128), F32)

    @each(STEPS)
    def _(i):
        sums = [0.0] * 6
        for h in range(2):
            latent = latent_ref[h, band(i), :].astype(F32)
            ctl_in = (latent + hint_ref[h, band(i), :].astype(F32)).astype(BF).astype(F32)
            under = under_ref[h, band(i), :].astype(F32)
            for k, value in enumerate((latent, latent * latent, ctl_in, ctl_in * ctl_in, under, under * under)):
                sums[k] = sums[k] + value
        put_sums(cols, 0, i, sums)

    pl.semaphore_wait(barrier, len(everyone))
    before = (d, (r + 7) % 8)
    after = (d, (r + 1) % 8)
    waiting = []

    def send_rows(event, top, bottom, above, below):
        first = remote(top, below, halo_send.at[event, 0], halo_recv.at[event, 0], before)
        second = remote(bottom, above, halo_send.at[event, 1], halo_recv.at[event, 1], after)
        first.start()
        second.start()
        waiting.extend([first, second])
        return (first, second)

    def arrive(pair):
        pair[0].wait_recv()
        pair[1].wait_recv()

    raw = send_rows(0, latent_ref.at[0], latent_ref.at[1], halo.at[0, 0], halo.at[1, 0])
    raw_hint = send_rows(8, hint_ref.at[0], hint_ref.at[1], halo.at[0, 1], halo.at[1, 1])
    first = []
    for k in range(7):
        s = (slot + k + 1) % 8
        first.append(remote(src.at[s], parts.at[slot], ph1_send.at[k], ph1_recv.at[k], plane_peers[k]))
        first[-1].start()
    waiting.extend(first)
    mine = pltpu.make_async_copy(src.at[slot], parts.at[slot], own_sem.at[4])
    mine.start()

    second = {}
    third = {}
    fourth = {}
    fifth = {}
    held = {}

    def gather_z():
        mine.wait()
        for copy in first:
            copy.wait_recv()
        for s in range(8):
            column[10 * s : 10 * s + 10, :] = parts[s, 0:10, :].astype(F32)
        home = pl.multiple_of(zh * 80, 16)
        gath[pl.ds(home, 80), :] = column[...].astype(BF)
        for g in range(4):
            block = gath.at[pl.ds(home, 80), 128 * g : 128 * g + 128]
            second[g] = []
            for k in (0, 2, 1):
                second[g].append(remote(block, block, ph2_send.at[g, k], ph2_recv.at[g, k], z_peers[k]))
                second[g][-1].start()
            waiting.extend(second[g])

    def gather_short(g):
        for copy in second[g]:
            copy.wait_recv()
        block = gath.at[:, 128 * g : 128 * g + 128]
        tile = (x * 2 + c) * 4 + y if g % 2 else slot * 4 + x
        short_peers = y_peers if g % 2 else x_peers
        spot = weights.at[:, lanes_at(g * 4096 + tile * 128, 128)]
        third[g] = []
        for k in (0, 2, 1):
            third[g].append(remote(block, spot, ph3_send.at[g, k], ph3_recv.at[g, k], short_peers[k]))
            third[g][-1].start()
        waiting.extend(third[g])
        held[g] = pltpu.make_async_copy(block, spot, own_sem.at[g])
        held[g].start()

    def column_of(g, steps, at, size):
        where = x if g % 2 else y
        return weights.at[:, lanes_at(g * 4096 + ((where + 4 + steps) % 4 * 2 + c) * 512 + at, size)]

    def to_partner(g, k, steps):
        block = column_of(g, steps, 0, 512)
        copy = remote(block, block, ph5_send.at[g, k], ph5_recv.at[g, k], partner)
        copy.start()
        fifth[g].append(copy)
        waiting.append(copy)

    def long_peers(g):
        return x_peers if g % 2 else y_peers

    def gather_long(g):
        held[g].wait()
        for copy in third[g]:
            copy.wait_recv()
        block = column_of(g, 0, 0, 512)
        fourth[g] = [
            remote(block, block, ph4_send.at[g, 0], ph4_recv.at[g, 0], long_peers(g)[0]),
            remote(block, block, ph4_send.at[g, 1], ph4_recv.at[g, 1], long_peers(g)[2]),
        ]
        for copy in fourth[g]:
            copy.start()
        waiting.extend(fourth[g])
        fifth[g] = []
        to_partner(g, 0, 0)

    def gather_relay(g):
        fourth[g][0].wait_recv()
        block = column_of(g, -1, 0, 256)
        up = remote(block, block, ph4_send.at[g, 2], ph4_recv.at[g, 2], long_peers(g)[0])
        up.start()
        fourth[g][1].wait_recv()
        block = column_of(g, 1, 256, 256)
        down = remote(block, block, ph4_send.at[g, 3], ph4_recv.at[g, 3], long_peers(g)[2])
        down.start()
        fourth[g].extend([up, down])
        waiting.extend([up, down])
        to_partner(g, 1, -1)
        to_partner(g, 2, 1)

    def gather_finish(g):
        fourth[g][2].wait_recv()
        fourth[g][3].wait_recv()
        to_partner(g, 3, 2)

    def gather_done(g):
        for copy in fifth[g]:
            copy.wait_recv()


    def share(turn):
        turned = cols[:, 0:8].T
        sums = dot(jnp.concatenate(three_parts(turned), axis=0).astype(BF), member[...])
        note[turn] = sums[0:8] + sums[8:16] + sums[16:24]
        copies = []
        for k in range(1, 8):
            copies.append(
                remote(
                    note.at[turn],
                    note_in.at[turn, k - 1],
                    note_send.at[turn, k - 1],
                    note_recv.at[turn, k - 1],
                    peers[k - 1],
                )
            )
            copies[-1].start()
        waiting.extend(copies)
        return copies

    def collect(turn, copies):
        for copy in copies:
            copy.wait_recv()
        total = note[turn]
        for k in range(7):
            total = total + note_in[turn, k]
        return total

    which = lax.broadcasted_iota(jnp.int32, (8, 128), 1)
    per_group = jnp.where(which < 32, 1.0 / (10 * 2048), 1.0 / (20 * 2048))

    def spread(table, at, rows):
        wide_rows = [
            jnp.broadcast_to(jnp.concatenate(three_parts(row), axis=1), (128, 384)).astype(BF) for row in rows
        ]
        columns = lax.dot_general(
            table[...], jnp.concatenate(wide_rows, axis=0), NT, preferred_element_type=F32
        )
        for k in range(len(rows)):
            coef[at + k] = columns[:, 128 * k : 128 * k + 128]

    def raw_sums(raw_ref, term_at, i):
        term = coef[term_at, band(i), :]
        one = raw_ref[band(i), 0:128] + term
        two = raw_ref[band(i), 128:256] + term
        put_sums(cols, 0, i, [one + two, one * one + two * two])

    def norm_rows(total, k):
        mean = total[k : k + 1] * per_group[0:1]
        square = total[k + 1 : k + 2] * per_group[0:1]
        return [mean, lax.rsqrt(square - mean * mean + EPSILON)]

    def mean_rows(total, k):
        return [total[k : k + 1] * per_group[0:1], total[k + 1 : k + 2] * per_group[0:1]]

    has_up = r > 0
    has_down = r < 7

    def masked(strips):
        return [
            jnp.where(has_up, strips[0], 0.0),
            strips[1],
            strips[2],
            jnp.where(has_down, strips[3], 0.0),
        ]

    first_note = share(0)
    late = send_rows(1, under_ref.at[0], under_ref.at[1], halo.at[0, 2], halo.at[1, 2])
    late_cot = send_rows(2, cot_ref, cot_ref, halo_cot.at[0], halo_cot.at[1])
    for load in loads[0:4]:
        load.wait()
    embed = dot(sinus[...], time_weight[...])
    embed = (embed * sig(embed)).astype(BF)
    for k in range(3):
        term = lax.dot_general(projections[k], embed, NT, preferred_element_type=F32)
        coef[20 + k] = jnp.broadcast_to(term[:, 0:1], (C, 128))
    for target in (back_dec_two, back_dec_one, back_ctl_two):
        for tap in range(9):
            target[:, 384 * tap + 320 : 384 * tap + 384] = jnp.zeros((C, 64), BF)
    for tap in range(9):
        col_g[384 * tap + 320 : 384 * tap + 384, :] = jnp.zeros((64, 256), BF)
    grads[0, :, 2816:HALF] = jnp.zeros((C, HALF - 2816), BF)
    grads[0, 160:C, :] = jnp.zeros((160, HALF), BF)
    grads[1, :, 2816:HALF] = jnp.zeros((C, HALF - 2816), BF)
    grads[1, 160:C, :] = jnp.zeros((160, HALF), BF)

    def turn(target, start, stride):
        for tap in range(9):
            block = weights[:, start + stride * tap : start + stride * tap + 320].astype(F32)
            target[:, 384 * (8 - tap) : 384 * (8 - tap) + 320] = block.T.astype(BF)

    def turn_square(target, start):
        target[...] = weights[:, start : start + 320].astype(F32).T.astype(BF)

    gather_z()
    total = collect(0, first_note)
    spread(ten, 0, norm_rows(total, 0) + norm_rows(total, 2))
    spread(twenty, 4, norm_rows(total, 4))
    arrive(raw)
    arrive(raw_hint)

    def plain(tap):
        return 320 * tap

    def first_act(source_of, at, col, base_of):
        @each(STEPS)
        def _(i):
            mean = coef[at, band(i), :]
            inv = coef[at + 1, band(i), :]
            strips = []
            for strip in source_of(i):
                normed = (strip - mean) * inv
                strips.append(normed * sig(normed))
            put_columns(col, base_of, i, masked(strips))

    def latent_of(i):
        return [
            halo[0, 0, band(i), :].astype(F32),
            latent_ref[0, band(i), :].astype(F32),
            latent_ref[1, band(i), :].astype(F32),
            halo[1, 0, band(i), :].astype(F32),
        ]

    def ctl_in_of(i):
        hint = [
            halo[0, 1, band(i), :].astype(F32),
            hint_ref[0, band(i), :].astype(F32),
            hint_ref[1, band(i), :].astype(F32),
            halo[1, 1, band(i), :].astype(F32),
        ]
        return [(a + b).astype(BF).astype(F32) for a, b in zip(latent_of(i), hint)]

    first_act(latent_of, 0, col_t, plain)
    load_one.wait()
    enc_raw[...] = taps_dot(enc_one, col_t)
    edge[0] = enc_raw[:, 0:128].astype(BF)
    edge[1] = enc_raw[:, 128:256].astype(BF)
    enc_rows = send_rows(3, edge.at[0], edge.at[1], inner_halo.at[0], inner_halo.at[1])

    @each(STEPS)
    def _(i):
        raw_sums(enc_raw, 20, i)

    second_note = share(1)
    gather_short(0)
    first_act(ctl_in_of, 2, col_a, plain)

    def under_of(i):
        return [
            halo[0, 2, band(i), :].astype(F32),
            under_ref[0, band(i), :].astype(F32),
            under_ref[1, band(i), :].astype(F32),
            halo[1, 2, band(i), :].astype(F32),
        ]

    def joined_low(tap):
        return 640 * tap

    def joined_high(tap):
        return 640 * tap + 320

    def spaced(tap):
        return 384 * tap

    arrive(late)
    first_act(under_of, 4, col_d, joined_low)

    gather_short(1)
    gather_long(0)
    gather_short(2)
    total = collect(1, second_note)
    spread(ten, 6, norm_rows(total, 0))

    def second_act(raw_ref, at_halo, term_at, at, col, keep):
        @each(STEPS)
        def _(i):
            mean = coef[at, band(i), :]
            inv = coef[at + 1, band(i), :]
            own = raw_ref[band(i), :]
            term = coef[20 + term_at, band(i), :]
            strips = []
            for strip in (
                inner_halo[at_halo, band(i), :].astype(F32),
                own[:, 0:128],
                own[:, 128:256],
                inner_halo[at_halo + 1, band(i), :].astype(F32),
            ):
                strips.append((strip + term - mean) * inv)
            if keep is not None:
                keep[band(i), 0:128] = strips[1]
                keep[band(i), 128:256] = strips[2]
            put_columns(col, plain, i, masked([v * sig(v) for v in strips]))

    arrive(enc_rows)
    second_act(enc_raw, 0, 0, 6, col_t, None)
    load_two.wait()
    enc_raw[...] = taps_dot(enc_two, col_t)
    gather_long(1)
    gather_relay(0)
    gather_short(3)
    gather_long(2)
    gather_finish(0)
    gather_done(0)
    ctl_raw[...] = dot(weights[:, AT_CTL_ONE : AT_CTL_ONE + 2880], col_a[...])
    edge[2] = ctl_raw[:, 0:128].astype(BF)
    edge[3] = ctl_raw[:, 128:256].astype(BF)
    ctl_rows = send_rows(4, edge.at[2], edge.at[3], inner_halo.at[2], inner_halo.at[3])

    @each(STEPS)
    def _(i):
        raw_sums(ctl_raw, 21, i)

    ctl_note = share(2)
    gather_relay(1)
    total = collect(2, ctl_note)
    spread(ten, 8, norm_rows(total, 0))
    arrive(ctl_rows)
    second_act(ctl_raw, 2, 1, 8, col_b, keep_n)
    gather_long(3)
    gather_finish(1)
    gather_done(1)
    inner[...] = dot(weights[:, AT_CTL_TWO : AT_CTL_TWO + 2880], col_b[...])

    @each(STEPS)
    def _(i):
        own = ctl_in_of(i)
        ctl_out[band(i), 0:128] = (own[1] + inner[band(i), 0:128]).astype(BF)
        ctl_out[band(i), 128:256] = (own[2] + inner[band(i), 128:256]).astype(BF)

    inner[...] = dot(weights[:, AT_ZERO : AT_ZERO + 320], ctl_out[...])

    @each(STEPS)
    def _(i):
        sums = [0.0, 0.0]
        for h in range(2):
            lanes = slice(128 * h, 128 * h + 128)
            latent = latent_ref[h, band(i), :].astype(F32)
            enc_out = (latent + enc_raw[band(i), lanes]).astype(BF).astype(F32)
            joined = (enc_out + inner[band(i), lanes]).astype(BF)
            skip[h, band(i), :] = joined
            value = joined.astype(F32)
            sums = [sums[0] + value, sums[1] + value * value]
        put_sums(cols, 0, i, sums)

    skip_rows = send_rows(5, skip.at[0], skip.at[1], skip_halo.at[0], skip_halo.at[1])
    third_note = share(3)
    turn(back_ctl_two, AT_CTL_TWO, 320)
    turn_square(zero_t, AT_ZERO)
    gather_relay(2)
    gather_relay(3)

    total = collect(3, third_note)
    spread(twenty, 10, norm_rows(total, 0))
    arrive(skip_rows)

    @each(STEPS)
    def _(i):
        mean = coef[10, band(i), :]
        inv = coef[11, band(i), :]
        strips = []
        for k, strip in enumerate(
            (skip_halo[0, band(i), :], skip[0, band(i), :], skip[1, band(i), :], skip_halo[1, band(i), :])
        ):
            normed = (strip.astype(F32) - mean) * inv
            keep_skip[band(i), 128 * k : 128 * k + 128] = normed
            strips.append(normed * sig(normed))
        put_columns(col_d, joined_high, i, masked(strips))

    gather_finish(2)
    gather_done(2)
    dec_raw[...] = dot(weights[:, AT_DEC_ONE : AT_DEC_ONE + 5760], col_d[...])
    dec_edge[0] = dec_raw[:, 0:128].astype(BF)
    dec_edge[1] = dec_raw[:, 128:256].astype(BF)
    dec_rows = send_rows(6, dec_edge.at[0], dec_edge.at[1], dec_halo.at[0], dec_halo.at[1])

    @each(STEPS)
    def _(i):
        raw_sums(dec_raw, 22, i)

    fourth_note = share(4)
    turn(back_dec_one, AT_DEC_ONE + 320, 640)
    gather_finish(3)
    arrive(late_cot)
    scale = 2.0**-8

    def cot_of(i):
        far_rows = [jnp.where(has_up, halo_cot[0, h, band(i), :].astype(F32), 0.0) for h in range(2)]
        own = [cot_ref[h, band(i), :].astype(F32) for h in range(2)]
        near_rows = [jnp.where(has_down, halo_cot[1, h, band(i), :].astype(F32), 0.0) for h in range(2)]
        return [strip * scale for strip in far_rows + own + near_rows]

    gather_done(3)
    turn(back_dec_two, AT_DEC_TWO, 320)
    turn_square(short_t, AT_SHORT)
    for part in range(2):

        @each(STEPS)
        def _(i):
            strips = cot_of(i)[2 * part : 2 * part + 4]
            put_columns(col_g, spaced, i, strips)

        up_grad[:, 256 * part : 256 * part + 256] = dot(back_dec_two[...], col_g[...])

    @each(STEPS)
    def _(i):
        for k, strip in enumerate(cot_of(i)[1:5]):
            wide[band(i), 128 * k : 128 * k + 128] = strip.astype(BF)

    mixed[...] = dot(short_t[...], wide[...])

    total = collect(4, fourth_note)
    spread(ten, 12, norm_rows(total, 0))

    def keep_dec_rows(i, strip, k):
        mean = coef[12, band(i), :]
        inv = coef[13, band(i), :]
        term = coef[22, band(i), :]
        normed = (strip + term - mean) * inv
        keep_dec[band(i), 128 * k : 128 * k + 128] = normed
        upstream = up_grad[band(i), 128 * k : 128 * k + 128] * slope(normed)
        up_grad[band(i), 128 * k : 128 * k + 128] = upstream
        return (normed, upstream)

    @each(STEPS)
    def _(i):
        one_n, one_g = keep_dec_rows(i, dec_raw[band(i), 0:128], 1)
        two_n, two_g = keep_dec_rows(i, dec_raw[band(i), 128:256], 2)
        put_sums(cols, 0, i, [one_g + two_g, one_g * one_n + two_g * two_n])

    fifth_note = share(5)
    arrive(dec_rows)

    @each(STEPS)
    def _(i):
        keep_dec_rows(i, dec_halo[0, band(i), :].astype(F32), 0)
        keep_dec_rows(i, dec_halo[1, band(i), :].astype(F32), 3)

    total = collect(5, fifth_note)
    spread(ten, 14, mean_rows(total, 0))

    @each(STEPS)
    def _(i):
        inv = coef[13, band(i), :]
        mean = coef[14, band(i), :]
        cross = coef[15, band(i), :]
        strips = []
        for k in range(4):
            lanes = slice(128 * k, 128 * k + 128)
            strips.append(inv * (up_grad[band(i), lanes] - mean - keep_dec[band(i), lanes] * cross))
        put_columns(col_g, spaced, i, masked(strips))

    sfg[...] = dot(back_dec_one[...], col_g[...])
    sfg_edge[0] = sfg[:, 0:128].astype(BF)
    sfg_edge[1] = sfg[:, 128:256].astype(BF)
    sfg_rows = send_rows(7, sfg_edge.at[0], sfg_edge.at[1], sfg_halo.at[0], sfg_halo.at[1])

    @each(STEPS)
    def _(i):
        normed = keep_skip[band(i), 128:384]
        value = sfg[band(i), :] * slope(normed)
        up_grad[band(i), 128:384] = value
        put_sums(cols, 0, i, [value, value * normed])

    sixth_note = share(6)
    arrive(sfg_rows)

    @each(STEPS)
    def _(i):
        for at, lanes in ((0, slice(0, 128)), (1, slice(384, 512))):
            up_grad[band(i), lanes] = sfg_halo[at, band(i), :].astype(F32) * slope(keep_skip[band(i), lanes])

    total = collect(6, sixth_note)
    spread(twenty, 16, mean_rows(total, 0))

    @each(STEPS)
    def _(i):
        inv = coef[11, band(i), :]
        mean = coef[16, band(i), :]
        cross = coef[17, band(i), :]
        for k in range(4):
            lanes = slice(128 * k, 128 * k + 128)
            value = inv * (up_grad[band(i), lanes] - mean - keep_skip[band(i), lanes] * cross) + mixed[band(i), lanes]
            wide[band(i), lanes] = value.astype(BF)

    up_grad[...] = dot(zero_t[...], wide[...])

    @each(STEPS)
    def _(i):
        strips = []
        for k in range(4):
            strips.append(up_grad[band(i), 128 * k : 128 * k + 128].astype(BF).astype(F32))
        wide_two[band(i), 0:128] = strips[1].astype(BF)
        wide_two[band(i), 128:256] = strips[2].astype(BF)
        put_columns(col_g, spaced, i, masked(strips))

    def store_grads(k, value, at):
        count = value.shape[1]
        grads[k, 0:160, at : at + count] = value[0:160].astype(BF)
        for start in range(0, count, 128):
            tile = (at + start) // 128
            spot = (tile // 16 * 16 + tile % 4 * 4 + tile // 4 % 4) * 128
            size = min(128, count - start)
            grads[k, 160:C, spot : spot + size] = value[160:C, start : start + size].astype(BF)

    swaps = {}
    pairs = {}
    fours = {}

    def reduce_core(k):
        swaps[k] = remote(
            grads.at[k, :, lanes_at((1 - c) * 2048, 2048)], swap.at[k], rs1_send.at[k], rs1_recv.at[k], partner
        )
        swaps[k].start()
        waiting.append(swaps[k])

    def reduce_far(k):
        swaps[k].wait_recv()

        @each(STEPS)
        def _(i):
            total = grads[k, band(i), lanes_at(c * 2048, 2048)].astype(F32) + swap[k, band(i), :].astype(F32)
            half[k, band(i), :] = total.astype(BF)

        pairs[k] = []
        for axis, (where, ring_peers) in enumerate(((y, y_peers), (x, x_peers))):
            rows = slice(160 * axis, 160 * axis + 160)
            for j, (steps, part, target) in enumerate(((1, 256, 0), (2, 0, 0), (3, 0, 2), (2, 256, 2))):
                block = half.at[k, rows, lanes_at((where + steps) % 4 * 512 + part, 256)]
                pairs[k].append(
                    remote(
                        block,
                        far.at[k, axis, j],
                        rs2_send.at[k, axis, j],
                        rs2_recv.at[k, axis, j],
                        ring_peers[target],
                    )
                )
                pairs[k][-1].start()
        waiting.extend(pairs[k])

    relays = {}

    def reduce_relay(k):
        relays[k] = []
        for axis, (where, ring_peers) in enumerate(((y, y_peers), (x, x_peers))):
            rows = slice(160 * axis, 160 * axis + 160)
            for j, (steps, part, target, source) in enumerate(((1, 0, 0, 1), (3, 256, 2, 3))):
                pairs[k][4 * axis + source].wait_recv()
                own = half[k, rows, lanes_at((where + steps) % 4 * 512 + part, 256)].astype(F32)
                passing[k, axis, j] = (own + far[k, axis, source].astype(F32)).astype(BF)
                relays[k].append(
                    remote(
                        passing.at[k, axis, j],
                        far.at[k, axis, 4 + j],
                        rs2_send.at[k, axis, 4 + j],
                        rs2_recv.at[k, axis, 4 + j],
                        ring_peers[target],
                    )
                )
                relays[k][-1].start()
        waiting.extend(relays[k])

    def reduce_near(k):
        for axis in range(2):
            pairs[k][4 * axis].wait_recv()
            pairs[k][4 * axis + 2].wait_recv()
        for copy in relays[k]:
            copy.wait_recv()
        for axis, where in ((0, y), (1, x)):
            rows = slice(160 * axis, 160 * axis + 160)
            for part, direct, relayed in ((0, 2, 4), (256, 0, 5)):
                total = half[k, rows, lanes_at(where * 512 + part, 256)].astype(F32)
                total = total + far[k, axis, direct].astype(F32) + far[k, axis, relayed].astype(F32)
                near[k, axis, :, part : part + 256] = total.astype(BF)

        fours[k] = []
        for j in (1, 3, 2):
            xa = (x + j) % 4
            yb = (y + j) % 4
            fours[k].append(
                remote(
                    near.at[k, 0, :, lanes_at(xa * 128, 128)],
                    near_in.at[k, 0, j - 1],
                    rs3_send.at[k, 0, j - 1],
                    rs3_recv.at[k, 0, j - 1],
                    x_peers[j - 1],
                )
            )
            fours[k].append(
                remote(
                    near.at[k, 1, :, lanes_at(yb * 128, 128)],
                    near_in.at[k, 1, j - 1],
                    rs3_send.at[k, 1, j - 1],
                    rs3_recv.at[k, 1, j - 1],
                    y_peers[j - 1],
                )
            )
        for copy in fours[k]:
            copy.start()
        waiting.extend(fours[k])

    def reduce_deep(k):
        for copy in fours[k]:
            copy.wait_recv()
        for which, where in ((0, x), (1, y)):
            total = near[k, which, :, lanes_at(where * 128, 128)].astype(F32)
            for j in range(3):
                total = total + near_in[k, which, j].astype(F32)
            deep[160 * which : 160 * which + 160, 128 * k : 128 * k + 128] = total.astype(BF)

    two_value = lax.dot_general(wide_two[...], col_b[...], NT, preferred_element_type=F32)
    store_grads(0, two_value, 0)
    zero_value = lax.dot_general(wide[:, 128:384], ctl_out[...], NT, preferred_element_type=F32)
    store_grads(0, zero_value, 2944)
    reduce_core(0)
    sfg[...] = dot(back_ctl_two[...], col_g[...])

    @each(STEPS)
    def _(i):
        normed = keep_n[band(i), :]
        value = sfg[band(i), :] * slope(normed)
        sfg[band(i), :] = value
        put_sums(cols, 0, i, [value, value * normed])

    seventh_note = share(7)
    reduce_far(0)
    total = collect(7, seventh_note)
    spread(ten, 18, mean_rows(total, 0))

    @each(STEPS)
    def _(i):
        inv = coef[9, band(i), :]
        mean = coef[18, band(i), :]
        cross = coef[19, band(i), :]
        for lanes in (slice(0, 128), slice(128, 256)):
            value = inv * (sfg[band(i), lanes] - mean - keep_n[band(i), lanes] * cross)
            wide_two[band(i), lanes] = value.astype(BF)

    one_value = lax.dot_general(wide_two[...], col_a[...], NT, preferred_element_type=F32)
    store_grads(1, one_value, 0)
    reduce_core(1)
    reduce_relay(0)
    reduce_far(1)
    reduce_near(0)
    reduce_relay(1)
    reduce_deep(0)
    reduce_near(1)
    reduce_deep(1)
    ring = []
    for k in range(1, 8):
        zt = (zh + k // 2) % 4
        lt = (zl + k) % 2
        ring.append(
            remote(
                deep.at[pl.ds(pl.multiple_of(zt * 80, 16), 80), lanes_at(lt * 128, 128)],
                deep_in.at[k - 1],
                rs4_send.at[k - 1],
                rs4_recv.at[k - 1],
                z_all[k - 1],
            )
        )
        ring[-1].start()
    total = deep[pl.ds(pl.multiple_of(zh * 80, 16), 80), lanes_at(zl * 128, 128)].astype(F32)
    for k in range(7):
        ring[k].wait_recv()
        total = total + deep_in[k].astype(F32)
    last[...] = total
    for s in range(8):
        spaced_rows = jnp.concatenate([last[10 * s : 10 * s + 10, :], jnp.zeros((6, 128), F32)], axis=0)
        fan[s] = spaced_rows.astype(BF)
    sixth = []
    for k in range(7):
        s = (slot + k + 1) % 8
        sixth.append(remote(fan.at[s], pool.at[slot], rs6_send.at[k], rs6_recv.at[k], plane_peers[k]))
        sixth[-1].start()
    mine = pltpu.make_async_copy(fan.at[slot], pool.at[slot], out_sem.at[0])
    mine.start()
    mine.wait()
    for copy in sixth:
        copy.wait_recv()
    for s in range(8):
        last[10 * s : 10 * s + 10, :] = pool[s, 0:10, :].astype(F32)
    tight[r] = last[...].astype(BF)
    seventh = []
    for k in range(1, 8):
        seventh.append(
            remote(tight.at[r], tight.at[r], rs7_send.at[k - 1], rs7_recv.at[k - 1], peers[k - 1])
        )
        seventh[-1].start()
    for copy in seventh:
        copy.wait_recv()
    opened[...] = tight[...].astype(F32)
    for which, target, count in ((0, two_out, 23), (1, one_out, 23), (0, None, 26)):
        for tile in range(23 if target is None else 0, count):
            core, row_at, column_at = tile // 16, tile // 4 % 4, tile % 4
            at = 10 * (row_at * 2 + core)
            value = opened[which * 4 + column_at, at : at + 10, :]
            if target is None:
                size = min(128, C - (tile - 23) * 128)
                zero_out[:, (tile - 23) * 128 : (tile - 23) * 128 + size] = value[:, 0:size]
                continue
            at = tile * 128
            while at < min(tile * 128 + 128, 2880):
                tap, offset = divmod(at, C)
                size = min(C - offset, tile * 128 + 128 - at)
                target[tap, :, offset : offset + size] = value[:, at - tile * 128 : at - tile * 128 + size]
                at += size
    for copy in waiting + ring + sixth + seventh:
        copy.wait_send()


def run_step(small, large):
    dma = pltpu.SemaphoreType.DMA
    whole = pl.BlockSpec(memory_space=pltpu.VMEM)
    far_off = pl.BlockSpec(memory_space=pl.ANY)
    return pl.pallas_call(
        step_kernel,
        out_shape=(
            jax.ShapeDtypeStruct((9, 10, C), F32),
            jax.ShapeDtypeStruct((9, 10, C), F32),
            jax.ShapeDtypeStruct((10, C), F32),
        ),
        in_specs=[whole] * len(small) + [far_off] * len(large),
        out_specs=(whole, whole, whole),
        scratch_shapes=[
            pltpu.VMEM((C, 128), BF),
            pltpu.VMEM((C, 384), BF),
            pltpu.VMEM((C, 384), BF),
            pltpu.VMEM((C, 128), F32),
            pltpu.VMEM((23, C, 128), F32),
            pltpu.VMEM((2, 3, C, 128), BF),
            pltpu.VMEM((2, 2, C, 128), BF),
            pltpu.VMEM((C, 256), F32),
            pltpu.VMEM((4, C, 128), BF),
            pltpu.VMEM((4, C, 128), BF),
            pltpu.VMEM((2880, 256), BF),
            pltpu.VMEM((2880, 256), BF),
            pltpu.VMEM((2880, 256), BF),
            pltpu.VMEM((5760, 256), BF),
            pltpu.VMEM((3456, 256), BF),
            pltpu.VMEM((C, 3456), BF),
            pltpu.VMEM((C, 3456), BF),
            pltpu.VMEM((C, 3456), BF),
            pltpu.VMEM((C, C), BF),
            pltpu.VMEM((C, C), BF),
            pltpu.VMEM((C, 256), F32),
            pltpu.VMEM((C, 256), F32),
            pltpu.VMEM((C, 256), BF),
            pltpu.VMEM((2, C, 128), BF),
            pltpu.VMEM((2, C, 128), BF),
            pltpu.VMEM((C, 256), F32),
            pltpu.VMEM((2, C, 128), BF),
            pltpu.VMEM((2, C, 128), BF),
            pltpu.VMEM((C, 512), F32),
            pltpu.VMEM((C, 256), F32),
            pltpu.VMEM((2, C, 128), BF),
            pltpu.VMEM((2, C, 128), BF),
            pltpu.VMEM((C, 256), F32),
            pltpu.VMEM((C, 512), F32),
            pltpu.VMEM((C, 512), F32),
            pltpu.VMEM((C, 512), F32),
            pltpu.VMEM((C, 512), BF),
            pltpu.VMEM((C, 256), BF),
            pltpu.VMEM((8, 8, 128), F32),
            pltpu.VMEM((8, 7, 8, 128), F32),
            dma((8, 7)),
            dma((8, 7)),
            dma((9, 2)),
            dma((9, 2)),
            pltpu.VMEM((C, 1280), BF),
            pltpu.VMEM((3, C, 1280), BF),
            pltpu.VMEM((16, LANES), BF),
            pltpu.VMEM((8, 16, 512), BF),
            pltpu.VMEM((9, C, C), BF),
            pltpu.VMEM((9, C, C), BF),
            dma((6,)),
            pltpu.VMEM((C, LANES), BF),
            pltpu.VMEM((8, 16, 512), BF),
            pltpu.VMEM((80, 512), F32),
            pltpu.VMEM((C, 512), BF),
            dma((5,)),
            dma((7,)),
            dma((7,)),
            dma((4, 3)),
            dma((4, 3)),
            dma((4, 3)),
            dma((4, 3)),
            dma((4, 4)),
            dma((4, 4)),
            dma((4, 4)),
            dma((4, 4)),
            pltpu.VMEM((2, C, HALF), BF),
            pltpu.VMEM((2, C, 2048), BF),
            pltpu.VMEM((2, C, 2048), BF),
            pltpu.VMEM((2, 2, 6, 160, 256), BF),
            pltpu.VMEM((2, 2, 160, 512), BF),
            pltpu.VMEM((2, 2, 2, 160, 256), BF),
            pltpu.VMEM((2, 2, 3, 160, 128), BF),
            pltpu.VMEM((C, 256), BF),
            pltpu.VMEM((7, 80, 128), BF),
            pltpu.VMEM((80, 128), F32),
            pltpu.VMEM((8, 16, 128), BF),
            pltpu.VMEM((8, 16, 128), BF),
            pltpu.VMEM((8, 80, 128), BF),
            pltpu.VMEM((8, 80, 128), F32),
            dma((1,)),
            dma((2,)),
            dma((2,)),
            dma((2, 2, 6)),
            dma((2, 2, 6)),
            dma((2, 2, 3)),
            dma((2, 2, 3)),
            dma((7,)),
            dma((7,)),
            dma((7,)),
            dma((7,)),
            dma((7,)),
            dma((7,)),
        ],
        compiler_params=pltpu.CompilerParams(
            collective_id=0, has_side_effects=True, vmem_limit_bytes=63 * 1024 * 1024
        ),
        name="train_step",
    )(*small, *large)


def per_device(
    latent,
    hint_field,
    from_below,
    cotangent,
    timesteps,
    time_weight,
    enc_proj,
    ctl_proj,
    dec_proj,
    enc_conv_one,
    enc_conv_two,
    ctl_conv_one,
    ctl_conv_two,
    dec_conv_one,
    dec_conv_two,
    dec_shortcut,
    zero_conv,
):
    half_width = C // 2
    frequency = jnp.exp(-math.log(10000.0) * jnp.arange(half_width, dtype=jnp.float32) / half_width)
    angles = timesteps.astype(jnp.float32)[:, None] * frequency[None, :]
    sinusoid = jnp.concatenate([jnp.cos(angles), jnp.sin(angles)], axis=1).astype(jnp.bfloat16)
    def by_row(field):
        return jnp.transpose(field[0], (1, 0, 2))

    def by_tap(kernel):
        return jnp.transpose(kernel, (1, 2, 0, 3)).reshape(9, kernel.shape[0], kernel.shape[3])

    def from_tap(grad):
        return jnp.transpose(grad.reshape(3, 3, 10, C), (2, 0, 1, 3))

    one_grad, two_grad, zero_grad = run_step(
        (
            jnp.broadcast_to(sinusoid, (16, C)),
            by_row(latent),
            by_row(hint_field),
            by_row(from_below),
            by_row(cotangent),
            by_tap(ctl_conv_one),
            by_tap(ctl_conv_two),
            by_tap(dec_conv_one),
            by_tap(dec_conv_two),
            dec_shortcut,
            zero_conv,
        ),
        (time_weight, enc_proj.T, ctl_proj.T, dec_proj.T, by_tap(enc_conv_one), by_tap(enc_conv_two)),
    )
    return (from_tap(one_grad), from_tap(two_grad), zero_grad)


def solution(mesh):
    in_specs = (
        P("dp", None, "rows", None),
        P("dp", None, "rows", None),
        P("dp", None, "rows", None),
        P("dp", None, "rows", None),
        P("dp"),
        P(),
        P(),
        P(),
        P(),
        P(),
        P(),
        P("dp", None, None, None),
        P("dp", None, None, None),
        P("dp", None, None, None),
        P("dp", None, None, None),
        P("dp", None),
        P("dp", None),
    )
    out_specs = (P("dp", None, None, None), P("dp", None, None, None), P("dp", None))
    return jax.shard_map(
        per_device, mesh=mesh, in_specs=in_specs, out_specs=out_specs, check_vma=False
    )
```

```python
import math

import jax
import jax.numpy as jnp
from jax import lax
from jax.experimental import pallas as pl
from jax.experimental.pallas import tpu as pltpu
from jax.sharding import PartitionSpec as P

C = 320
EPSILON = 1e-05
MESH = pl.DeviceIdType.MESH
LANES = 16384
HALF = 4096
BF = jnp.bfloat16
F32 = jnp.float32
ROWS = 16
STEPS = C // ROWS
NT = (((1,), (1,)), ((), ()))
TN = (((0,), (0,)), ((), ()))
EXACT = lax.Precision.HIGHEST
AT_CTL_ONE = 0
AT_CTL_TWO = 2944
AT_ZERO = 5888
AT_DEC_ONE = 6272
AT_SHORT = 12032
AT_DEC_TWO = 12416


def place():
    d = lax.axis_index("dp")
    r = lax.axis_index("rows")
    return (d // 8, (d // 2) % 4, d % 2, r // 4, r % 4)


def device_of(zh, y, c, zl, x):
    return (zh * 8 + y * 2 + c, zl * 4 + x)


def remote(src, dst, send, recv, where):
    return pltpu.make_async_remote_copy(
        src_ref=src, dst_ref=dst, send_sem=send, recv_sem=recv, device_id=where, device_id_type=MESH
    )


def greet(peers):
    barrier = pltpu.get_barrier_semaphore()
    for where in peers:
        pl.semaphore_signal(barrier, inc=1, device_id=where, device_id_type=MESH)
    pl.semaphore_wait(barrier, len(peers))


def lanes_at(start, size):
    return pl.ds(pl.multiple_of(start, 128), size)


def band(i):
    return slice(i * ROWS, i * ROWS + ROWS)


def each(count):
    def run(body):
        for i in range(count):
            body(i)

    return run


def put_columns(col, base_of, i, strips):
    lane = lax.broadcasted_iota(jnp.int32, (ROWS, 128), 1)
    shifted_of = []
    for strip in strips:
        left = jnp.where(lane == 0, 0.0, pltpu.roll(strip, 1, axis=1))
        right = jnp.where(lane == 127, 0.0, pltpu.roll(strip, 127, axis=1))
        shifted_of.append([left.astype(BF), strip.astype(BF), right.astype(BF)])
    for p in range(3):
        for q in range(3):
            start = base_of(3 * p + q) + i * ROWS
            col[start : start + ROWS, 0:128] = shifted_of[p][q]
            col[start : start + ROWS, 128:256] = shifted_of[p + 1][q]


def sig(v):
    return jax.nn.sigmoid(v)


def slope(v):
    s = sig(v)
    return s * (1.0 + v * (1.0 - s))


def dot(a, b):
    return jnp.dot(a, b, preferred_element_type=F32)


def taps_dot(kernel, col):
    total = dot(kernel[0], col[0:C, :])
    for tap in range(1, 9):
        total = total + dot(kernel[tap], col[C * tap : C * tap + C, :])
    return total


def three_parts(value):
    high = value.astype(BF).astype(F32)
    rest = value - high
    middle = rest.astype(BF).astype(F32)
    return [high, middle, rest - middle]


def put_sums(cols, at, i, pairs):
    for k, value in enumerate(pairs):
        cols[band(i), at + k : at + k + 1] = jnp.sum(value, axis=1, keepdims=True)


def step_kernel(
    sinus,
    latent_ref,
    hint_ref,
    under_ref,
    cot_ref,
    shard_ctl_one,
    shard_ctl_two,
    shard_dec_one,
    shard_dec_two,
    shard_short,
    shard_zero,
    time_weight_hbm,
    enc_proj_hbm,
    ctl_proj_hbm,
    dec_proj_hbm,
    enc_one_hbm,
    enc_two_hbm,
    one_out,
    two_out,
    zero_out,
    member,
    ten,
    twenty,
    cols,
    coef,
    halo,
    halo_cot,
    inner,
    inner_halo,
    edge,
    col_t,
    col_a,
    col_b,
    col_d,
    col_g,
    back_dec_two,
    back_dec_one,
    back_ctl_two,
    zero_t,
    short_t,
    enc_raw,
    ctl_raw,
    ctl_out,
    skip,
    skip_halo,
    dec_raw,
    dec_halo,
    dec_edge,
    up_grad,
    sfg,
    sfg_edge,
    sfg_halo,
    keep_n,
    keep_skip,
    keep_dec,
    mixed,
    wide,
    wide_two,
    note,
    note_in,
    note_send,
    note_recv,
    halo_send,
    halo_recv,
    time_weight,
    projections,
    stage,
    src,
    enc_one,
    enc_two,
    enc_sem,
    weights,
    parts,
    column,
    gath,
    own_sem,
    ph1_send,
    ph1_recv,
    ph2_send,
    ph2_recv,
    ph3_send,
    ph3_recv,
    ph4_send,
    ph4_recv,
    ph5_send,
    ph5_recv,
    grads,
    swap,
    half,
    far,
    near,
    passing,
    near_in,
    deep,
    deep_in,
    last,
    fan,
    pool,
    tight,
    opened,
    out_sem,
    rs1_send,
    rs1_recv,
    rs2_send,
    rs2_recv,
    rs3_send,
    rs3_recv,
    rs4_send,
    rs4_recv,
    rs6_send,
    rs6_recv,
    rs7_send,
    rs7_recv,
):
    d = lax.axis_index("dp")
    r = lax.axis_index("rows")
    zh, y, c, zl, x = place()
    slot = y * 2 + c
    peers = [(d, (r + k) % 8) for k in range(1, 8)]
    plane_peers = []
    for k in range(1, 8):
        s = (slot + k) % 8
        plane_peers.append(device_of(zh, s // 2, s % 2, zl, x))
    z_peers = [device_of((zh + k) % 4, y, c, zl, x) for k in range(1, 4)]
    x_peers = [device_of(zh, y, c, zl, (x + k) % 4) for k in range(1, 4)]
    y_peers = [device_of(zh, (y + k) % 4, c, zl, x) for k in range(1, 4)]
    partner = device_of(zh, y, 1 - c, zl, x)
    other_z = device_of(zh, y, c, 1 - zl, x)
    z_all = [device_of((zh + k // 2) % 4, y, c, (zl + k) % 2, x) for k in range(1, 8)]
    everyone = peers + plane_peers + z_all[1:]
    barrier = pltpu.get_barrier_semaphore()
    for where in everyone:
        pl.semaphore_signal(barrier, inc=1, device_id=where, device_id_type=MESH)
    loads = []
    for k, (source, target) in enumerate(
        (
            (time_weight_hbm, time_weight),
            (enc_proj_hbm, projections.at[0]),
            (ctl_proj_hbm, projections.at[1]),
            (dec_proj_hbm, projections.at[2]),
            (enc_one_hbm, enc_one),
            (enc_two_hbm, enc_two),
        )
    ):
        loads.append(pltpu.make_async_copy(source, target, enc_sem.at[k]))
        loads[-1].start()
    load_one, load_two = loads[4:]

    stage[...] = jnp.zeros((16, LANES), BF)
    for kernel, start, count, width in (
        (shard_ctl_one, AT_CTL_ONE, 9, C),
        (shard_ctl_two, AT_CTL_TWO, 9, C),
        (shard_dec_one, AT_DEC_ONE, 9, 2 * C),
        (shard_dec_two, AT_DEC_TWO, 9, C),
    ):
        for tap in range(count):
            stage[0:10, start + width * tap : start + width * tap + width] = kernel[:, tap // 3, tap % 3, :]
    stage[0:10, AT_ZERO : AT_ZERO + C] = shard_zero[...]
    stage[0:10, AT_SHORT : AT_SHORT + C] = shard_short[:, C : 2 * C]
    for s in range(8):
        for g in range(4):
            tile = (x * 2 + s % 2) * 4 + s // 2 if g % 2 else s * 4 + x
            src[s, :, 128 * g : 128 * g + 128] = stage[:, lanes_at(g * 4096 + tile * 128, 128)]

    lane = lax.broadcasted_iota(jnp.int32, (C, 128), 1)
    channel = lax.broadcasted_iota(jnp.int32, (C, 128), 0)
    in_ten = (channel >= 10 * lane) & (channel < 10 * lane + 10)
    other = lane - 32
    in_twenty = (channel >= 20 * other) & (channel < 20 * other + 20)
    one_ten = jnp.where(in_ten, 1.0, 0.0)
    one_twenty = jnp.where(in_twenty, 1.0, 0.0)
    member[...] = (one_ten + one_twenty).astype(BF)
    for k in range(3):
        ten[:, 128 * k : 128 * k + 128] = one_ten.astype(BF)
        twenty[:, 128 * k : 128 * k + 128] = one_twenty.astype(BF)
    cols[...] = jnp.zeros((C, 128), F32)

    @each(STEPS)
    def _(i):
        sums = [0.0] * 6
        for h in range(2):
            latent = latent_ref[h, band(i), :].astype(F32)
            ctl_in = (latent + hint_ref[h, band(i), :].astype(F32)).astype(BF).astype(F32)
            under = under_ref[h, band(i), :].astype(F32)
            for k, value in enumerate((latent, latent * latent, ctl_in, ctl_in * ctl_in, under, under * under)):
                sums[k] = sums[k] + value
        put_sums(cols, 0, i, sums)

    pl.semaphore_wait(barrier, len(everyone))
    before = (d, (r + 7) % 8)
    after = (d, (r + 1) % 8)
    waiting = []

    def send_rows(event, top, bottom, above, below):
        first = remote(top, below, halo_send.at[event, 0], halo_recv.at[event, 0], before)
        second = remote(bottom, above, halo_send.at[event, 1], halo_recv.at[event, 1], after)
        first.start()
        second.start()
        waiting.extend([first, second])
        return (first, second)

    def arrive(pair):
        pair[0].wait_recv()
        pair[1].wait_recv()

    raw = send_rows(0, latent_ref.at[0], latent_ref.at[1], halo.at[0, 0], halo.at[1, 0])
    raw_hint = send_rows(8, hint_ref.at[0], hint_ref.at[1], halo.at[0, 1], halo.at[1, 1])
    first = []
    for k in range(7):
        s = (slot + k + 1) % 8
        first.append(remote(src.at[s], parts.at[slot], ph1_send.at[k], ph1_recv.at[k], plane_peers[k]))
        first[-1].start()
    waiting.extend(first)
    mine = pltpu.make_async_copy(src.at[slot], parts.at[slot], own_sem.at[4])
    mine.start()

    second = {}
    third = {}
    fourth = {}
    fifth = {}
    held = {}

    def gather_z():
        mine.wait()
        for copy in first:
            copy.wait_recv()
        for s in range(8):
            column[10 * s : 10 * s + 10, :] = parts[s, 0:10, :].astype(F32)
        home = pl.multiple_of(zh * 80, 16)
        gath[pl.ds(home, 80), :] = column[...].astype(BF)
        for g in range(4):
            block = gath.at[pl.ds(home, 80), 128 * g : 128 * g + 128]
            second[g] = []
            for k in (0, 2, 1):
                second[g].append(remote(block, block, ph2_send.at[g, k], ph2_recv.at[g, k], z_peers[k]))
                second[g][-1].start()
            waiting.extend(second[g])

    def gather_short(g):
        for copy in second[g]:
            copy.wait_recv()
        block = gath.at[:, 128 * g : 128 * g + 128]
        tile = (x * 2 + c) * 4 + y if g % 2 else slot * 4 + x
        short_peers = y_peers if g % 2 else x_peers
        spot = weights.at[:, lanes_at(g * 4096 + tile * 128, 128)]
        third[g] = []
        for k in (0, 2, 1):
            third[g].append(remote(block, spot, ph3_send.at[g, k], ph3_recv.at[g, k], short_peers[k]))
            third[g][-1].start()
        waiting.extend(third[g])
        held[g] = pltpu.make_async_copy(block, spot, own_sem.at[g])
        held[g].start()

    def column_of(g, steps, at, size):
        where = x if g % 2 else y
        return weights.at[:, lanes_at(g * 4096 + ((where + 4 + steps) % 4 * 2 + c) * 512 + at, size)]

    def to_partner(g, k, steps):
        block = column_of(g, steps, 0, 512)
        copy = remote(block, block, ph5_send.at[g, k], ph5_recv.at[g, k], partner)
        copy.start()
        fifth[g].append(copy)
        waiting.append(copy)

    def long_peers(g):
        return x_peers if g % 2 else y_peers

    def gather_long(g):
        held[g].wait()
        for copy in third[g]:
            copy.wait_recv()
        block = column_of(g, 0, 0, 512)
        fourth[g] = [
            remote(block, block, ph4_send.at[g, 0], ph4_recv.at[g, 0], long_peers(g)[0]),
            remote(block, block, ph4_send.at[g, 1], ph4_recv.at[g, 1], long_peers(g)[2]),
        ]
        for copy in fourth[g]:
            copy.start()
        waiting.extend(fourth[g])
        fifth[g] = []
        to_partner(g, 0, 0)

    def gather_relay(g):
        fourth[g][0].wait_recv()
        block = column_of(g, -1, 0, 256)
        up = remote(block, block, ph4_send.at[g, 2], ph4_recv.at[g, 2], long_peers(g)[0])
        up.start()
        fourth[g][1].wait_recv()
        block = column_of(g, 1, 256, 256)
        down = remote(block, block, ph4_send.at[g, 3], ph4_recv.at[g, 3], long_peers(g)[2])
        down.start()
        fourth[g].extend([up, down])
        waiting.extend([up, down])
        to_partner(g, 1, -1)
        to_partner(g, 2, 1)

    def gather_finish(g):
        fourth[g][2].wait_recv()
        fourth[g][3].wait_recv()
        to_partner(g, 3, 2)

    def gather_done(g):
        for copy in fifth[g]:
            copy.wait_recv()


    def share(turn):
        turned = cols[:, 0:8].T
        sums = dot(jnp.concatenate(three_parts(turned), axis=0).astype(BF), member[...])
        note[turn] = sums[0:8] + sums[8:16] + sums[16:24]
        copies = []
        for k in range(1, 8):
            copies.append(
                remote(
                    note.at[turn],
                    note_in.at[turn, k - 1],
                    note_send.at[turn, k - 1],
                    note_recv.at[turn, k - 1],
                    peers[k - 1],
                )
            )
            copies[-1].start()
        waiting.extend(copies)
        return copies

    def collect(turn, copies):
        for copy in copies:
            copy.wait_recv()
        total = note[turn]
        for k in range(7):
            total = total + note_in[turn, k]
        return total

    which = lax.broadcasted_iota(jnp.int32, (8, 128), 1)
    per_group = jnp.where(which < 32, 1.0 / (10 * 2048), 1.0 / (20 * 2048))

    def spread(table, at, rows):
        wide_rows = [
            jnp.broadcast_to(jnp.concatenate(three_parts(row), axis=1), (128, 384)).astype(BF) for row in rows
        ]
        columns = lax.dot_general(
            table[...], jnp.concatenate(wide_rows, axis=0), NT, preferred_element_type=F32
        )
        for k in range(len(rows)):
            coef[at + k] = columns[:, 128 * k : 128 * k + 128]

    def raw_sums(raw_ref, term_at, i):
        term = coef[term_at, band(i), :]
        one = raw_ref[band(i), 0:128] + term
        two = raw_ref[band(i), 128:256] + term
        put_sums(cols, 0, i, [one + two, one * one + two * two])

    def norm_rows(total, k):
        mean = total[k : k + 1] * per_group[0:1]
        square = total[k + 1 : k + 2] * per_group[0:1]
        return [mean, lax.rsqrt(square - mean * mean + EPSILON)]

    def mean_rows(total, k):
        return [total[k : k + 1] * per_group[0:1], total[k + 1 : k + 2] * per_group[0:1]]

    has_up = r > 0
    has_down = r < 7

    def masked(strips):
        return [
            jnp.where(has_up, strips[0], 0.0),
            strips[1],
            strips[2],
            jnp.where(has_down, strips[3], 0.0),
        ]

    first_note = share(0)
    for load in loads[0:4]:
        load.wait()
    embed = dot(sinus[...], time_weight[...])
    embed = (embed * sig(embed)).astype(BF)
    for k in range(3):
        term = lax.dot_general(projections[k], embed, NT, preferred_element_type=F32)
        coef[20 + k] = jnp.broadcast_to(term[:, 0:1], (C, 128))
    for target in (back_dec_two, back_dec_one, back_ctl_two):
        for tap in range(9):
            target[:, 384 * tap + 320 : 384 * tap + 384] = jnp.zeros((C, 64), BF)
    for tap in range(9):
        col_g[384 * tap + 320 : 384 * tap + 384, :] = jnp.zeros((64, 256), BF)
    grads[0, :, 2816:HALF] = jnp.zeros((C, HALF - 2816), BF)
    grads[0, 160:C, :] = jnp.zeros((160, HALF), BF)
    grads[1, :, 2816:HALF] = jnp.zeros((C, HALF - 2816), BF)
    grads[1, 160:C, :] = jnp.zeros((160, HALF), BF)

    def turn(target, start, stride):
        for tap in range(9):
            block = weights[:, start + stride * tap : start + stride * tap + 320].astype(F32)
            target[:, 384 * (8 - tap) : 384 * (8 - tap) + 320] = block.T.astype(BF)

    def turn_square(target, start):
        target[...] = weights[:, start : start + 320].astype(F32).T.astype(BF)

    gather_z()
    late = send_rows(1, under_ref.at[0], under_ref.at[1], halo.at[0, 2], halo.at[1, 2])
    late_cot = send_rows(2, cot_ref, cot_ref, halo_cot.at[0], halo_cot.at[1])
    total = collect(0, first_note)
    spread(ten, 0, norm_rows(total, 0) + norm_rows(total, 2))
    spread(twenty, 4, norm_rows(total, 4))
    arrive(raw)
    arrive(raw_hint)

    def plain(tap):
        return 320 * tap

    def first_act(source_of, at, col, base_of):
        @each(STEPS)
        def _(i):
            mean = coef[at, band(i), :]
            inv = coef[at + 1, band(i), :]
            strips = []
            for strip in source_of(i):
                normed = (strip - mean) * inv
                strips.append(normed * sig(normed))
            put_columns(col, base_of, i, masked(strips))

    def latent_of(i):
        return [
            halo[0, 0, band(i), :].astype(F32),
            latent_ref[0, band(i), :].astype(F32),
            latent_ref[1, band(i), :].astype(F32),
            halo[1, 0, band(i), :].astype(F32),
        ]

    def ctl_in_of(i):
        hint = [
            halo[0, 1, band(i), :].astype(F32),
            hint_ref[0, band(i), :].astype(F32),
            hint_ref[1, band(i), :].astype(F32),
            halo[1, 1, band(i), :].astype(F32),
        ]
        return [(a + b).astype(BF).astype(F32) for a, b in zip(latent_of(i), hint)]

    first_act(latent_of, 0, col_t, plain)
    load_one.wait()
    enc_raw[...] = taps_dot(enc_one, col_t)
    edge[0] = enc_raw[:, 0:128].astype(BF)
    edge[1] = enc_raw[:, 128:256].astype(BF)
    enc_rows = send_rows(3, edge.at[0], edge.at[1], inner_halo.at[0], inner_halo.at[1])

    @each(STEPS)
    def _(i):
        raw_sums(enc_raw, 20, i)

    second_note = share(1)
    gather_short(0)
    first_act(ctl_in_of, 2, col_a, plain)

    def under_of(i):
        return [
            halo[0, 2, band(i), :].astype(F32),
            under_ref[0, band(i), :].astype(F32),
            under_ref[1, band(i), :].astype(F32),
            halo[1, 2, band(i), :].astype(F32),
        ]

    def joined_low(tap):
        return 640 * tap

    def joined_high(tap):
        return 640 * tap + 320

    def spaced(tap):
        return 384 * tap

    arrive(late)
    first_act(under_of, 4, col_d, joined_low)

    gather_short(1)
    gather_long(0)
    gather_short(2)
    total = collect(1, second_note)
    spread(ten, 6, norm_rows(total, 0))

    def second_act(raw_ref, at_halo, term_at, at, col, keep):
        @each(STEPS)
        def _(i):
            mean = coef[at, band(i), :]
            inv = coef[at + 1, band(i), :]
            own = raw_ref[band(i), :]
            term = coef[20 + term_at, band(i), :]
            strips = []
            for strip in (
                inner_halo[at_halo, band(i), :].astype(F32),
                own[:, 0:128],
                own[:, 128:256],
                inner_halo[at_halo + 1, band(i), :].astype(F32),
            ):
                strips.append((strip + term - mean) * inv)
            if keep is not None:
                keep[band(i), 0:128] = strips[1]
                keep[band(i), 128:256] = strips[2]
            put_columns(col, plain, i, masked([v * sig(v) for v in strips]))

    arrive(enc_rows)
    second_act(enc_raw, 0, 0, 6, col_t, None)
    load_two.wait()
    enc_raw[...] = taps_dot(enc_two, col_t)
    gather_long(1)
    gather_relay(0)
    gather_short(3)
    gather_long(2)
    gather_finish(0)
    gather_done(0)
    ctl_raw[...] = dot(weights[:, AT_CTL_ONE : AT_CTL_ONE + 2880], col_a[...])
    edge[2] = ctl_raw[:, 0:128].astype(BF)
    edge[3] = ctl_raw[:, 128:256].astype(BF)
    ctl_rows = send_rows(4, edge.at[2], edge.at[3], inner_halo.at[2], inner_halo.at[3])

    @each(STEPS)
    def _(i):
        raw_sums(ctl_raw, 21, i)

    ctl_note = share(2)
    gather_relay(1)
    total = collect(2, ctl_note)
    spread(ten, 8, norm_rows(total, 0))
    arrive(ctl_rows)
    second_act(ctl_raw, 2, 1, 8, col_b, keep_n)
    gather_long(3)
    gather_finish(1)
    gather_done(1)
    inner[...] = dot(weights[:, AT_CTL_TWO : AT_CTL_TWO + 2880], col_b[...])

    @each(STEPS)
    def _(i):
        own = ctl_in_of(i)
        ctl_out[band(i), 0:128] = (own[1] + inner[band(i), 0:128]).astype(BF)
        ctl_out[band(i), 128:256] = (own[2] + inner[band(i), 128:256]).astype(BF)

    inner[...] = dot(weights[:, AT_ZERO : AT_ZERO + 320], ctl_out[...])

    @each(STEPS)
    def _(i):
        sums = [0.0, 0.0]
        for h in range(2):
            lanes = slice(128 * h, 128 * h + 128)
            latent = latent_ref[h, band(i), :].astype(F32)
            enc_out = (latent + enc_raw[band(i), lanes]).astype(BF).astype(F32)
            joined = (enc_out + inner[band(i), lanes]).astype(BF)
            skip[h, band(i), :] = joined
            value = joined.astype(F32)
            sums = [sums[0] + value, sums[1] + value * value]
        put_sums(cols, 0, i, sums)

    skip_rows = send_rows(5, skip.at[0], skip.at[1], skip_halo.at[0], skip_halo.at[1])
    third_note = share(3)
    turn(back_ctl_two, AT_CTL_TWO, 320)
    turn_square(zero_t, AT_ZERO)
    gather_relay(2)
    gather_relay(3)

    total = collect(3, third_note)
    spread(twenty, 10, norm_rows(total, 0))
    arrive(skip_rows)

    @each(STEPS)
    def _(i):
        mean = coef[10, band(i), :]
        inv = coef[11, band(i), :]
        strips = []
        for k, strip in enumerate(
            (skip_halo[0, band(i), :], skip[0, band(i), :], skip[1, band(i), :], skip_halo[1, band(i), :])
        ):
            normed = (strip.astype(F32) - mean) * inv
            keep_skip[band(i), 128 * k : 128 * k + 128] = normed
            strips.append(normed * sig(normed))
        put_columns(col_d, joined_high, i, masked(strips))

    gather_finish(2)
    gather_done(2)
    dec_raw[...] = dot(weights[:, AT_DEC_ONE : AT_DEC_ONE + 5760], col_d[...])
    dec_edge[0] = dec_raw[:, 0:128].astype(BF)
    dec_edge[1] = dec_raw[:, 128:256].astype(BF)
    dec_rows = send_rows(6, dec_edge.at[0], dec_edge.at[1], dec_halo.at[0], dec_halo.at[1])

    @each(STEPS)
    def _(i):
        raw_sums(dec_raw, 22, i)

    fourth_note = share(4)
    turn(back_dec_one, AT_DEC_ONE + 320, 640)
    gather_finish(3)
    arrive(late_cot)
    scale = 2.0**-8

    def cot_of(i):
        far_rows = [jnp.where(has_up, halo_cot[0, h, band(i), :].astype(F32), 0.0) for h in range(2)]
        own = [cot_ref[h, band(i), :].astype(F32) for h in range(2)]
        near_rows = [jnp.where(has_down, halo_cot[1, h, band(i), :].astype(F32), 0.0) for h in range(2)]
        return [strip * scale for strip in far_rows + own + near_rows]

    gather_done(3)
    turn(back_dec_two, AT_DEC_TWO, 320)
    turn_square(short_t, AT_SHORT)
    for part in range(2):

        @each(STEPS)
        def _(i):
            strips = cot_of(i)[2 * part : 2 * part + 4]
            put_columns(col_g, spaced, i, strips)

        up_grad[:, 256 * part : 256 * part + 256] = dot(back_dec_two[...], col_g[...])

    @each(STEPS)
    def _(i):
        for k, strip in enumerate(cot_of(i)[1:5]):
            wide[band(i), 128 * k : 128 * k + 128] = strip.astype(BF)

    mixed[...] = dot(short_t[...], wide[...])

    total = collect(4, fourth_note)
    spread(ten, 12, norm_rows(total, 0))

    def keep_dec_rows(i, strip, k):
        mean = coef[12, band(i), :]
        inv = coef[13, band(i), :]
        term = coef[22, band(i), :]
        normed = (strip + term - mean) * inv
        keep_dec[band(i), 128 * k : 128 * k + 128] = normed
        upstream = up_grad[band(i), 128 * k : 128 * k + 128] * slope(normed)
        up_grad[band(i), 128 * k : 128 * k + 128] = upstream
        return (normed, upstream)

    @each(STEPS)
    def _(i):
        one_n, one_g = keep_dec_rows(i, dec_raw[band(i), 0:128], 1)
        two_n, two_g = keep_dec_rows(i, dec_raw[band(i), 128:256], 2)
        put_sums(cols, 0, i, [one_g + two_g, one_g * one_n + two_g * two_n])

    fifth_note = share(5)
    arrive(dec_rows)

    @each(STEPS)
    def _(i):
        keep_dec_rows(i, dec_halo[0, band(i), :].astype(F32), 0)
        keep_dec_rows(i, dec_halo[1, band(i), :].astype(F32), 3)

    total = collect(5, fifth_note)
    spread(ten, 14, mean_rows(total, 0))

    @each(STEPS)
    def _(i):
        inv = coef[13, band(i), :]
        mean = coef[14, band(i), :]
        cross = coef[15, band(i), :]
        strips = []
        for k in range(4):
            lanes = slice(128 * k, 128 * k + 128)
            strips.append(inv * (up_grad[band(i), lanes] - mean - keep_dec[band(i), lanes] * cross))
        put_columns(col_g, spaced, i, masked(strips))

    sfg[...] = dot(back_dec_one[...], col_g[...])
    sfg_edge[0] = sfg[:, 0:128].astype(BF)
    sfg_edge[1] = sfg[:, 128:256].astype(BF)
    sfg_rows = send_rows(7, sfg_edge.at[0], sfg_edge.at[1], sfg_halo.at[0], sfg_halo.at[1])

    @each(STEPS)
    def _(i):
        normed = keep_skip[band(i), 128:384]
        value = sfg[band(i), :] * slope(normed)
        up_grad[band(i), 128:384] = value
        put_sums(cols, 0, i, [value, value * normed])

    sixth_note = share(6)
    arrive(sfg_rows)

    @each(STEPS)
    def _(i):
        for at, lanes in ((0, slice(0, 128)), (1, slice(384, 512))):
            up_grad[band(i), lanes] = sfg_halo[at, band(i), :].astype(F32) * slope(keep_skip[band(i), lanes])

    total = collect(6, sixth_note)
    spread(twenty, 16, mean_rows(total, 0))

    @each(STEPS)
    def _(i):
        inv = coef[11, band(i), :]
        mean = coef[16, band(i), :]
        cross = coef[17, band(i), :]
        for k in range(4):
            lanes = slice(128 * k, 128 * k + 128)
            value = inv * (up_grad[band(i), lanes] - mean - keep_skip[band(i), lanes] * cross) + mixed[band(i), lanes]
            wide[band(i), lanes] = value.astype(BF)

    up_grad[...] = dot(zero_t[...], wide[...])

    @each(STEPS)
    def _(i):
        strips = []
        for k in range(4):
            strips.append(up_grad[band(i), 128 * k : 128 * k + 128].astype(BF).astype(F32))
        wide_two[band(i), 0:128] = strips[1].astype(BF)
        wide_two[band(i), 128:256] = strips[2].astype(BF)
        put_columns(col_g, spaced, i, masked(strips))

    def store_grads(k, value, at):
        count = value.shape[1]
        grads[k, 0:160, at : at + count] = value[0:160].astype(BF)
        for start in range(0, count, 128):
            tile = (at + start) // 128
            spot = (tile // 16 * 16 + tile % 4 * 4 + tile // 4 % 4) * 128
            size = min(128, count - start)
            grads[k, 160:C, spot : spot + size] = value[160:C, start : start + size].astype(BF)

    swaps = {}
    pairs = {}
    fours = {}

    def reduce_core(k):
        swaps[k] = remote(
            grads.at[k, :, lanes_at((1 - c) * 2048, 2048)], swap.at[k], rs1_send.at[k], rs1_recv.at[k], partner
        )
        swaps[k].start()
        waiting.append(swaps[k])

    def reduce_far(k):
        swaps[k].wait_recv()

        @each(STEPS)
        def _(i):
            total = grads[k, band(i), lanes_at(c * 2048, 2048)].astype(F32) + swap[k, band(i), :].astype(F32)
            half[k, band(i), :] = total.astype(BF)

        pairs[k] = []
        for axis, (where, ring_peers) in enumerate(((y, y_peers), (x, x_peers))):
            rows = slice(160 * axis, 160 * axis + 160)
            for j, (steps, part, target) in enumerate(((1, 256, 0), (2, 0, 0), (3, 0, 2), (2, 256, 2))):
                block = half.at[k, rows, lanes_at((where + steps) % 4 * 512 + part, 256)]
                pairs[k].append(
                    remote(
                        block,
                        far.at[k, axis, j],
                        rs2_send.at[k, axis, j],
                        rs2_recv.at[k, axis, j],
                        ring_peers[target],
                    )
                )
                pairs[k][-1].start()
        waiting.extend(pairs[k])

    relays = {}

    def reduce_relay(k):
        relays[k] = []
        for axis, (where, ring_peers) in enumerate(((y, y_peers), (x, x_peers))):
            rows = slice(160 * axis, 160 * axis + 160)
            for j, (steps, part, target, source) in enumerate(((1, 0, 0, 1), (3, 256, 2, 3))):
                pairs[k][4 * axis + source].wait_recv()
                own = half[k, rows, lanes_at((where + steps) % 4 * 512 + part, 256)].astype(F32)
                passing[k, axis, j] = (own + far[k, axis, source].astype(F32)).astype(BF)
                relays[k].append(
                    remote(
                        passing.at[k, axis, j],
                        far.at[k, axis, 4 + j],
                        rs2_send.at[k, axis, 4 + j],
                        rs2_recv.at[k, axis, 4 + j],
                        ring_peers[target],
                    )
                )
                relays[k][-1].start()
        waiting.extend(relays[k])

    def reduce_near(k):
        for axis in range(2):
            pairs[k][4 * axis].wait_recv()
            pairs[k][4 * axis + 2].wait_recv()
        for copy in relays[k]:
            copy.wait_recv()
        for axis, where in ((0, y), (1, x)):
            rows = slice(160 * axis, 160 * axis + 160)
            for part, direct, relayed in ((0, 2, 4), (256, 0, 5)):
                total = half[k, rows, lanes_at(where * 512 + part, 256)].astype(F32)
                total = total + far[k, axis, direct].astype(F32) + far[k, axis, relayed].astype(F32)
                near[k, axis, :, part : part + 256] = total.astype(BF)

        fours[k] = []
        for j in (1, 3, 2):
            xa = (x + j) % 4
            yb = (y + j) % 4
            fours[k].append(
                remote(
                    near.at[k, 0, :, lanes_at(xa * 128, 128)],
                    near_in.at[k, 0, j - 1],
                    rs3_send.at[k, 0, j - 1],
                    rs3_recv.at[k, 0, j - 1],
                    x_peers[j - 1],
                )
            )
            fours[k].append(
                remote(
                    near.at[k, 1, :, lanes_at(yb * 128, 128)],
                    near_in.at[k, 1, j - 1],
                    rs3_send.at[k, 1, j - 1],
                    rs3_recv.at[k, 1, j - 1],
                    y_peers[j - 1],
                )
            )
        for copy in fours[k]:
            copy.start()
        waiting.extend(fours[k])

    def reduce_deep(k):
        for copy in fours[k]:
            copy.wait_recv()
        for which, where in ((0, x), (1, y)):
            total = near[k, which, :, lanes_at(where * 128, 128)].astype(F32)
            for j in range(3):
                total = total + near_in[k, which, j].astype(F32)
            deep[160 * which : 160 * which + 160, 128 * k : 128 * k + 128] = total.astype(BF)

    two_value = lax.dot_general(wide_two[...], col_b[...], NT, preferred_element_type=F32)
    store_grads(0, two_value, 0)
    zero_value = lax.dot_general(wide[:, 128:384], ctl_out[...], NT, preferred_element_type=F32)
    store_grads(0, zero_value, 2944)
    reduce_core(0)
    sfg[...] = dot(back_ctl_two[...], col_g[...])

    @each(STEPS)
    def _(i):
        normed = keep_n[band(i), :]
        value = sfg[band(i), :] * slope(normed)
        sfg[band(i), :] = value
        put_sums(cols, 0, i, [value, value * normed])

    seventh_note = share(7)
    reduce_far(0)
    total = collect(7, seventh_note)
    spread(ten, 18, mean_rows(total, 0))

    @each(STEPS)
    def _(i):
        inv = coef[9, band(i), :]
        mean = coef[18, band(i), :]
        cross = coef[19, band(i), :]
        for lanes in (slice(0, 128), slice(128, 256)):
            value = inv * (sfg[band(i), lanes] - mean - keep_n[band(i), lanes] * cross)
            wide_two[band(i), lanes] = value.astype(BF)

    one_value = lax.dot_general(wide_two[...], col_a[...], NT, preferred_element_type=F32)
    store_grads(1, one_value, 0)
    reduce_core(1)
    reduce_relay(0)
    reduce_far(1)
    reduce_near(0)
    reduce_relay(1)
    reduce_deep(0)
    reduce_near(1)
    reduce_deep(1)
    ring = []
    for k in range(1, 8):
        zt = (zh + k // 2) % 4
        lt = (zl + k) % 2
        ring.append(
            remote(
                deep.at[pl.ds(pl.multiple_of(zt * 80, 16), 80), lanes_at(lt * 128, 128)],
                deep_in.at[k - 1],
                rs4_send.at[k - 1],
                rs4_recv.at[k - 1],
                z_all[k - 1],
            )
        )
        ring[-1].start()
    total = deep[pl.ds(pl.multiple_of(zh * 80, 16), 80), lanes_at(zl * 128, 128)].astype(F32)
    for k in range(7):
        ring[k].wait_recv()
        total = total + deep_in[k].astype(F32)
    last[...] = total
    for s in range(8):
        spaced_rows = jnp.concatenate([last[10 * s : 10 * s + 10, :], jnp.zeros((6, 128), F32)], axis=0)
        fan[s] = spaced_rows.astype(BF)
    sixth = []
    for k in range(7):
        s = (slot + k + 1) % 8
        sixth.append(remote(fan.at[s], pool.at[slot], rs6_send.at[k], rs6_recv.at[k], plane_peers[k]))
        sixth[-1].start()
    mine = pltpu.make_async_copy(fan.at[slot], pool.at[slot], out_sem.at[0])
    mine.start()
    mine.wait()
    for copy in sixth:
        copy.wait_recv()
    for s in range(8):
        last[10 * s : 10 * s + 10, :] = pool[s, 0:10, :].astype(F32)
    tight[r] = last[...].astype(BF)
    seventh = []
    for k in range(1, 8):
        seventh.append(
            remote(tight.at[r], tight.at[r], rs7_send.at[k - 1], rs7_recv.at[k - 1], peers[k - 1])
        )
        seventh[-1].start()
    for copy in seventh:
        copy.wait_recv()
    opened[...] = tight[...].astype(F32)
    for which, target, count in ((0, two_out, 23), (1, one_out, 23), (0, None, 26)):
        for tile in range(23 if target is None else 0, count):
            core, row_at, column_at = tile // 16, tile // 4 % 4, tile % 4
            at = 10 * (row_at * 2 + core)
            value = opened[which * 4 + column_at, at : at + 10, :]
            if target is None:
                size = min(128, C - (tile - 23) * 128)
                zero_out[:, (tile - 23) * 128 : (tile - 23) * 128 + size] = value[:, 0:size]
                continue
            at = tile * 128
            while at < min(tile * 128 + 128, 2880):
                tap, offset = divmod(at, C)
                size = min(C - offset, tile * 128 + 128 - at)
                target[tap, :, offset : offset + size] = value[:, at - tile * 128 : at - tile * 128 + size]
                at += size
    for copy in waiting + ring + sixth + seventh:
        copy.wait_send()


def run_step(small, large):
    dma = pltpu.SemaphoreType.DMA
    whole = pl.BlockSpec(memory_space=pltpu.VMEM)
    far_off = pl.BlockSpec(memory_space=pl.ANY)
    return pl.pallas_call(
        step_kernel,
        out_shape=(
            jax.ShapeDtypeStruct((9, 10, C), F32),
            jax.ShapeDtypeStruct((9, 10, C), F32),
            jax.ShapeDtypeStruct((10, C), F32),
        ),
        in_specs=[whole] * len(small) + [far_off] * len(large),
        out_specs=(whole, whole, whole),
        scratch_shapes=[
            pltpu.VMEM((C, 128), BF),
            pltpu.VMEM((C, 384), BF),
            pltpu.VMEM((C, 384), BF),
            pltpu.VMEM((C, 128), F32),
            pltpu.VMEM((23, C, 128), F32),
            pltpu.VMEM((2, 3, C, 128), BF),
            pltpu.VMEM((2, 2, C, 128), BF),
            pltpu.VMEM((C, 256), F32),
            pltpu.VMEM((4, C, 128), BF),
            pltpu.VMEM((4, C, 128), BF),
            pltpu.VMEM((2880, 256), BF),
            pltpu.VMEM((2880, 256), BF),
            pltpu.VMEM((2880, 256), BF),
            pltpu.VMEM((5760, 256), BF),
            pltpu.VMEM((3456, 256), BF),
            pltpu.VMEM((C, 3456), BF),
            pltpu.VMEM((C, 3456), BF),
            pltpu.VMEM((C, 3456), BF),
            pltpu.VMEM((C, C), BF),
            pltpu.VMEM((C, C), BF),
            pltpu.VMEM((C, 256), F32),
            pltpu.VMEM((C, 256), F32),
            pltpu.VMEM((C, 256), BF),
            pltpu.VMEM((2, C, 128), BF),
            pltpu.VMEM((2, C, 128), BF),
            pltpu.VMEM((C, 256), F32),
            pltpu.VMEM((2, C, 128), BF),
            pltpu.VMEM((2, C, 128), BF),
            pltpu.VMEM((C, 512), F32),
            pltpu.VMEM((C, 256), F32),
            pltpu.VMEM((2, C, 128), BF),
            pltpu.VMEM((2, C, 128), BF),
            pltpu.VMEM((C, 256), F32),
            pltpu.VMEM((C, 512), F32),
            pltpu.VMEM((C, 512), F32),
            pltpu.VMEM((C, 512), F32),
            pltpu.VMEM((C, 512), BF),
            pltpu.VMEM((C, 256), BF),
            pltpu.VMEM((8, 8, 128), F32),
            pltpu.VMEM((8, 7, 8, 128), F32),
            dma((8, 7)),
            dma((8, 7)),
            dma((9, 2)),
            dma((9, 2)),
            pltpu.VMEM((C, 1280), BF),
            pltpu.VMEM((3, C, 1280), BF),
            pltpu.VMEM((16, LANES), BF),
            pltpu.VMEM((8, 16, 512), BF),
            pltpu.VMEM((9, C, C), BF),
            pltpu.VMEM((9, C, C), BF),
            dma((6,)),
            pltpu.VMEM((C, LANES), BF),
            pltpu.VMEM((8, 16, 512), BF),
            pltpu.VMEM((80, 512), F32),
            pltpu.VMEM((C, 512), BF),
            dma((5,)),
            dma((7,)),
            dma((7,)),
            dma((4, 3)),
            dma((4, 3)),
            dma((4, 3)),
            dma((4, 3)),
            dma((4, 4)),
            dma((4, 4)),
            dma((4, 4)),
            dma((4, 4)),
            pltpu.VMEM((2, C, HALF), BF),
            pltpu.VMEM((2, C, 2048), BF),
            pltpu.VMEM((2, C, 2048), BF),
            pltpu.VMEM((2, 2, 6, 160, 256), BF),
            pltpu.VMEM((2, 2, 160, 512), BF),
            pltpu.VMEM((2, 2, 2, 160, 256), BF),
            pltpu.VMEM((2, 2, 3, 160, 128), BF),
            pltpu.VMEM((C, 256), BF),
            pltpu.VMEM((7, 80, 128), BF),
            pltpu.VMEM((80, 128), F32),
            pltpu.VMEM((8, 16, 128), BF),
            pltpu.VMEM((8, 16, 128), BF),
            pltpu.VMEM((8, 80, 128), BF),
            pltpu.VMEM((8, 80, 128), F32),
            dma((1,)),
            dma((2,)),
            dma((2,)),
            dma((2, 2, 6)),
            dma((2, 2, 6)),
            dma((2, 2, 3)),
            dma((2, 2, 3)),
            dma((7,)),
            dma((7,)),
            dma((7,)),
            dma((7,)),
            dma((7,)),
            dma((7,)),
        ],
        compiler_params=pltpu.CompilerParams(
            collective_id=0, has_side_effects=True, vmem_limit_bytes=63 * 1024 * 1024
        ),
        name="train_step",
    )(*small, *large)


def per_device(
    latent,
    hint_field,
    from_below,
    cotangent,
    timesteps,
    time_weight,
    enc_proj,
    ctl_proj,
    dec_proj,
    enc_conv_one,
    enc_conv_two,
    ctl_conv_one,
    ctl_conv_two,
    dec_conv_one,
    dec_conv_two,
    dec_shortcut,
    zero_conv,
):
    half_width = C // 2
    frequency = jnp.exp(-math.log(10000.0) * jnp.arange(half_width, dtype=jnp.float32) / half_width)
    angles = timesteps.astype(jnp.float32)[:, None] * frequency[None, :]
    sinusoid = jnp.concatenate([jnp.cos(angles), jnp.sin(angles)], axis=1).astype(jnp.bfloat16)
    def by_row(field):
        return jnp.transpose(field[0], (1, 0, 2))

    def by_tap(kernel):
        return jnp.transpose(kernel, (1, 2, 0, 3)).reshape(9, kernel.shape[0], kernel.shape[3])

    def from_tap(grad):
        return jnp.transpose(grad.reshape(3, 3, 10, C), (2, 0, 1, 3))

    one_grad, two_grad, zero_grad = run_step(
        (
            jnp.broadcast_to(sinusoid, (16, C)),
            by_row(latent),
            by_row(hint_field),
            by_row(from_below),
            by_row(cotangent),
            ctl_conv_one,
            ctl_conv_two,
            dec_conv_one,
            dec_conv_two,
            dec_shortcut,
            zero_conv,
        ),
        (time_weight, enc_proj.T, ctl_proj.T, dec_proj.T, by_tap(enc_conv_one), by_tap(enc_conv_two)),
    )
    return (from_tap(one_grad), from_tap(two_grad), zero_grad)


def solution(mesh):
    in_specs = (
        P("dp", None, "rows", None),
        P("dp", None, "rows", None),
        P("dp", None, "rows", None),
        P("dp", None, "rows", None),
        P("dp"),
        P(),
        P(),
        P(),
        P(),
        P(),
        P(),
        P("dp", None, None, None),
        P("dp", None, None, None),
        P("dp", None, None, None),
        P("dp", None, None, None),
        P("dp", None),
        P("dp", None),
    )
    out_specs = (P("dp", None, None, None), P("dp", None, None, None), P("dp", None))
    return jax.shard_map(
        per_device, mesh=mesh, in_specs=in_specs, out_specs=out_specs, check_vma=False
    )
```

```python
import math

import jax
import jax.numpy as jnp
from jax import lax
from jax.experimental import pallas as pl
from jax.experimental.pallas import tpu as pltpu
from jax.sharding import PartitionSpec as P

C = 320
EPSILON = 1e-05
MESH = pl.DeviceIdType.MESH
LANES = 16384
HALF = 4096
BF = jnp.bfloat16
F32 = jnp.float32
ROWS = 16
STEPS = C // ROWS
NT = (((1,), (1,)), ((), ()))
TN = (((0,), (0,)), ((), ()))
EXACT = lax.Precision.HIGHEST
AT_CTL_ONE = 0
AT_CTL_TWO = 2944
AT_ZERO = 5888
AT_DEC_ONE = 6272
AT_SHORT = 12032
AT_DEC_TWO = 12416


def place():
    d = lax.axis_index("dp")
    r = lax.axis_index("rows")
    return (d // 8, (d // 2) % 4, d % 2, r // 4, r % 4)


def device_of(zh, y, c, zl, x):
    return (zh * 8 + y * 2 + c, zl * 4 + x)


def remote(src, dst, send, recv, where):
    return pltpu.make_async_remote_copy(
        src_ref=src, dst_ref=dst, send_sem=send, recv_sem=recv, device_id=where, device_id_type=MESH
    )


def greet(peers):
    barrier = pltpu.get_barrier_semaphore()
    for where in peers:
        pl.semaphore_signal(barrier, inc=1, device_id=where, device_id_type=MESH)
    pl.semaphore_wait(barrier, len(peers))


def lanes_at(start, size):
    return pl.ds(pl.multiple_of(start, 128), size)


def band(i):
    return slice(i * ROWS, i * ROWS + ROWS)


def each(count):
    def run(body):
        for i in range(count):
            body(i)

    return run


def put_columns(col, base_of, i, strips):
    lane = lax.broadcasted_iota(jnp.int32, (ROWS, 128), 1)
    shifted_of = []
    for strip in strips:
        left = jnp.where(lane == 0, 0.0, pltpu.roll(strip, 1, axis=1))
        right = jnp.where(lane == 127, 0.0, pltpu.roll(strip, 127, axis=1))
        shifted_of.append([left.astype(BF), strip.astype(BF), right.astype(BF)])
    for p in range(3):
        for q in range(3):
            start = base_of(3 * p + q) + i * ROWS
            col[start : start + ROWS, 0:128] = shifted_of[p][q]
            col[start : start + ROWS, 128:256] = shifted_of[p + 1][q]


def sig(v):
    return jax.nn.sigmoid(v)


def slope(v):
    s = sig(v)
    return s * (1.0 + v * (1.0 - s))


def dot(a, b):
    return jnp.dot(a, b, preferred_element_type=F32)


def taps_dot(kernel, col):
    total = dot(kernel[0], col[0:C, :])
    for tap in range(1, 9):
        total = total + dot(kernel[tap], col[C * tap : C * tap + C, :])
    return total


def three_parts(value):
    high = value.astype(BF).astype(F32)
    rest = value - high
    middle = rest.astype(BF).astype(F32)
    return [high, middle, rest - middle]


def put_sums(cols, at, i, pairs):
    for k, value in enumerate(pairs):
        cols[band(i), at + k : at + k + 1] = jnp.sum(value, axis=1, keepdims=True)


def step_kernel(
    sinus,
    latent_ref,
    hint_ref,
    under_ref,
    cot_ref,
    shard_ctl_one,
    shard_ctl_two,
    shard_dec_one,
    shard_dec_two,
    shard_short,
    shard_zero,
    time_weight_hbm,
    enc_proj_hbm,
    ctl_proj_hbm,
    dec_proj_hbm,
    enc_one_hbm,
    enc_two_hbm,
    one_out,
    two_out,
    zero_out,
    member,
    ten,
    twenty,
    cols,
    coef,
    halo,
    halo_cot,
    inner,
    inner_halo,
    edge,
    col_t,
    col_a,
    col_b,
    col_d,
    col_g,
    back_dec_two,
    back_dec_one,
    back_ctl_two,
    zero_t,
    short_t,
    enc_raw,
    ctl_raw,
    ctl_out,
    skip,
    skip_halo,
    dec_raw,
    dec_halo,
    dec_edge,
    up_grad,
    sfg,
    sfg_edge,
    sfg_halo,
    keep_n,
    keep_skip,
    keep_dec,
    mixed,
    wide,
    wide_two,
    note,
    note_in,
    note_send,
    note_recv,
    halo_send,
    halo_recv,
    time_weight,
    projections,
    stage,
    src,
    enc_one,
    enc_two,
    enc_sem,
    weights,
    parts,
    column,
    gath,
    own_sem,
    ph1_send,
    ph1_recv,
    ph2_send,
    ph2_recv,
    ph3_send,
    ph3_recv,
    ph4_send,
    ph4_recv,
    ph5_send,
    ph5_recv,
    grads,
    swap,
    half,
    far,
    near,
    passing,
    near_in,
    deep,
    deep_in,
    last,
    fan,
    pool,
    tight,
    opened,
    out_sem,
    rs1_send,
    rs1_recv,
    rs2_send,
    rs2_recv,
    rs3_send,
    rs3_recv,
    rs4_send,
    rs4_recv,
    rs6_send,
    rs6_recv,
    rs7_send,
    rs7_recv,
):
    d = lax.axis_index("dp")
    r = lax.axis_index("rows")
    zh, y, c, zl, x = place()
    slot = y * 2 + c
    peers = [(d, (r + k) % 8) for k in range(1, 8)]
    plane_peers = []
    for k in range(1, 8):
        s = (slot + k) % 8
        plane_peers.append(device_of(zh, s // 2, s % 2, zl, x))
    z_peers = [device_of((zh + k) % 4, y, c, zl, x) for k in range(1, 4)]
    x_peers = [device_of(zh, y, c, zl, (x + k) % 4) for k in range(1, 4)]
    y_peers = [device_of(zh, (y + k) % 4, c, zl, x) for k in range(1, 4)]
    partner = device_of(zh, y, 1 - c, zl, x)
    other_z = device_of(zh, y, c, 1 - zl, x)
    z_all = [device_of((zh + k // 2) % 4, y, c, (zl + k) % 2, x) for k in range(1, 8)]
    everyone = peers + plane_peers + z_all[1:]
    barrier = pltpu.get_barrier_semaphore()
    for where in everyone:
        pl.semaphore_signal(barrier, inc=1, device_id=where, device_id_type=MESH)
    loads = []
    for k, (source, target) in enumerate(
        (
            (time_weight_hbm, time_weight),
            (enc_proj_hbm, projections.at[0]),
            (ctl_proj_hbm, projections.at[1]),
            (dec_proj_hbm, projections.at[2]),
            (enc_one_hbm, enc_one),
            (enc_two_hbm, enc_two),
        )
    ):
        loads.append(pltpu.make_async_copy(source, target, enc_sem.at[k]))
        loads[-1].start()
    load_one, load_two = loads[4:]

    stage[...] = jnp.zeros((16, LANES), BF)
    for kernel, start, count, width in (
        (shard_ctl_one, AT_CTL_ONE, 9, C),
        (shard_ctl_two, AT_CTL_TWO, 9, C),
        (shard_dec_one, AT_DEC_ONE, 9, 2 * C),
        (shard_dec_two, AT_DEC_TWO, 9, C),
    ):
        for tap in range(count):
            stage[0:10, start + width * tap : start + width * tap + width] = kernel[:, tap // 3, tap % 3, :]
    stage[0:10, AT_ZERO : AT_ZERO + C] = shard_zero[...]
    stage[0:10, AT_SHORT : AT_SHORT + C] = shard_short[:, C : 2 * C]
    for s in range(8):
        for g in range(4):
            tile = (x * 2 + s % 2) * 4 + s // 2 if g % 2 else s * 4 + x
            src[s, :, 128 * g : 128 * g + 128] = stage[:, lanes_at(g * 4096 + tile * 128, 128)]

    lane = lax.broadcasted_iota(jnp.int32, (C, 128), 1)
    channel = lax.broadcasted_iota(jnp.int32, (C, 128), 0)
    in_ten = (channel >= 10 * lane) & (channel < 10 * lane + 10)
    other = lane - 32
    in_twenty = (channel >= 20 * other) & (channel < 20 * other + 20)
    one_ten = jnp.where(in_ten, 1.0, 0.0)
    one_twenty = jnp.where(in_twenty, 1.0, 0.0)
    member[...] = (one_ten + one_twenty).astype(BF)
    for k in range(3):
        ten[:, 128 * k : 128 * k + 128] = one_ten.astype(BF)
        twenty[:, 128 * k : 128 * k + 128] = one_twenty.astype(BF)
    cols[...] = jnp.zeros((C, 128), F32)

    @each(STEPS)
    def _(i):
        sums = [0.0] * 6
        for h in range(2):
            latent = latent_ref[h, band(i), :].astype(F32)
            ctl_in = (latent + hint_ref[h, band(i), :].astype(F32)).astype(BF).astype(F32)
            under = under_ref[h, band(i), :].astype(F32)
            for k, value in enumerate((latent, latent * latent, ctl_in, ctl_in * ctl_in, under, under * under)):
                sums[k] = sums[k] + value
        put_sums(cols, 0, i, sums)

    pl.semaphore_wait(barrier, len(everyone))
    before = (d, (r + 7) % 8)
    after = (d, (r + 1) % 8)
    waiting = []

    def send_rows(event, top, bottom, above, below):
        first = remote(top, below, halo_send.at[event, 0], halo_recv.at[event, 0], before)
        second = remote(bottom, above, halo_send.at[event, 1], halo_recv.at[event, 1], after)
        first.start()
        second.start()
        waiting.extend([first, second])
        return (first, second)

    def arrive(pair):
        pair[0].wait_recv()
        pair[1].wait_recv()

    raw = send_rows(0, latent_ref.at[0], latent_ref.at[1], halo.at[0, 0], halo.at[1, 0])
    raw_hint = send_rows(8, hint_ref.at[0], hint_ref.at[1], halo.at[0, 1], halo.at[1, 1])
    first = []
    for k in range(7):
        s = (slot + k + 1) % 8
        first.append(remote(src.at[s], parts.at[slot], ph1_send.at[k], ph1_recv.at[k], plane_peers[k]))
        first[-1].start()
    waiting.extend(first)
    mine = pltpu.make_async_copy(src.at[slot], parts.at[slot], own_sem.at[4])
    mine.start()

    second = {}
    third = {}
    fourth = {}
    fifth = {}
    held = {}

    def gather_z():
        mine.wait()
        for copy in first:
            copy.wait_recv()
        for s in range(8):
            column[10 * s : 10 * s + 10, :] = parts[s, 0:10, :].astype(F32)
        home = pl.multiple_of(zh * 80, 16)
        gath[pl.ds(home, 80), :] = column[...].astype(BF)
        for g in range(4):
            block = gath.at[pl.ds(home, 80), 128 * g : 128 * g + 128]
            second[g] = []
            for k in (0, 2, 1):
                second[g].append(remote(block, block, ph2_send.at[g, k], ph2_recv.at[g, k], z_peers[k]))
                second[g][-1].start()
            waiting.extend(second[g])

    def gather_short(g):
        for copy in second[g]:
            copy.wait_recv()
        block = gath.at[:, 128 * g : 128 * g + 128]
        tile = (x * 2 + c) * 4 + y if g % 2 else slot * 4 + x
        short_peers = y_peers if g % 2 else x_peers
        spot = weights.at[:, lanes_at(g * 4096 + tile * 128, 128)]
        third[g] = []
        for k in (0, 2, 1):
            third[g].append(remote(block, spot, ph3_send.at[g, k], ph3_recv.at[g, k], short_peers[k]))
            third[g][-1].start()
        waiting.extend(third[g])
        held[g] = pltpu.make_async_copy(block, spot, own_sem.at[g])
        held[g].start()

    def column_of(g, steps, at, size):
        where = x if g % 2 else y
        return weights.at[:, lanes_at(g * 4096 + ((where + 4 + steps) % 4 * 2 + c) * 512 + at, size)]

    def to_partner(g, k, steps):
        block = column_of(g, steps, 0, 512)
        copy = remote(block, block, ph5_send.at[g, k], ph5_recv.at[g, k], partner)
        copy.start()
        fifth[g].append(copy)
        waiting.append(copy)

    def long_peers(g):
        return x_peers if g % 2 else y_peers

    def gather_long(g):
        held[g].wait()
        for copy in third[g]:
            copy.wait_recv()
        block = column_of(g, 0, 0, 512)
        fourth[g] = [
            remote(block, block, ph4_send.at[g, 0], ph4_recv.at[g, 0], long_peers(g)[0]),
            remote(block, block, ph4_send.at[g, 1], ph4_recv.at[g, 1], long_peers(g)[2]),
        ]
        for copy in fourth[g]:
            copy.start()
        waiting.extend(fourth[g])
        fifth[g] = []
        to_partner(g, 0, 0)

    def gather_relay(g):
        fourth[g][0].wait_recv()
        block = column_of(g, -1, 0, 256)
        up = remote(block, block, ph4_send.at[g, 2], ph4_recv.at[g, 2], long_peers(g)[0])
        up.start()
        fourth[g][1].wait_recv()
        block = column_of(g, 1, 256, 256)
        down = remote(block, block, ph4_send.at[g, 3], ph4_recv.at[g, 3], long_peers(g)[2])
        down.start()
        fourth[g].extend([up, down])
        waiting.extend([up, down])
        to_partner(g, 1, -1)
        to_partner(g, 2, 1)

    def gather_finish(g):
        fourth[g][2].wait_recv()
        fourth[g][3].wait_recv()
        to_partner(g, 3, 2)

    def gather_done(g):
        for copy in fifth[g]:
            copy.wait_recv()


    def share(turn):
        turned = cols[:, 0:8].T
        sums = dot(jnp.concatenate(three_parts(turned), axis=0).astype(BF), member[...])
        note[turn] = sums[0:8] + sums[8:16] + sums[16:24]
        copies = []
        for k in range(1, 8):
            copies.append(
                remote(
                    note.at[turn],
                    note_in.at[turn, k - 1],
                    note_send.at[turn, k - 1],
                    note_recv.at[turn, k - 1],
                    peers[k - 1],
                )
            )
            copies[-1].start()
        waiting.extend(copies)
        return copies

    def collect(turn, copies):
        for copy in copies:
            copy.wait_recv()
        total = note[turn]
        for k in range(7):
            total = total + note_in[turn, k]
        return total

    which = lax.broadcasted_iota(jnp.int32, (8, 128), 1)
    per_group = jnp.where(which < 32, 1.0 / (10 * 2048), 1.0 / (20 * 2048))

    def spread(table, at, rows):
        wide_rows = [
            jnp.broadcast_to(jnp.concatenate(three_parts(row), axis=1), (128, 384)).astype(BF) for row in rows
        ]
        columns = lax.dot_general(
            table[...], jnp.concatenate(wide_rows, axis=0), NT, preferred_element_type=F32
        )
        for k in range(len(rows)):
            coef[at + k] = columns[:, 128 * k : 128 * k + 128]

    def raw_sums(raw_ref, term_at, i):
        term = coef[term_at, band(i), :]
        one = raw_ref[band(i), 0:128] + term
        two = raw_ref[band(i), 128:256] + term
        put_sums(cols, 0, i, [one + two, one * one + two * two])

    def norm_rows(total, k):
        mean = total[k : k + 1] * per_group[0:1]
        square = total[k + 1 : k + 2] * per_group[0:1]
        return [mean, lax.rsqrt(square - mean * mean + EPSILON)]

    def mean_rows(total, k):
        return [total[k : k + 1] * per_group[0:1], total[k + 1 : k + 2] * per_group[0:1]]

    has_up = r > 0
    has_down = r < 7

    def masked(strips):
        return [
            jnp.where(has_up, strips[0], 0.0),
            strips[1],
            strips[2],
            jnp.where(has_down, strips[3], 0.0),
        ]

    first_note = share(0)
    for load in loads[0:4]:
        load.wait()
    embed = dot(sinus[...], time_weight[...])
    embed = (embed * sig(embed)).astype(BF)
    for k in range(3):
        term = lax.dot_general(projections[k], embed, NT, preferred_element_type=F32)
        coef[20 + k] = jnp.broadcast_to(term[:, 0:1], (C, 128))
    for target in (back_dec_two, back_dec_one, back_ctl_two):
        for tap in range(9):
            target[:, 384 * tap + 320 : 384 * tap + 384] = jnp.zeros((C, 64), BF)
    for tap in range(9):
        col_g[384 * tap + 320 : 384 * tap + 384, :] = jnp.zeros((64, 256), BF)
    grads[0, :, 2816:HALF] = jnp.zeros((C, HALF - 2816), BF)
    grads[0, 160:C, :] = jnp.zeros((160, HALF), BF)
    grads[1, :, 2816:HALF] = jnp.zeros((C, HALF - 2816), BF)
    grads[1, 160:C, :] = jnp.zeros((160, HALF), BF)

    def turn(target, start, stride):
        for tap in range(9):
            block = weights[:, start + stride * tap : start + stride * tap + 320].astype(F32)
            target[:, 384 * (8 - tap) : 384 * (8 - tap) + 320] = block.T.astype(BF)

    def turn_square(target, start):
        target[...] = weights[:, start : start + 320].astype(F32).T.astype(BF)

    gather_z()
    late = send_rows(1, under_ref.at[0], under_ref.at[1], halo.at[0, 2], halo.at[1, 2])
    total = collect(0, first_note)
    spread(ten, 0, norm_rows(total, 0) + norm_rows(total, 2))
    spread(twenty, 4, norm_rows(total, 4))
    arrive(raw)
    arrive(raw_hint)

    def plain(tap):
        return 320 * tap

    def first_act(source_of, at, col, base_of):
        @each(STEPS)
        def _(i):
            mean = coef[at, band(i), :]
            inv = coef[at + 1, band(i), :]
            strips = []
            for strip in source_of(i):
                normed = (strip - mean) * inv
                strips.append(normed * sig(normed))
            put_columns(col, base_of, i, masked(strips))

    def latent_of(i):
        return [
            halo[0, 0, band(i), :].astype(F32),
            latent_ref[0, band(i), :].astype(F32),
            latent_ref[1, band(i), :].astype(F32),
            halo[1, 0, band(i), :].astype(F32),
        ]

    def ctl_in_of(i):
        hint = [
            halo[0, 1, band(i), :].astype(F32),
            hint_ref[0, band(i), :].astype(F32),
            hint_ref[1, band(i), :].astype(F32),
            halo[1, 1, band(i), :].astype(F32),
        ]
        return [(a + b).astype(BF).astype(F32) for a, b in zip(latent_of(i), hint)]

    first_act(latent_of, 0, col_t, plain)
    load_one.wait()
    enc_raw[...] = taps_dot(enc_one, col_t)
    edge[0] = enc_raw[:, 0:128].astype(BF)
    edge[1] = enc_raw[:, 128:256].astype(BF)
    enc_rows = send_rows(3, edge.at[0], edge.at[1], inner_halo.at[0], inner_halo.at[1])

    @each(STEPS)
    def _(i):
        raw_sums(enc_raw, 20, i)

    second_note = share(1)
    gather_short(0)
    first_act(ctl_in_of, 2, col_a, plain)

    def under_of(i):
        return [
            halo[0, 2, band(i), :].astype(F32),
            under_ref[0, band(i), :].astype(F32),
            under_ref[1, band(i), :].astype(F32),
            halo[1, 2, band(i), :].astype(F32),
        ]

    def joined_low(tap):
        return 640 * tap

    def joined_high(tap):
        return 640 * tap + 320

    def spaced(tap):
        return 384 * tap


    gather_short(1)
    gather_long(0)
    gather_short(2)
    total = collect(1, second_note)
    spread(ten, 6, norm_rows(total, 0))

    def second_act(raw_ref, at_halo, term_at, at, col, keep):
        @each(STEPS)
        def _(i):
            mean = coef[at, band(i), :]
            inv = coef[at + 1, band(i), :]
            own = raw_ref[band(i), :]
            term = coef[20 + term_at, band(i), :]
            strips = []
            for strip in (
                inner_halo[at_halo, band(i), :].astype(F32),
                own[:, 0:128],
                own[:, 128:256],
                inner_halo[at_halo + 1, band(i), :].astype(F32),
            ):
                strips.append((strip + term - mean) * inv)
            if keep is not None:
                keep[band(i), 0:128] = strips[1]
                keep[band(i), 128:256] = strips[2]
            put_columns(col, plain, i, masked([v * sig(v) for v in strips]))

    arrive(enc_rows)
    second_act(enc_raw, 0, 0, 6, col_t, None)
    load_two.wait()
    enc_raw[...] = taps_dot(enc_two, col_t)
    gather_long(1)
    arrive(late)
    first_act(under_of, 4, col_d, joined_low)
    gather_relay(0)
    gather_short(3)
    gather_long(2)
    gather_finish(0)
    gather_done(0)
    ctl_raw[...] = dot(weights[:, AT_CTL_ONE : AT_CTL_ONE + 2880], col_a[...])
    edge[2] = ctl_raw[:, 0:128].astype(BF)
    edge[3] = ctl_raw[:, 128:256].astype(BF)
    ctl_rows = send_rows(4, edge.at[2], edge.at[3], inner_halo.at[2], inner_halo.at[3])

    @each(STEPS)
    def _(i):
        raw_sums(ctl_raw, 21, i)

    ctl_note = share(2)
    gather_relay(1)
    late_cot = send_rows(2, cot_ref, cot_ref, halo_cot.at[0], halo_cot.at[1])
    total = collect(2, ctl_note)
    spread(ten, 8, norm_rows(total, 0))
    arrive(ctl_rows)
    second_act(ctl_raw, 2, 1, 8, col_b, keep_n)
    gather_long(3)
    gather_finish(1)
    gather_done(1)
    inner[...] = dot(weights[:, AT_CTL_TWO : AT_CTL_TWO + 2880], col_b[...])

    @each(STEPS)
    def _(i):
        own = ctl_in_of(i)
        ctl_out[band(i), 0:128] = (own[1] + inner[band(i), 0:128]).astype(BF)
        ctl_out[band(i), 128:256] = (own[2] + inner[band(i), 128:256]).astype(BF)

    inner[...] = dot(weights[:, AT_ZERO : AT_ZERO + 320], ctl_out[...])

    @each(STEPS)
    def _(i):
        sums = [0.0, 0.0]
        for h in range(2):
            lanes = slice(128 * h, 128 * h + 128)
            latent = latent_ref[h, band(i), :].astype(F32)
            enc_out = (latent + enc_raw[band(i), lanes]).astype(BF).astype(F32)
            joined = (enc_out + inner[band(i), lanes]).astype(BF)
            skip[h, band(i), :] = joined
            value = joined.astype(F32)
            sums = [sums[0] + value, sums[1] + value * value]
        put_sums(cols, 0, i, sums)

    skip_rows = send_rows(5, skip.at[0], skip.at[1], skip_halo.at[0], skip_halo.at[1])
    third_note = share(3)
    turn(back_ctl_two, AT_CTL_TWO, 320)
    turn_square(zero_t, AT_ZERO)
    gather_relay(2)
    gather_relay(3)

    total = collect(3, third_note)
    spread(twenty, 10, norm_rows(total, 0))
    arrive(skip_rows)

    @each(STEPS)
    def _(i):
        mean = coef[10, band(i), :]
        inv = coef[11, band(i), :]
        strips = []
        for k, strip in enumerate(
            (skip_halo[0, band(i), :], skip[0, band(i), :], skip[1, band(i), :], skip_halo[1, band(i), :])
        ):
            normed = (strip.astype(F32) - mean) * inv
            keep_skip[band(i), 128 * k : 128 * k + 128] = normed
            strips.append(normed * sig(normed))
        put_columns(col_d, joined_high, i, masked(strips))

    gather_finish(2)
    gather_done(2)
    dec_raw[...] = dot(weights[:, AT_DEC_ONE : AT_DEC_ONE + 5760], col_d[...])
    dec_edge[0] = dec_raw[:, 0:128].astype(BF)
    dec_edge[1] = dec_raw[:, 128:256].astype(BF)
    dec_rows = send_rows(6, dec_edge.at[0], dec_edge.at[1], dec_halo.at[0], dec_halo.at[1])

    @each(STEPS)
    def _(i):
        raw_sums(dec_raw, 22, i)

    fourth_note = share(4)
    turn(back_dec_one, AT_DEC_ONE + 320, 640)
    gather_finish(3)
    arrive(late_cot)
    scale = 2.0**-8

    def cot_of(i):
        far_rows = [jnp.where(has_up, halo_cot[0, h, band(i), :].astype(F32), 0.0) for h in range(2)]
        own = [cot_ref[h, band(i), :].astype(F32) for h in range(2)]
        near_rows = [jnp.where(has_down, halo_cot[1, h, band(i), :].astype(F32), 0.0) for h in range(2)]
        return [strip * scale for strip in far_rows + own + near_rows]

    gather_done(3)
    turn(back_dec_two, AT_DEC_TWO, 320)
    turn_square(short_t, AT_SHORT)
    for part in range(2):

        @each(STEPS)
        def _(i):
            strips = cot_of(i)[2 * part : 2 * part + 4]
            put_columns(col_g, spaced, i, strips)

        up_grad[:, 256 * part : 256 * part + 256] = dot(back_dec_two[...], col_g[...])

    @each(STEPS)
    def _(i):
        for k, strip in enumerate(cot_of(i)[1:5]):
            wide[band(i), 128 * k : 128 * k + 128] = strip.astype(BF)

    mixed[...] = dot(short_t[...], wide[...])

    total = collect(4, fourth_note)
    spread(ten, 12, norm_rows(total, 0))

    def keep_dec_rows(i, strip, k):
        mean = coef[12, band(i), :]
        inv = coef[13, band(i), :]
        term = coef[22, band(i), :]
        normed = (strip + term - mean) * inv
        keep_dec[band(i), 128 * k : 128 * k + 128] = normed
        upstream = up_grad[band(i), 128 * k : 128 * k + 128] * slope(normed)
        up_grad[band(i), 128 * k : 128 * k + 128] = upstream
        return (normed, upstream)

    @each(STEPS)
    def _(i):
        one_n, one_g = keep_dec_rows(i, dec_raw[band(i), 0:128], 1)
        two_n, two_g = keep_dec_rows(i, dec_raw[band(i), 128:256], 2)
        put_sums(cols, 0, i, [one_g + two_g, one_g * one_n + two_g * two_n])

    fifth_note = share(5)
    arrive(dec_rows)

    @each(STEPS)
    def _(i):
        keep_dec_rows(i, dec_halo[0, band(i), :].astype(F32), 0)
        keep_dec_rows(i, dec_halo[1, band(i), :].astype(F32), 3)

    total = collect(5, fifth_note)
    spread(ten, 14, mean_rows(total, 0))

    @each(STEPS)
    def _(i):
        inv = coef[13, band(i), :]
        mean = coef[14, band(i), :]
        cross = coef[15, band(i), :]
        strips = []
        for k in range(4):
            lanes = slice(128 * k, 128 * k + 128)
            strips.append(inv * (up_grad[band(i), lanes] - mean - keep_dec[band(i), lanes] * cross))
        put_columns(col_g, spaced, i, masked(strips))

    sfg[...] = dot(back_dec_one[...], col_g[...])
    sfg_edge[0] = sfg[:, 0:128].astype(BF)
    sfg_edge[1] = sfg[:, 128:256].astype(BF)
    sfg_rows = send_rows(7, sfg_edge.at[0], sfg_edge.at[1], sfg_halo.at[0], sfg_halo.at[1])

    @each(STEPS)
    def _(i):
        normed = keep_skip[band(i), 128:384]
        value = sfg[band(i), :] * slope(normed)
        up_grad[band(i), 128:384] = value
        put_sums(cols, 0, i, [value, value * normed])

    sixth_note = share(6)
    arrive(sfg_rows)

    @each(STEPS)
    def _(i):
        for at, lanes in ((0, slice(0, 128)), (1, slice(384, 512))):
            up_grad[band(i), lanes] = sfg_halo[at, band(i), :].astype(F32) * slope(keep_skip[band(i), lanes])

    total = collect(6, sixth_note)
    spread(twenty, 16, mean_rows(total, 0))

    @each(STEPS)
    def _(i):
        inv = coef[11, band(i), :]
        mean = coef[16, band(i), :]
        cross = coef[17, band(i), :]
        for k in range(4):
            lanes = slice(128 * k, 128 * k + 128)
            value = inv * (up_grad[band(i), lanes] - mean - keep_skip[band(i), lanes] * cross) + mixed[band(i), lanes]
            wide[band(i), lanes] = value.astype(BF)

    up_grad[...] = dot(zero_t[...], wide[...])

    @each(STEPS)
    def _(i):
        strips = []
        for k in range(4):
            strips.append(up_grad[band(i), 128 * k : 128 * k + 128].astype(BF).astype(F32))
        wide_two[band(i), 0:128] = strips[1].astype(BF)
        wide_two[band(i), 128:256] = strips[2].astype(BF)
        put_columns(col_g, spaced, i, masked(strips))

    def store_grads(k, value, at):
        count = value.shape[1]
        grads[k, 0:160, at : at + count] = value[0:160].astype(BF)
        for start in range(0, count, 128):
            tile = (at + start) // 128
            spot = (tile // 16 * 16 + tile % 4 * 4 + tile // 4 % 4) * 128
            size = min(128, count - start)
            grads[k, 160:C, spot : spot + size] = value[160:C, start : start + size].astype(BF)

    swaps = {}
    pairs = {}
    fours = {}

    def reduce_core(k):
        swaps[k] = remote(
            grads.at[k, :, lanes_at((1 - c) * 2048, 2048)], swap.at[k], rs1_send.at[k], rs1_recv.at[k], partner
        )
        swaps[k].start()
        waiting.append(swaps[k])

    def reduce_far(k):
        swaps[k].wait_recv()

        @each(STEPS)
        def _(i):
            total = grads[k, band(i), lanes_at(c * 2048, 2048)].astype(F32) + swap[k, band(i), :].astype(F32)
            half[k, band(i), :] = total.astype(BF)

        pairs[k] = []
        for axis, (where, ring_peers) in enumerate(((y, y_peers), (x, x_peers))):
            rows = slice(160 * axis, 160 * axis + 160)
            for j, (steps, part, target) in enumerate(((1, 256, 0), (2, 0, 0), (3, 0, 2), (2, 256, 2))):
                block = half.at[k, rows, lanes_at((where + steps) % 4 * 512 + part, 256)]
                pairs[k].append(
                    remote(
                        block,
                        far.at[k, axis, j],
                        rs2_send.at[k, axis, j],
                        rs2_recv.at[k, axis, j],
                        ring_peers[target],
                    )
                )
                pairs[k][-1].start()
        waiting.extend(pairs[k])

    relays = {}

    def reduce_relay(k):
        relays[k] = []
        for axis, (where, ring_peers) in enumerate(((y, y_peers), (x, x_peers))):
            rows = slice(160 * axis, 160 * axis + 160)
            for j, (steps, part, target, source) in enumerate(((1, 0, 0, 1), (3, 256, 2, 3))):
                pairs[k][4 * axis + source].wait_recv()
                own = half[k, rows, lanes_at((where + steps) % 4 * 512 + part, 256)].astype(F32)
                passing[k, axis, j] = (own + far[k, axis, source].astype(F32)).astype(BF)
                relays[k].append(
                    remote(
                        passing.at[k, axis, j],
                        far.at[k, axis, 4 + j],
                        rs2_send.at[k, axis, 4 + j],
                        rs2_recv.at[k, axis, 4 + j],
                        ring_peers[target],
                    )
                )
                relays[k][-1].start()
        waiting.extend(relays[k])

    def reduce_near(k):
        for axis in range(2):
            pairs[k][4 * axis].wait_recv()
            pairs[k][4 * axis + 2].wait_recv()
        for copy in relays[k]:
            copy.wait_recv()
        for axis, where in ((0, y), (1, x)):
            rows = slice(160 * axis, 160 * axis + 160)
            for part, direct, relayed in ((0, 2, 4), (256, 0, 5)):
                total = half[k, rows, lanes_at(where * 512 + part, 256)].astype(F32)
                total = total + far[k, axis, direct].astype(F32) + far[k, axis, relayed].astype(F32)
                near[k, axis, :, part : part + 256] = total.astype(BF)

        fours[k] = []
        for j in (1, 3, 2):
            xa = (x + j) % 4
            yb = (y + j) % 4
            fours[k].append(
                remote(
                    near.at[k, 0, :, lanes_at(xa * 128, 128)],
                    near_in.at[k, 0, j - 1],
                    rs3_send.at[k, 0, j - 1],
                    rs3_recv.at[k, 0, j - 1],
                    x_peers[j - 1],
                )
            )
            fours[k].append(
                remote(
                    near.at[k, 1, :, lanes_at(yb * 128, 128)],
                    near_in.at[k, 1, j - 1],
                    rs3_send.at[k, 1, j - 1],
                    rs3_recv.at[k, 1, j - 1],
                    y_peers[j - 1],
                )
            )
        for copy in fours[k]:
            copy.start()
        waiting.extend(fours[k])

    def reduce_deep(k):
        for copy in fours[k]:
            copy.wait_recv()
        for which, where in ((0, x), (1, y)):
            total = near[k, which, :, lanes_at(where * 128, 128)].astype(F32)
            for j in range(3):
                total = total + near_in[k, which, j].astype(F32)
            deep[160 * which : 160 * which + 160, 128 * k : 128 * k + 128] = total.astype(BF)

    two_value = lax.dot_general(wide_two[...], col_b[...], NT, preferred_element_type=F32)
    store_grads(0, two_value, 0)
    zero_value = lax.dot_general(wide[:, 128:384], ctl_out[...], NT, preferred_element_type=F32)
    store_grads(0, zero_value, 2944)
    reduce_core(0)
    sfg[...] = dot(back_ctl_two[...], col_g[...])

    @each(STEPS)
    def _(i):
        normed = keep_n[band(i), :]
        value = sfg[band(i), :] * slope(normed)
        sfg[band(i), :] = value
        put_sums(cols, 0, i, [value, value * normed])

    seventh_note = share(7)
    reduce_far(0)
    total = collect(7, seventh_note)
    spread(ten, 18, mean_rows(total, 0))

    @each(STEPS)
    def _(i):
        inv = coef[9, band(i), :]
        mean = coef[18, band(i), :]
        cross = coef[19, band(i), :]
        for lanes in (slice(0, 128), slice(128, 256)):
            value = inv * (sfg[band(i), lanes] - mean - keep_n[band(i), lanes] * cross)
            wide_two[band(i), lanes] = value.astype(BF)

    one_value = lax.dot_general(wide_two[...], col_a[...], NT, preferred_element_type=F32)
    store_grads(1, one_value, 0)
    reduce_core(1)
    reduce_relay(0)
    reduce_far(1)
    reduce_near(0)
    reduce_relay(1)
    reduce_deep(0)
    reduce_near(1)
    reduce_deep(1)
    ring = []
    for k in range(1, 8):
        zt = (zh + k // 2) % 4
        lt = (zl + k) % 2
        ring.append(
            remote(
                deep.at[pl.ds(pl.multiple_of(zt * 80, 16), 80), lanes_at(lt * 128, 128)],
                deep_in.at[k - 1],
                rs4_send.at[k - 1],
                rs4_recv.at[k - 1],
                z_all[k - 1],
            )
        )
        ring[-1].start()
    total = deep[pl.ds(pl.multiple_of(zh * 80, 16), 80), lanes_at(zl * 128, 128)].astype(F32)
    for k in range(7):
        ring[k].wait_recv()
        total = total + deep_in[k].astype(F32)
    last[...] = total
    for s in range(8):
        spaced_rows = jnp.concatenate([last[10 * s : 10 * s + 10, :], jnp.zeros((6, 128), F32)], axis=0)
        fan[s] = spaced_rows.astype(BF)
    sixth = []
    for k in range(7):
        s = (slot + k + 1) % 8
        sixth.append(remote(fan.at[s], pool.at[slot], rs6_send.at[k], rs6_recv.at[k], plane_peers[k]))
        sixth[-1].start()
    mine = pltpu.make_async_copy(fan.at[slot], pool.at[slot], out_sem.at[0])
    mine.start()
    mine.wait()
    for copy in sixth:
        copy.wait_recv()
    for s in range(8):
        last[10 * s : 10 * s + 10, :] = pool[s, 0:10, :].astype(F32)
    tight[r] = last[...].astype(BF)
    seventh = []
    for k in range(1, 8):
        seventh.append(
            remote(tight.at[r], tight.at[r], rs7_send.at[k - 1], rs7_recv.at[k - 1], peers[k - 1])
        )
        seventh[-1].start()
    for copy in seventh:
        copy.wait_recv()
    opened[...] = tight[...].astype(F32)
    for which, target, count in ((0, two_out, 23), (1, one_out, 23), (0, None, 26)):
        for tile in range(23 if target is None else 0, count):
            core, row_at, column_at = tile // 16, tile // 4 % 4, tile % 4
            at = 10 * (row_at * 2 + core)
            value = opened[which * 4 + column_at, at : at + 10, :]
            if target is None:
                size = min(128, C - (tile - 23) * 128)
                zero_out[:, (tile - 23) * 128 : (tile - 23) * 128 + size] = value[:, 0:size]
                continue
            at = tile * 128
            while at < min(tile * 128 + 128, 2880):
                tap, offset = divmod(at, C)
                size = min(C - offset, tile * 128 + 128 - at)
                target[tap, :, offset : offset + size] = value[:, at - tile * 128 : at - tile * 128 + size]
                at += size
    for copy in waiting + ring + sixth + seventh:
        copy.wait_send()


def run_step(small, large):
    dma = pltpu.SemaphoreType.DMA
    whole = pl.BlockSpec(memory_space=pltpu.VMEM)
    far_off = pl.BlockSpec(memory_space=pl.ANY)
    return pl.pallas_call(
        step_kernel,
        out_shape=(
            jax.ShapeDtypeStruct((9, 10, C), F32),
            jax.ShapeDtypeStruct((9, 10, C), F32),
            jax.ShapeDtypeStruct((10, C), F32),
        ),
        in_specs=[whole] * len(small) + [far_off] * len(large),
        out_specs=(whole, whole, whole),
        scratch_shapes=[
            pltpu.VMEM((C, 128), BF),
            pltpu.VMEM((C, 384), BF),
            pltpu.VMEM((C, 384), BF),
            pltpu.VMEM((C, 128), F32),
            pltpu.VMEM((23, C, 128), F32),
            pltpu.VMEM((2, 3, C, 128), BF),
            pltpu.VMEM((2, 2, C, 128), BF),
            pltpu.VMEM((C, 256), F32),
            pltpu.VMEM((4, C, 128), BF),
            pltpu.VMEM((4, C, 128), BF),
            pltpu.VMEM((2880, 256), BF),
            pltpu.VMEM((2880, 256), BF),
            pltpu.VMEM((2880, 256), BF),
            pltpu.VMEM((5760, 256), BF),
            pltpu.VMEM((3456, 256), BF),
            pltpu.VMEM((C, 3456), BF),
            pltpu.VMEM((C, 3456), BF),
            pltpu.VMEM((C, 3456), BF),
            pltpu.VMEM((C, C), BF),
            pltpu.VMEM((C, C), BF),
            pltpu.VMEM((C, 256), F32),
            pltpu.VMEM((C, 256), F32),
            pltpu.VMEM((C, 256), BF),
            pltpu.VMEM((2, C, 128), BF),
            pltpu.VMEM((2, C, 128), BF),
            pltpu.VMEM((C, 256), F32),
            pltpu.VMEM((2, C, 128), BF),
            pltpu.VMEM((2, C, 128), BF),
            pltpu.VMEM((C, 512), F32),
            pltpu.VMEM((C, 256), F32),
            pltpu.VMEM((2, C, 128), BF),
            pltpu.VMEM((2, C, 128), BF),
            pltpu.VMEM((C, 256), F32),
            pltpu.VMEM((C, 512), F32),
            pltpu.VMEM((C, 512), F32),
            pltpu.VMEM((C, 512), F32),
            pltpu.VMEM((C, 512), BF),
            pltpu.VMEM((C, 256), BF),
            pltpu.VMEM((8, 8, 128), F32),
            pltpu.VMEM((8, 7, 8, 128), F32),
            dma((8, 7)),
            dma((8, 7)),
            dma((9, 2)),
            dma((9, 2)),
            pltpu.VMEM((C, 1280), BF),
            pltpu.VMEM((3, C, 1280), BF),
            pltpu.VMEM((16, LANES), BF),
            pltpu.VMEM((8, 16, 512), BF),
            pltpu.VMEM((9, C, C), BF),
            pltpu.VMEM((9, C, C), BF),
            dma((6,)),
            pltpu.VMEM((C, LANES), BF),
            pltpu.VMEM((8, 16, 512), BF),
            pltpu.VMEM((80, 512), F32),
            pltpu.VMEM((C, 512), BF),
            dma((5,)),
            dma((7,)),
            dma((7,)),
            dma((4, 3)),
            dma((4, 3)),
            dma((4, 3)),
            dma((4, 3)),
            dma((4, 4)),
            dma((4, 4)),
            dma((4, 4)),
            dma((4, 4)),
            pltpu.VMEM((2, C, HALF), BF),
            pltpu.VMEM((2, C, 2048), BF),
            pltpu.VMEM((2, C, 2048), BF),
            pltpu.VMEM((2, 2, 6, 160, 256), BF),
            pltpu.VMEM((2, 2, 160, 512), BF),
            pltpu.VMEM((2, 2, 2, 160, 256), BF),
            pltpu.VMEM((2, 2, 3, 160, 128), BF),
            pltpu.VMEM((C, 256), BF),
            pltpu.VMEM((7, 80, 128), BF),
            pltpu.VMEM((80, 128), F32),
            pltpu.VMEM((8, 16, 128), BF),
            pltpu.VMEM((8, 16, 128), BF),
            pltpu.VMEM((8, 80, 128), BF),
            pltpu.VMEM((8, 80, 128), F32),
            dma((1,)),
            dma((2,)),
            dma((2,)),
            dma((2, 2, 6)),
            dma((2, 2, 6)),
            dma((2, 2, 3)),
            dma((2, 2, 3)),
            dma((7,)),
            dma((7,)),
            dma((7,)),
            dma((7,)),
            dma((7,)),
            dma((7,)),
        ],
        compiler_params=pltpu.CompilerParams(
            collective_id=0, has_side_effects=True, vmem_limit_bytes=63 * 1024 * 1024
        ),
        name="train_step",
    )(*small, *large)


def per_device(
    latent,
    hint_field,
    from_below,
    cotangent,
    timesteps,
    time_weight,
    enc_proj,
    ctl_proj,
    dec_proj,
    enc_conv_one,
    enc_conv_two,
    ctl_conv_one,
    ctl_conv_two,
    dec_conv_one,
    dec_conv_two,
    dec_shortcut,
    zero_conv,
):
    half_width = C // 2
    frequency = jnp.exp(-math.log(10000.0) * jnp.arange(half_width, dtype=jnp.float32) / half_width)
    angles = timesteps.astype(jnp.float32)[:, None] * frequency[None, :]
    sinusoid = jnp.concatenate([jnp.cos(angles), jnp.sin(angles)], axis=1).astype(jnp.bfloat16)
    def by_row(field):
        return jnp.transpose(field[0], (1, 0, 2))

    def by_tap(kernel):
        return jnp.transpose(kernel, (1, 2, 0, 3)).reshape(9, kernel.shape[0], kernel.shape[3])

    def from_tap(grad):
        return jnp.transpose(grad.reshape(3, 3, 10, C), (2, 0, 1, 3))

    one_grad, two_grad, zero_grad = run_step(
        (
            jnp.broadcast_to(sinusoid, (16, C)),
            by_row(latent),
            by_row(hint_field),
            by_row(from_below),
            by_row(cotangent),
            ctl_conv_one,
            ctl_conv_two,
            dec_conv_one,
            dec_conv_two,
            dec_shortcut,
            zero_conv,
        ),
        (time_weight, enc_proj.T, ctl_proj.T, dec_proj.T, by_tap(enc_conv_one), by_tap(enc_conv_two)),
    )
    return (from_tap(one_grad), from_tap(two_grad), zero_grad)


def solution(mesh):
    in_specs = (
        P("dp", None, "rows", None),
        P("dp", None, "rows", None),
        P("dp", None, "rows", None),
        P("dp", None, "rows", None),
        P("dp"),
        P(),
        P(),
        P(),
        P(),
        P(),
        P(),
        P("dp", None, None, None),
        P("dp", None, None, None),
        P("dp", None, None, None),
        P("dp", None, None, None),
        P("dp", None),
        P("dp", None),
    )
    out_specs = (P("dp", None, None, None), P("dp", None, None, None), P("dp", None))
    return jax.shard_map(
        per_device, mesh=mesh, in_specs=in_specs, out_specs=out_specs, check_vma=False
    )
```
